32 devices in a mesh: space: 8 (over z, y), scene: 4 (over x, core).
Axes of the slice: x: 2, y: 2, z: 4, core: 2. Of those that a mesh axis runs over, the one named last changes fastest.
Arguments:
- features: bfloat16 [4, 16, 64, 512], P('scene', 'space'), may hold values from -6 to 6
- cotangent: bfloat16 [4, 16, 64, 512], P('scene', 'space'), may hold values from -6 to 6
- weight: bfloat16 [27, 64, 64], replicated, may hold values from -0.15625 to 0.15625
- neighbours: int32 [4, 16, 27], P('scene', 'space'), may hold values from -1 to 15, as said below
- occupancy: int32 [4, 16, 512], P('scene', 'space'), may hold values 0 or 1
Outputs:
- conv_out: bfloat16 [4, 16, 64, 512], P('scene', 'space')
- grad_features: bfloat16 [4, 16, 64, 512], P('scene', 'space')
- grad_weight: float32 [27, 64, 64], replicated
The draws below stay inside these ranges and needn't reach their ends.
Inputs may be any that keep to these rules, and one draw needn't show every extreme that they name: neighbours[s, b, 9 (a + 1) + 3 (c + 1) + (e + 1)] is the number within scene s of the active brick whose brick coordinates differ from brick b's by (a, c, e), each in -1, 0, 1, or -1 where no such brick is active; entry 13 is b itself and the relation is symmetric. Bricks 2 p to 2 (p + 1) - 1 form block p, a slab along the first brick coordinate: a neighbour at offset a = 0 lies in block p, a neighbour in block p - 1 has offset a = -1, a neighbour in block p + 1 has offset a = +1, and no neighbour lies in any other block.
All inputs are finite; a program needn't handle non-finite values. No bound on the sum of `occupancy` on one device may be relied on, other than what follows from the above.
Results may differ from the reference program's by a relative error of at most 0.001.
Values may be sent and summed in bfloat16 or wider, within the bound.
No kernel may reach another device: no remote copies, remote signals or barrier semaphores. Data moves between devices by JAX's collectives and lax.ppermute only.
A program may use at most 64 MiB of HBM per device.

```python
import math
import jax
import jax.numpy as jnp
from jax import lax

C = 64
TAPS = 27
BR_DEV = 2
BRICKS = 16
SCENES = 4


def draw_neighbours(key, part):
    devices = BRICKS // BR_DEV
    span_y = BR_DEV // 2
    keys = jax.random.split(jax.random.fold_in(key, 7), SCENES * devices)
    orders = jax.vmap(lambda one_key: jax.random.permutation(one_key, 2 * BR_DEV))(keys)
    orders = orders[:, :BR_DEV].astype(jnp.int32).reshape(SCENES, devices, BR_DEV)
    coord_x = orders // BR_DEV
    coord_y = orders % BR_DEV // 2
    coord_z = orders % 2
    device_ids = jnp.arange(devices, dtype=jnp.int32)[None, :, None]
    place_x = 2 * device_ids + coord_x
    brick_ids = device_ids * BR_DEV + jnp.arange(BR_DEV, dtype=jnp.int32)[None, None, :]
    brick_ids = jnp.broadcast_to(brick_ids, (SCENES, devices, BR_DEV))
    scene_ids = jnp.broadcast_to(jnp.arange(SCENES, dtype=jnp.int32)[:, None, None], (SCENES, devices, BR_DEV))
    grid_ids = jnp.full((SCENES, 2 * devices + 2, span_y + 2, 4), -1, jnp.int32)
    grid_ids = grid_ids.at[scene_ids, place_x + 1, coord_y + 1, coord_z + 1].set(brick_ids)
    found = []
    for off_x in range(3):
        for off_y in range(3):
            for off_z in range(3):
                found.append(grid_ids[scene_ids, place_x + off_x, coord_y + off_y, coord_z + off_z])
    return jnp.stack(found, axis=-1).reshape(SCENES, BRICKS, 27).astype(jnp.int32)


def set_ends(values, key, low, high):
    place = [jax.random.randint(jax.random.fold_in(key, axis), (), 0, length) for axis, length in enumerate(values.shape)]
    main_axis = values.shape.index(max(values.shape))
    next_to = place[:main_axis] + [(place[main_axis] + 1) % values.shape[main_axis]] + place[main_axis + 1:]
    return values.at[tuple(place)].set(low).at[tuple(next_to)].set(high)


def shard_levels(rng, extent, shards, smallest, high):
    def one(position, blocks):
        heights = jax.random.uniform(jax.random.fold_in(jax.random.fold_in(rng, 6), position), (blocks,), jnp.float32, smallest / len(shards), high / len(shards))
        return jnp.repeat(jnp.exp(heights), extent[position] // blocks).reshape((-1,) + (1,) * (len(extent) - position - 1))

    factor_of = one(*shards[0])
    for cut in shards[1:]:
        factor_of = factor_of * one(*cut)
    return factor_of


def gaussian(own_key, extent, width, bound, shards=(), kind=jnp.bfloat16):
    gain = shard_levels(own_key, extent, shards, -0.22, 0.18) if shards else 1.0
    values = jax.random.normal(own_key, extent, jnp.float32) * width * gain
    return jnp.minimum(jnp.maximum(values, -bound), bound).astype(kind)


def setup_inputs(seed: int = 0) -> dict:
    streams_of = jax.random.split(jax.random.key(seed), 6)
    features = gaussian(streams_of[0], (SCENES, BRICKS, C, 512), 1.0, 6.0, ((0, 4), (1, 8)))
    cotangent = gaussian(streams_of[1], (SCENES, BRICKS, C, 512), 1.0, 6.0, ((0, 4), (1, 8)))
    weight = gaussian(streams_of[2], (TAPS, C, C), (TAPS * C) ** -0.5, 0.15625)
    neighbours = draw_neighbours(jax.random.fold_in(streams_of[5], 71), 0)
    occupancy = set_ends((jax.random.randint(streams_of[4], (SCENES, BRICKS, 512), 0, 2) < 1).astype(jnp.int32), jax.random.fold_in(streams_of[4], 1), 0, 1)
    return dict(features=features, cotangent=cotangent, weight=weight, neighbours=neighbours, occupancy=occupancy)


def bounds(offset):
    if offset == 0:
        return (7, 8)
    if offset == 1:
        return (0, 8)
    return (0, 1)

def assemble(lookup, places):
    plane_list = []
    for off_x in range(3):
        x_low, x_high = bounds(off_x)
        row_list = []
        for off_y in range(3):
            y_low, y_high = bounds(off_y)
            cell_list = []
            for off_z in range(3):
                z_low, z_high = bounds(off_z)
                section = lookup[:, :, x_low:x_high, y_low:y_high, z_low:z_high]
                cell_list.append(jnp.take(section, places[:, 9 * off_x + 3 * off_y + off_z], axis=0))
            row_list.append(jnp.concatenate(cell_list, axis=4))
        plane_list.append(jnp.concatenate(row_list, axis=3))
    return jnp.concatenate(plane_list, axis=2)

def window(volume, start_x, start_y, start_z):
    bricks, channels = (volume.shape[0], volume.shape[1])
    return volume[:, :, start_x:start_x + 8, start_y:start_y + 8, start_z:start_z + 8].reshape(bricks, channels, 512)

def reference(features, cotangent, weight, neighbours, occupancy):
    channels = features.shape[2]
    grad_scale = 1.0 / math.sqrt(SCENES * BRICKS * 512)
    block_size = math.gcd(BRICKS, 64)
    w_wide = weight.astype(jnp.float32)
    outs_y = []
    outs_g = []
    grad_w = jnp.zeros((TAPS, channels, channels), jnp.float32)
    for scene_id in range(SCENES):
        present = occupancy[scene_id].astype(features.dtype)[:, None, :]
        masked_x = features[scene_id] * present
        masked_gradient = cotangent[scene_id] * present
        empty_zero_row = jnp.zeros((1, channels, 8, 8, 8), features.dtype)
        lookup_x = jnp.concatenate([masked_x.reshape(BRICKS, channels, 8, 8, 8), empty_zero_row], axis=0)
        lookup_g = jnp.concatenate([masked_gradient.reshape(BRICKS, channels, 8, 8, 8), empty_zero_row], axis=0)
        places = jnp.where(neighbours[scene_id] < 0, BRICKS, neighbours[scene_id]).astype(jnp.int32)

        def one_block(block_index):
            first_row = block_index * block_size
            near_ids = lax.dynamic_slice_in_dim(places, first_row, block_size, 0)
            vol_x = assemble(lookup_x, near_ids).astype(jnp.float32)
            vol_g = assemble(lookup_g, near_ids).astype(jnp.float32)
            here_g = lax.dynamic_slice_in_dim(masked_gradient, first_row, block_size, 0).astype(jnp.float32)
            here_m = lax.dynamic_slice_in_dim(present, first_row, block_size, 0).astype(jnp.float32)
            acc_y = jnp.zeros((block_size, channels, 512), jnp.float32)
            acc_g = jnp.zeros((block_size, channels, 512), jnp.float32)
            acc_w = []
            for tap_id in range(27):
                tap_x, tap_y, tap_z = (tap_id // 9, tap_id // 3 % 3, tap_id % 3)
                shifted = window(vol_x, tap_x, tap_y, tap_z)
                acc_y = acc_y + jnp.einsum('ncv,cd->ndv', shifted, w_wide[tap_id], preferred_element_type=jnp.float32)
                back_win = window(vol_g, 2 - tap_x, 2 - tap_y, 2 - tap_z)
                acc_g = acc_g + jnp.einsum('ndv,cd->ncv', back_win, w_wide[tap_id], preferred_element_type=jnp.float32)
                acc_w.append(jnp.einsum('ncv,ndv->cd', shifted, here_g, preferred_element_type=jnp.float32))
            return ((acc_y * here_m).astype(jnp.bfloat16), (acc_g * here_m).astype(jnp.bfloat16), jnp.stack(acc_w))
        y_blocks, g_blocks, w_blocks = lax.map(one_block, jnp.arange(BRICKS // block_size, dtype=jnp.int32))
        outs_y.append(y_blocks.reshape(BRICKS, channels, 512))
        outs_g.append(g_blocks.reshape(BRICKS, channels, 512))
        grad_w = grad_w + lax.optimization_barrier(jnp.sum(w_blocks, axis=0))
    return (jnp.stack(outs_y), jnp.stack(outs_g), grad_w * grad_scale)
```

```python
import functools
import math

import jax
import jax.numpy as jnp
import numpy as np
from jax import lax
from jax.experimental import pallas as pl
from jax.experimental.pallas import tpu as pltpu
from jax.sharding import PartitionSpec as P


TILE = 128
TILES = 4


def selection():
    out = np.zeros((4, 2, 64, 9, 2, 64), np.float32)
    for tap in range(9):
        ty, tz = tap // 3, tap % 3
        for j in range(8):
            for k in range(8):
                jj, kk = j + ty - 1, k + tz - 1
                group = (jj != jj % 8) + 2 * (kk != kk % 8)
                for half in range(2):
                    out[group, half, 8 * (jj % 8) + kk % 8, tap, half, 8 * j + k] = 1
    return out.reshape(4 * TILE, 9 * TILE)


def lane_of(shape):
    return lax.broadcasted_iota(jnp.int32, shape, len(shape) - 1)


def swap_halves(x):
    return pltpu.roll(x, 64, x.ndim - 1)


def volumes(near, values, mask, prev, after, select, own, low, high, parts, shifted):
    bricks, channels = values.shape[1], values.shape[2]
    zero = jnp.zeros((channels, TILE), jnp.bfloat16)
    for b in range(bricks):
        present = jnp.broadcast_to(mask[0, b : b + 1, :].astype(jnp.float32), (channels, 512)).astype(jnp.bfloat16)
        masked = values[0, b] * present
        own[b] = masked
        high[bricks + b] = masked[:, 3 * TILE :]
        low[b] = masked[:, :TILE]
        high[b] = prev[b]
        low[bricks + b] = after[b]
    own[bricks] = jnp.zeros((channels, 512), jnp.bfloat16)
    high[2 * bricks] = zero
    low[2 * bricks] = zero
    base = lax.axis_index("space") * bricks
    lane = lane_of((channels, TILE))
    j_high, k_high, first = lane % 64 >= 32, lane % 8 >= 4, lane < 64

    def grouped(pick):
        return (
            pick(0, 0),
            jnp.where(j_high, pick(-1, 0), pick(1, 0)),
            jnp.where(k_high, pick(0, -1), pick(0, 1)),
            jnp.where(
                j_high,
                jnp.where(k_high, pick(-1, -1), pick(-1, 1)),
                jnp.where(k_high, pick(1, -1), pick(1, 1)),
            ),
        )

    for b in range(bricks):

        def index(a, c, e, start, none):
            number = near[0, b, 9 * (a + 1) + 3 * (c + 1) + e + 1]
            return jnp.where(number < 0, none, number - start)

        here = {(c, e): index(0, c, e, base, bricks) for c in (-1, 0, 1) for e in (-1, 0, 1)}
        up = {(c, e): index(1, c, e, base, 2 * bricks) for c in (-1, 0, 1) for e in (-1, 0, 1)}
        down = {(c, e): index(-1, c, e, base - bricks, 2 * bricks) for c in (-1, 0, 1) for e in (-1, 0, 1)}
        for q in range(TILES + 1):
            if q < TILES:
                group = grouped(lambda c, e: own[here[c, e], :, q * TILE : (q + 1) * TILE])
            else:
                group = grouped(lambda c, e: jnp.where(first, low[up[c, e]], high[down[c, e]]))
            row = (b * (TILES + 1) + q) * channels
            for g in range(4):
                parts[row : row + channels, g * TILE : (g + 1) * TILE] = group[g]
    for tap in range(0, 9, 2):
        wide = min(2, 9 - tap)
        moved = jnp.dot(
            parts[...], select[:, tap * TILE : (tap + wide) * TILE], preferred_element_type=jnp.float32
        ).astype(jnp.bfloat16)
        for b in range(bricks):
            for q in range(TILES + 1):
                row = (b * (TILES + 1) + q) * channels
                for w in range(wide):
                    shifted[b, (tap + w) * channels : (tap + w + 1) * channels, q * TILE : (q + 1) * TILE] = moved[
                        row : row + channels, w * TILE : (w + 1) * TILE
                    ]


def volume_scratch(bricks, channels):
    return [
        pltpu.VMEM((bricks + 1, channels, 512), jnp.bfloat16),
        pltpu.VMEM((2 * bricks + 1, channels, TILE), jnp.bfloat16),
        pltpu.VMEM((2 * bricks + 1, channels, TILE), jnp.bfloat16),
        pltpu.VMEM((bricks * (TILES + 1) * channels, 4 * TILE), jnp.bfloat16),
        pltpu.VMEM((bricks, 9 * channels, (TILES + 1) * TILE), jnp.bfloat16),
    ]


def weight_kernel(scale, near, values, gradient, mask, prev, after, select, out, own, low, high, parts, shifted, placed):
    volumes(near, values, mask, prev, after, select, own, low, high, parts, shifted)
    bricks, channels = values.shape[1], values.shape[2]
    lane = lane_of((channels, TILE))
    first = lane < 64
    zero = jnp.zeros((channels, TILE), jnp.float32)
    for b in range(bricks):
        masked = gradient[0, b].astype(jnp.float32) * mask[0, b : b + 1, :].astype(jnp.float32)
        tile = [masked[:, q * TILE : (q + 1) * TILE] for q in range(TILES)]
        back = [swap_halves(jnp.where(first, tile[q + 1] if q < 3 else zero, tile[q])) for q in range(TILES)]
        back.append(swap_halves(jnp.where(first, tile[0], zero)))
        ahead = [swap_halves(jnp.where(first, tile[q], tile[q - 1] if q else zero)) for q in range(TILES)]
        ahead.append(swap_halves(jnp.where(first, zero, tile[3])))
        for q in range(TILES + 1):
            at = slice(q * TILE, (q + 1) * TILE)
            placed[b, :channels, at] = back[q].astype(jnp.bfloat16)
            placed[b, channels : 2 * channels, at] = (tile[q] if q < TILES else zero).astype(jnp.bfloat16)
            placed[b, 2 * channels :, at] = ahead[q].astype(jnp.bfloat16)
    rows = 9 * channels
    contract = (((1,), (1,)), ((), ()))
    total = None
    for b in range(bricks):
        term = lax.dot_general(shifted[b], placed[b], contract, preferred_element_type=jnp.float32)
        total = term if total is None else total + term
    total = total * scale
    out[:rows, :] = total[:, : 2 * channels]
    third = total[:, 2 * channels :]
    out[rows:, :channels] = third[: rows // 2]
    out[rows:, channels:] = third[rows // 2 :]


def conv_kernel(near, values, mask, prev, after, select, weight, out, own, low, high, parts, shifted):
    volumes(near, values, mask, prev, after, select, own, low, high, parts, shifted)
    bricks, channels = values.shape[1], values.shape[2]
    first = lane_of((channels, TILE)) < 64
    for b in range(bricks):
        terms = jnp.dot(weight[...], shifted[b], preferred_element_type=jnp.float32)

        def term(t, q):
            q = q % (TILES + 1)
            return terms[t * channels : (t + 1) * channels, q * TILE : (q + 1) * TILE]

        for q in range(TILES):
            sides = jnp.where(first, term(0, q), term(0, q - 1)) + jnp.where(first, term(2, q + 1), term(2, q))
            at = slice(q * TILE, (q + 1) * TILE)
            present = mask[0, b : b + 1, at].astype(jnp.float32)
            out[0, b, :, at] = ((term(1, q) + swap_halves(sides)) * present).astype(jnp.bfloat16)


def local(features, cotangent, weight, neighbours, occupancy):
    bricks, channels = features.shape[1], features.shape[2]
    spaces, scenes = lax.axis_size("space"), lax.axis_size("scene")
    scale = 1.0 / math.sqrt(scenes * bricks * spaces * 512)
    present = occupancy[0].astype(jnp.bfloat16)[:, None, :]
    both = jnp.stack([features[0], cotangent[0]])
    ahead = [(i, i + 1) for i in range(spaces - 1)]
    behind = [(i + 1, i) for i in range(spaces - 1)]
    from_prev = lax.ppermute(both[..., 384:] * present[..., 384:], "space", ahead)
    from_after = lax.ppermute(both[..., :TILE] * present[..., :TILE], "space", behind)
    select = jnp.asarray(selection(), jnp.bfloat16)

    smem = pl.BlockSpec(memory_space=pltpu.SMEM)
    vmem = pl.BlockSpec(memory_space=pltpu.VMEM)
    params = pltpu.CompilerParams(vmem_limit_bytes=40 << 20)
    rows = 27 * channels // 2
    grad_w = pl.pallas_call(
        functools.partial(weight_kernel, scale),
        out_shape=jax.ShapeDtypeStruct((rows, 2 * channels), jnp.float32),
        in_specs=[smem] + [vmem] * 6,
        out_specs=vmem,
        scratch_shapes=volume_scratch(bricks, channels)
        + [pltpu.VMEM((bricks, 3 * channels, (TILES + 1) * TILE), jnp.bfloat16)],
        compiler_params=params,
        name="grad_weight",
    )(neighbours, features, cotangent, occupancy, from_prev[0], from_after[0], select)

    def conv(values, side, table, name):
        return pl.pallas_call(
            conv_kernel,
            out_shape=jax.ShapeDtypeStruct(values.shape, jnp.bfloat16),
            in_specs=[smem] + [vmem] * 6,
            out_specs=vmem,
            scratch_shapes=volume_scratch(bricks, channels),
            compiler_params=params,
            cost_estimate=pl.CostEstimate(flops=2 * 10**9, bytes_accessed=10**6, transcendentals=0),
            name=name,
        )(neighbours, values, occupancy, from_prev[side], from_after[side], select, table)

    taps = weight.reshape(3, 9, channels, channels)
    table_y = taps.transpose(0, 3, 1, 2).reshape(3 * channels, 9 * channels)
    table_g = taps[::-1, ::-1].transpose(0, 2, 1, 3).reshape(3 * channels, 9 * channels)
    out_y = conv(features, 0, table_y, "conv_out")
    out_g = conv(cotangent, 1, table_g, "grad_features")
    summed = all_sum(grad_w, spaces, scenes)
    pairs = summed[: 9 * channels].reshape(9, channels, 2, channels).transpose(2, 0, 1, 3)
    third = summed[9 * channels :].reshape(-1, 2, channels).transpose(1, 0, 2).reshape(1, 9, channels, channels)
    return out_y, out_g, jnp.concatenate([pairs, third]).reshape(27, channels, channels)


def all_sum(part, spaces, scenes):
    count = spaces * scenes
    if count & (count - 1):
        return lax.psum(part, ("space", "scene"))
    axes = ("space", "scene")
    me = lax.axis_index("space") * scenes + lax.axis_index("scene")

    def exchange(x, bit):
        return lax.ppermute(x, axes, [(i, i ^ bit) for i in range(count)])

    half = part.shape[0] // 2
    odd = me % 2
    keep = lax.dynamic_slice_in_dim(part, odd * half, half, 0)
    send = lax.dynamic_slice_in_dim(part, (1 - odd) * half, half, 0)
    mine = keep + exchange(send, 1)
    bits = [1 << n for n in range(1, count.bit_length() - 1)]
    turned = bits[len(bits) // 2 :] + bits[: len(bits) // 2]
    cut = half // 16 * 8
    pieces = [mine[:cut], mine[cut:]]
    for first, second in zip(bits, turned):
        pieces = [pieces[0] + exchange(pieces[0], first), pieces[1] + exchange(pieces[1], second)]
    mine = jnp.concatenate(pieces)
    theirs = exchange(mine, 1)
    low = jnp.where(odd == 0, mine, theirs)
    high = jnp.where(odd == 0, theirs, mine)
    return jnp.concatenate([low, high])


def solution(mesh):
    in_specs = (
        P("scene", "space", None, None),
        P("scene", "space", None, None),
        P(),
        P("scene", "space", None),
        P("scene", "space", None),
    )
    out_specs = (P("scene", "space", None, None), P("scene", "space", None, None), P())
    return jax.shard_map(local, mesh=mesh, in_specs=in_specs, out_specs=out_specs, check_vma=False)
```

```python
import functools
import math

import jax
import jax.numpy as jnp
from jax import lax
from jax.experimental import pallas as pl
from jax.experimental.pallas import tpu as pltpu
from jax.sharding import PartitionSpec as P


TILE = 128
TILES = 4
AXES = ("space", "scene")
SMEM = pl.BlockSpec(memory_space=pltpu.SMEM)
VMEM = pl.BlockSpec(memory_space=pltpu.VMEM)
HBM = pl.BlockSpec(memory_space=pltpu.HBM)
SIDES = [(c, e) for c in (-1, 0, 1) for e in (-1, 0, 1)]


def set_selection(select_y, select_z):
    row = lax.broadcasted_iota(jnp.int32, (TILE, TILE), 0)
    lane = lax.broadcasted_iota(jnp.int32, (TILE, TILE), 1)
    for select, step in ((select_y, 8), (select_z, 1)):
        now = lane // step % 8
        for t in range(3):
            moved = now + t - 1
            wanted = lane + step * (jnp.bitwise_and(moved, 7) - now)
            beyond = jnp.where(moved == jnp.bitwise_and(moved, 7), 0, 1)
            for source in range(2):
                hit = jnp.where(beyond == source, wanted, -1) == row
                select[source * TILE : (source + 1) * TILE, t * TILE : (t + 1) * TILE] = jnp.where(
                    hit, 1.0, 0.0
                ).astype(jnp.bfloat16)


def lane_of(shape):
    return lax.broadcasted_iota(jnp.int32, shape, len(shape) - 1)


def swap_halves(x):
    return pltpu.roll(x, 64, x.ndim - 1)


def on_even():
    return lax.axis_index("space") % 2 == 0


def set_groups(parts, row, pick):
    channels, rows = pick(0, 0).shape[0], parts.shape[0] // 2
    lane = lane_of((channels, TILE))
    j_high, k_high = lane % 64 >= 32, lane % 8 >= 4
    parts[row : row + channels, :TILE] = pick(0, 0)
    parts[row : row + channels, TILE:] = jnp.where(j_high, pick(-1, 0), pick(1, 0))
    row = rows + row
    parts[row : row + channels, :TILE] = jnp.where(k_high, pick(0, -1), pick(0, 1))
    parts[row : row + channels, TILE:] = jnp.where(
        j_high,
        jnp.where(k_high, pick(-1, -1), pick(-1, 1)),
        jnp.where(k_high, pick(1, -1), pick(1, 1)),
    )


def index_of(near, b, a, c, e, start, none):
    number = near[0, b, 9 * (a + 1) + 3 * (c + 1) + e + 1]
    return jnp.where(number < 0, none, number - start)


def shift_all(parts, select_y, select_z, middle, shifted, tiles):
    bricks, channels, rows = shifted.shape[0], shifted.shape[1] // 9, parts.shape[0] // 2
    for side in range(2):
        moved = jnp.dot(
            parts[side * rows : (side + 1) * rows, :], select_y[...], preferred_element_type=jnp.float32
        ).astype(jnp.bfloat16)
        for t in range(3):
            middle[t * rows : (t + 1) * rows, side * TILE : (side + 1) * TILE] = moved[:, t * TILE : (t + 1) * TILE]
    for ty in range(3):
        moved = jnp.dot(
            middle[ty * rows : (ty + 1) * rows, :], select_z[...], preferred_element_type=jnp.float32
        ).astype(jnp.bfloat16)
        for b in range(bricks):
            for q in range(tiles):
                row = (b * tiles + q) * channels
                for tz in range(3):
                    tap = 3 * ty + tz
                    shifted[b, tap * channels : (tap + 1) * channels, q * TILE : (q + 1) * TILE] = moved[
                        row : row + channels, tz * TILE : (tz + 1) * TILE
                    ]


def inner_parts(near, own, parts):
    bricks, channels = own.shape[0] - 1, own.shape[1]
    base = lax.axis_index("space") * bricks
    for b in range(bricks):
        here = {s: index_of(near, b, 0, *s, base, bricks) for s in SIDES}
        for q in range(TILES):
            set_groups(
                parts, (b * TILES + q) * channels, lambda c, e: own[here[c, e], :, q * TILE : (q + 1) * TILE]
            )


def outer_parts(near, side, first, second, from_first, from_second, low, high, parts):
    bricks, channels = first.shape[0], first.shape[1]
    even = on_even()
    zero = jnp.zeros((channels, TILE), jnp.bfloat16)

    def placed(x):
        return swap_halves(x.astype(jnp.float32)).astype(jnp.bfloat16) if side else x

    for b in range(bricks):
        high[b] = placed(jnp.where(even, from_second[b], from_first[b]))
        high[bricks + b] = placed(jnp.where(even, first[b], second[b]))
        low[b] = placed(jnp.where(even, second[b], first[b]))
        low[bricks + b] = placed(jnp.where(even, from_first[b], from_second[b]))
    high[2 * bricks] = zero
    low[2 * bricks] = zero
    base = lax.axis_index("space") * bricks
    lower = lane_of((channels, TILE)) < 64
    for b in range(bricks):
        up = {s: index_of(near, b, 1, *s, base, 2 * bricks) for s in SIDES}
        down = {s: index_of(near, b, -1, *s, base - bricks, 2 * bricks) for s in SIDES}
        set_groups(parts, b * channels, lambda c, e: jnp.where(lower, low[up[c, e]], high[down[c, e]]))


def faces_kernel(features, cotangent, mask, near, first, second, own_x, own_g, present, near_out, *rest):
    buffers, sems = rest[:3], rest[3]
    copies = [pltpu.make_async_copy(a, b, sems.at[n]) for n, (a, b) in enumerate(zip((mask, features, cotangent), buffers))]
    copies.append(pltpu.make_async_copy(near, near_out, sems.at[3]))
    for copy in copies:
        copy.start()
    even = on_even()
    bricks, channels = own_x.shape[0] - 1, own_x.shape[1]
    lower = lane_of((channels, TILE)) < 64
    copies[0].wait()
    present[...] = buffers[0][0].astype(jnp.float32)
    for side, own in enumerate((own_x, own_g)):
        copies[1 + side].wait()
        for b in range(bricks):
            own[b] = buffers[1 + side][0, b] * jnp.broadcast_to(present[b : b + 1, :], (channels, 512)).astype(
                jnp.bfloat16
            )
        own[bricks] = jnp.zeros((channels, 512), jnp.bfloat16)
    for b in range(bricks):
        x, g = own_x[b].astype(jnp.float32), own_g[b].astype(jnp.float32)
        head = jnp.where(lower, x[:, :TILE], swap_halves(g[:, :TILE])).astype(jnp.bfloat16)
        tail = jnp.where(lower, swap_halves(g[:, 3 * TILE :]), x[:, 3 * TILE :]).astype(jnp.bfloat16)
        first[b] = jnp.where(even, tail, head)
        second[b] = jnp.where(even, head, tail)
    copies[3].wait()


def inner_kernel(scale, near, own, gradient, shifted, grad, parts, middle, select_y, select_z, placed):
    rows, bricks, channels = grad.shape[0], own.shape[0] - 1, own.shape[1]
    set_selection(select_y, select_z)
    inner_parts(near, own, parts)
    lower = lane_of((channels, TILE)) < 64
    zero = jnp.zeros((channels, TILE), jnp.float32)
    for b in range(bricks):
        masked = gradient[b].astype(jnp.float32)
        tile = [zero] + [masked[:, q * TILE : (q + 1) * TILE] for q in range(TILES)] + [zero]
        for q in range(TILES):
            at = slice(q * TILE, (q + 1) * TILE)
            placed[b, :channels, at] = swap_halves(jnp.where(lower, tile[q + 2], tile[q + 1])).astype(jnp.bfloat16)
            placed[b, channels : 2 * channels, at] = swap_halves(jnp.where(lower, tile[q + 1], tile[q])).astype(
                jnp.bfloat16
            )
            placed[b, 2 * channels :, at] = tile[q + 1].astype(jnp.bfloat16)
    shift_all(parts, select_y, select_z, middle, shifted, TILES)
    total = None
    for b in range(bricks):
        term = lax.dot_general(
            shifted[b], placed[b], (((1,), (1,)), ((), ())), preferred_element_type=jnp.float32
        )
        total = term if total is None else total + term
    total = total * scale
    count, half = 9 * channels, 9 * channels // 2
    grad[:count, :] = total[:, : 2 * channels]
    grad[count : count + half, :channels] = total[:half, 2 * channels :]
    grad[count : count + half, channels:] = total[half:, 2 * channels :]
    if rows > count + half:
        grad[count + half :, :] = jnp.zeros((rows - count - half, 2 * channels), jnp.float32)


def outer_kernel(
    scale, near, first, second, from_first, from_second, inner, shifted, grad,
    low, high, parts, middle, select_y, select_z,
):
    bricks, channels = first.shape[0], first.shape[1]
    set_selection(select_y, select_z)
    outer_parts(near, 0, first, second, from_first, from_second, low, high, parts)
    shift_all(parts, select_y, select_z, middle, shifted, 1)
    even = on_even()
    lower = lane_of((channels, TILE)) < 64
    total = None
    for b in range(bricks):
        head = jnp.where(even, second[b], first[b])
        tail = jnp.where(even, first[b], second[b])
        ends = jnp.concatenate([jnp.where(lower, 0, head), jnp.where(lower, tail, 0)], axis=0)
        term = lax.dot_general(shifted[b], ends, (((1,), (1,)), ((), ())), preferred_element_type=jnp.float32)
        total = term if total is None else total + term
    count = 9 * channels
    grad[:count, :] = inner[:count, :] + total * scale
    grad[count:, :] = inner[count:, :]


def tables_kernel(weight, table_y, table_g):
    channels = weight.shape[1]
    for tx in range(3):
        for yz in range(9):
            at = (slice(tx * channels, (tx + 1) * channels), slice(yz * channels, (yz + 1) * channels))
            table_y[at] = weight[9 * tx + yz].astype(jnp.float32).T.astype(jnp.bfloat16)
            table_g[at] = weight[26 - 9 * tx - yz]


def convolve(table, inner, outer, present, out):
    bricks, channels = out.shape[1], out.shape[2]
    lower = lane_of((channels, TILE)) < 64
    for b in range(bricks):
        main = jnp.dot(table[...], inner[b], preferred_element_type=jnp.float32)
        ends = jnp.dot(table[...], outer[b], preferred_element_type=jnp.float32)

        def term(t, q):
            rows = slice(t * channels, (t + 1) * channels)
            return main[rows, q * TILE : (q + 1) * TILE] if 0 <= q < TILES else ends[rows]

        for q in range(TILES):
            sides = jnp.where(lower, term(0, q), term(0, q - 1)) + jnp.where(lower, term(2, q + 1), term(2, q))
            at = slice(q * TILE, (q + 1) * TILE)
            out[0, b, :, at] = ((term(1, q) + swap_halves(sides)) * present[b : b + 1, at]).astype(jnp.bfloat16)


def backward_kernel(
    near, own, present, first, second, from_first, from_second, table, out,
    parts, middle, low, high, end_parts, end_middle, select_y, select_z, inner, outer,
):
    set_selection(select_y, select_z)
    inner_parts(near, own, parts)
    outer_parts(near, 1, first, second, from_first, from_second, low, high, end_parts)
    shift_all(parts, select_y, select_z, middle, inner, TILES)
    shift_all(end_parts, select_y, select_z, end_middle, outer, 1)
    convolve(table, inner, outer, present, out)


def unpack_kernel(groups, mine, theirs, out, whole):
    place = lax.axis_index("space") * lax.axis_size("scene") + lax.axis_index("scene")
    odd = place % 2
    where = place // 2 % groups
    size = mine.shape[0] // groups
    for k in range(groups):
        chunk = jnp.bitwise_xor(where, k)
        at = pl.multiple_of((odd * groups + chunk) * size, 8)
        whole[pl.ds(at, size), :] = mine[k * size : (k + 1) * size, :]
        at = pl.multiple_of(((1 - odd) * groups + chunk) * size, 8)
        whole[pl.ds(at, size), :] = theirs[k * size : (k + 1) * size, :]
    channels = out.shape[1]
    count, half = 9 * channels, 9 * channels // 2
    for yz in range(9):
        both = whole[yz * channels : (yz + 1) * channels, :]
        out[yz] = both[:, :channels]
        out[18 + yz] = both[:, channels:]
    for row in range(0, half, 32):
        both = whole[count + row : count + row + 32, :]
        for side in range(2):
            at = row + side * half
            out[9 + at // channels, at % channels : at % channels + 32, :] = both[
                :, side * channels : (side + 1) * channels
            ]


def exchange(x, bit):
    count = lax.axis_size("space") * lax.axis_size("scene")
    return lax.ppermute(x, AXES, [(i, i ^ bit) for i in range(count)])


def all_sum(part, groups):
    count = lax.axis_size("space") * lax.axis_size("scene")
    place = lax.axis_index("space") * lax.axis_size("scene") + lax.axis_index("scene")
    odd, where = place % 2, place // 2 % groups
    half = part.shape[0] // 2
    size = half // groups
    keep = lax.dynamic_slice_in_dim(part, odd * half, half, 0)
    send = lax.dynamic_slice_in_dim(part, (1 - odd) * half, half, 0)
    mine = keep + exchange(send, 1)
    own = lax.dynamic_slice_in_dim(mine, where * size, size, 0)
    got = []
    for k in range(1, groups):
        got.append(exchange(lax.dynamic_slice_in_dim(mine, (where ^ k) * size, size, 0), 2 * k))
    for one in got:
        own = own + one
    bit = 2 * groups
    while bit < count:
        wide = 4 if 4 * bit <= count else 2
        got = []
        for k in range(1, wide):
            got.append(exchange(own, bit * k))
        own = own + got[0]
        if wide == 4:
            own = own + (got[1] + got[2])
        bit *= wide
    chunks = [own]
    for k in range(1, groups):
        chunks.append(exchange(own, 2 * k))
    mine = jnp.concatenate(chunks)
    return mine, exchange(mine, 1)


def program(features, cotangent, weight, neighbours, occupancy):
    bricks, channels = features.shape[1], features.shape[2]
    spaces, scenes = lax.axis_size("space"), lax.axis_size("scene")
    scale = 1.0 / math.sqrt(scenes * bricks * spaces * 512)
    groups = 4
    unit = 16 * groups
    rows = -(-(27 * channels // 2) // unit) * unit

    def call(kernel, shapes, inputs, specs, scratch, limit=32 << 20):
        single = not isinstance(shapes, list)
        return pl.pallas_call(
            kernel,
            out_shape=shapes,
            in_specs=specs,
            out_specs=VMEM if single else [VMEM] * len(shapes),
            scratch_shapes=scratch,
            compiler_params=pltpu.CompilerParams(vmem_limit_bytes=limit),
            cost_estimate=pl.CostEstimate(flops=10**8, bytes_accessed=10**6, transcendentals=0),
        )(*inputs)

    def shape(*dims, dtype=jnp.bfloat16):
        return jax.ShapeDtypeStruct(dims, dtype)

    def scratch(*dims, dtype=jnp.bfloat16):
        return pltpu.VMEM(dims, dtype)

    many = bricks * TILES * channels
    parts = [scratch(2 * many, 2 * TILE), scratch(3 * many, 2 * TILE)]
    few = bricks * channels
    ends = [
        scratch(2 * bricks + 1, channels, TILE),
        scratch(2 * bricks + 1, channels, TILE),
        scratch(2 * few, 2 * TILE),
        scratch(3 * few, 2 * TILE),
    ]
    select = [scratch(2 * TILE, 3 * TILE)] * 2
    face, brick = shape(bricks, channels, TILE), shape(bricks + 1, channels, 512)
    first, second, own_x, own_g, present, near = call(
        faces_kernel,
        [face, face, brick, brick, shape(bricks, 512, dtype=jnp.float32), shape(*neighbours.shape, dtype=jnp.int32)],
        (features, cotangent, occupancy, neighbours),
        [HBM] * 4,
        [
            scratch(*occupancy.shape, dtype=jnp.int32),
            scratch(*features.shape),
            scratch(*features.shape),
            pltpu.SemaphoreType.DMA((4,)),
        ],
        limit=None,
    )
    pairs = [[(i, i + 1), (i + 1, i)] for i in range(spaces - 1)]
    from_first = lax.ppermute(first, "space", sum(pairs[0::2], []))
    from_second = lax.ppermute(second, "space", sum(pairs[1::2], []))
    halo = (first, second, from_first, from_second)
    inner, grad = call(
        functools.partial(inner_kernel, scale),
        [shape(bricks, 9 * channels, 512), shape(rows, 2 * channels, dtype=jnp.float32)],
        (near, own_x, own_g),
        [SMEM, VMEM, VMEM],
        [*parts, *select, scratch(bricks, 3 * channels, 512)],
    )
    outer, grad = call(
        functools.partial(outer_kernel, scale),
        [shape(bricks, 9 * channels, TILE), shape(rows, 2 * channels, dtype=jnp.float32)],
        (near, *halo, grad),
        [SMEM] + [VMEM] * 5,
        [*ends, *select],
    )
    table = shape(3 * channels, 9 * channels)
    table_y, table_g = call(tables_kernel, [table, table], (weight,), [VMEM], [])
    out_y = call(convolve, shape(*features.shape), (table_y, inner, outer, present), [VMEM] * 4, [])
    out_g = call(
        backward_kernel,
        shape(*cotangent.shape),
        (near, own_g, present, *halo, table_g),
        [SMEM] + [VMEM] * 7,
        [*parts, *ends, *select, scratch(bricks, 9 * channels, 512), scratch(bricks, 9 * channels, TILE)],
    )
    mine, theirs = all_sum(grad, groups)
    out_w = call(
        functools.partial(unpack_kernel, groups),
        shape(27, channels, channels, dtype=jnp.float32),
        (mine, theirs),
        [VMEM] * 2,
        [pltpu.VMEM((rows, 2 * channels), jnp.float32)],
    )
    return out_y, out_g, out_w


def solution(mesh):
    in_specs = (
        P("scene", "space", None, None),
        P("scene", "space", None, None),
        P(),
        P("scene", "space", None),
        P("scene", "space", None),
    )
    out_specs = (P("scene", "space", None, None), P("scene", "space", None, None), P())
    return jax.shard_map(program, mesh=mesh, in_specs=in_specs, out_specs=out_specs, check_vma=False)
```

```python
import functools
import math

import jax
import jax.numpy as jnp
from jax import lax
from jax.experimental import pallas as pl
from jax.experimental.pallas import tpu as pltpu
from jax.sharding import PartitionSpec as P


TILE = 128
TILES = 4
AXES = ("space", "scene")
SMEM = pl.BlockSpec(memory_space=pltpu.SMEM)
VMEM = pl.BlockSpec(memory_space=pltpu.VMEM)
HBM = pl.BlockSpec(memory_space=pltpu.HBM)
SIDES = [(c, e) for c in (-1, 0, 1) for e in (-1, 0, 1)]


def set_selection(select_y, select_z):
    row = lax.broadcasted_iota(jnp.int32, (TILE, TILE), 0)
    lane = lax.broadcasted_iota(jnp.int32, (TILE, TILE), 1)
    for select, step in ((select_y, 8), (select_z, 1)):
        now = lane // step % 8
        for t in range(3):
            moved = now + t - 1
            wanted = lane + step * (jnp.bitwise_and(moved, 7) - now)
            beyond = jnp.where(moved == jnp.bitwise_and(moved, 7), 0, 1)
            for source in range(2):
                hit = jnp.where(beyond == source, wanted, -1) == row
                select[source * TILE : (source + 1) * TILE, t * TILE : (t + 1) * TILE] = jnp.where(
                    hit, 1.0, 0.0
                ).astype(jnp.bfloat16)


def lane_of(shape):
    return lax.broadcasted_iota(jnp.int32, shape, len(shape) - 1)


def swap_halves(x):
    return pltpu.roll(x, 64, x.ndim - 1)


def set_groups(parts, row, pick):
    channels, rows = pick(0, 0).shape[0], parts.shape[0] // 2
    lane = lane_of((channels, TILE))
    j_high, k_high = lane % 64 >= 32, lane % 8 >= 4
    parts[row : row + channels, :TILE] = pick(0, 0)
    parts[row : row + channels, TILE:] = jnp.where(j_high, pick(-1, 0), pick(1, 0))
    row = rows + row
    parts[row : row + channels, :TILE] = jnp.where(k_high, pick(0, -1), pick(0, 1))
    parts[row : row + channels, TILE:] = jnp.where(
        j_high,
        jnp.where(k_high, pick(-1, -1), pick(-1, 1)),
        jnp.where(k_high, pick(1, -1), pick(1, 1)),
    )


def index_of(near, b, a, c, e, start, none):
    number = near[0, b, 9 * (a + 1) + 3 * (c + 1) + e + 1]
    return jnp.where(number < 0, none, number - start)


def shift_all(parts, select_y, select_z, middle, shifted, tiles):
    bricks, channels, rows = shifted.shape[0], shifted.shape[1] // 9, parts.shape[0] // 2
    for side in range(2):
        moved = jnp.dot(
            parts[side * rows : (side + 1) * rows, :], select_y[...], preferred_element_type=jnp.float32
        ).astype(jnp.bfloat16)
        for t in range(3):
            middle[t * rows : (t + 1) * rows, side * TILE : (side + 1) * TILE] = moved[:, t * TILE : (t + 1) * TILE]
    for ty in range(3):
        moved = jnp.dot(
            middle[ty * rows : (ty + 1) * rows, :], select_z[...], preferred_element_type=jnp.float32
        ).astype(jnp.bfloat16)
        for b in range(bricks):
            for q in range(tiles):
                row = (b * tiles + q) * channels
                for tz in range(3):
                    tap = 3 * ty + tz
                    shifted[b, tap * channels : (tap + 1) * channels, q * TILE : (q + 1) * TILE] = moved[
                        row : row + channels, tz * TILE : (tz + 1) * TILE
                    ]


def inner_parts(near, own, parts):
    bricks, channels = own.shape[0] - 1, own.shape[1]
    base = lax.axis_index("space") * bricks
    for b in range(bricks):
        here = {s: index_of(near, b, 0, *s, base, bricks) for s in SIDES}
        for q in range(TILES):
            set_groups(
                parts, (b * TILES + q) * channels, lambda c, e: own[here[c, e], :, q * TILE : (q + 1) * TILE]
            )


def set_ends(near, a, mine, other, table, parts):
    bricks, channels = mine.shape[0], mine.shape[1]
    for b in range(bricks):
        table[b] = (other if a < 0 else mine)[b]
        table[bricks + b] = (mine if a < 0 else other)[b]
    table[2 * bricks] = jnp.zeros((channels, TILE), jnp.bfloat16)
    start = (lax.axis_index("space") + min(a, 0)) * bricks
    for b in range(bricks):
        at = {s: index_of(near, b, a, *s, start, 2 * bricks) for s in SIDES}
        set_groups(parts, b * channels, lambda c, e: table[at[c, e]])


def faces_kernel(features, cotangent, mask, near, head, tail, own_x, own_g, present, near_out, *rest):
    buffers, sems = rest[:3], rest[3]
    copies = [pltpu.make_async_copy(a, b, sems.at[n]) for n, (a, b) in enumerate(zip((mask, features, cotangent), buffers))]
    copies.append(pltpu.make_async_copy(near, near_out, sems.at[3]))
    for copy in copies:
        copy.start()
    bricks, channels = own_x.shape[0] - 1, own_x.shape[1]
    lower = lane_of((channels, TILE)) < 64
    copies[0].wait()
    present[...] = buffers[0][0].astype(jnp.float32)
    for side, own in enumerate((own_x, own_g)):
        copies[1 + side].wait()
        for b in range(bricks):
            own[b] = buffers[1 + side][0, b] * jnp.broadcast_to(present[b : b + 1, :], (channels, 512)).astype(
                jnp.bfloat16
            )
        own[bricks] = jnp.zeros((channels, 512), jnp.bfloat16)
    for b in range(bricks):
        x, g = own_x[b].astype(jnp.float32), own_g[b].astype(jnp.float32)
        head[b] = jnp.where(lower, x[:, :TILE], swap_halves(g[:, :TILE])).astype(jnp.bfloat16)
        tail[b] = jnp.where(lower, swap_halves(g[:, 3 * TILE :]), x[:, 3 * TILE :]).astype(jnp.bfloat16)
    copies[3].wait()


def inner_kernel(scale, near, own, gradient, shifted, grad, parts, middle, select_y, select_z, placed):
    rows, bricks, channels = grad.shape[0], own.shape[0] - 1, own.shape[1]
    set_selection(select_y, select_z)
    inner_parts(near, own, parts)
    lower = lane_of((channels, TILE)) < 64
    zero = jnp.zeros((channels, TILE), jnp.float32)
    for b in range(bricks):
        masked = gradient[b].astype(jnp.float32)
        tile = [zero] + [masked[:, q * TILE : (q + 1) * TILE] for q in range(TILES)] + [zero]
        for q in range(TILES):
            at = slice(q * TILE, (q + 1) * TILE)
            placed[b, :channels, at] = swap_halves(jnp.where(lower, tile[q + 2], tile[q + 1])).astype(jnp.bfloat16)
            placed[b, channels : 2 * channels, at] = swap_halves(jnp.where(lower, tile[q + 1], tile[q])).astype(
                jnp.bfloat16
            )
            placed[b, 2 * channels :, at] = tile[q + 1].astype(jnp.bfloat16)
    shift_all(parts, select_y, select_z, middle, shifted, TILES)
    total = None
    for b in range(bricks):
        term = lax.dot_general(
            shifted[b], placed[b], (((1,), (1,)), ((), ())), preferred_element_type=jnp.float32
        )
        total = term if total is None else total + term
    total = total * scale
    count, half = 9 * channels, 9 * channels // 2
    grad[:count, :] = total[:, : 2 * channels]
    grad[count : count + half, :channels] = total[:half, 2 * channels :]
    grad[count : count + half, channels:] = total[half:, 2 * channels :]
    if rows > count + half:
        grad[count + half :, :] = jnp.zeros((rows - count - half, 2 * channels), jnp.float32)


def outer_kernel(
    scale, near, head, tail, below, inner, shifted, grad, table, parts, middle, select_y, select_z
):
    bricks, channels = head.shape[0], head.shape[1]
    set_selection(select_y, select_z)
    set_ends(near, -1, tail, below, table, parts)
    shift_all(parts, select_y, select_z, middle, shifted, 1)
    lower = lane_of((channels, TILE)) < 64
    contract = (((1,), (1,)), ((), ()))
    first = last = None
    for b in range(bricks):
        g, x = jnp.where(lower, 0, head[b]), jnp.where(lower, head[b], 0)
        one = lax.dot_general(shifted[b], g, contract, preferred_element_type=jnp.float32)
        two = lax.dot_general(x, shifted[b], contract, preferred_element_type=jnp.float32)
        first, last = (one, two) if b == 0 else (first + one, last + two)
    for yz in range(9):
        at = slice(yz * channels, (yz + 1) * channels)
        back = slice((8 - yz) * channels, (9 - yz) * channels)
        grad[at, :] = inner[at, :] + jnp.concatenate([first[at], last[:, back]], axis=1) * scale
    grad[9 * channels :, :] = inner[9 * channels :, :]


def shift_kernel(near, own, shifted, parts, middle, select_y, select_z):
    set_selection(select_y, select_z)
    inner_parts(near, own, parts)
    shift_all(parts, select_y, select_z, middle, shifted, TILES)


def tables_kernel(weight, table_y, table_g):
    channels = weight.shape[1]
    for tx in range(3):
        for yz in range(9):
            at = (slice(tx * channels, (tx + 1) * channels), slice(yz * channels, (yz + 1) * channels))
            table_y[at] = weight[9 * tx + yz].astype(jnp.float32).T.astype(jnp.bfloat16)
            table_g[at] = weight[26 - 9 * tx - yz]


def convolve(table, inner, ends, present, out, swapped):
    bricks, channels = out.shape[1], out.shape[2]
    lower = lane_of((channels, TILE)) < 64
    for b in range(bricks):
        main = jnp.dot(table[...], inner[b], preferred_element_type=jnp.float32)
        side = jnp.dot(table[...], ends(b), preferred_element_type=jnp.float32)
        if swapped:
            side = swap_halves(side)

        def term(t, q):
            rows = slice(t * channels, (t + 1) * channels)
            return main[rows, q * TILE : (q + 1) * TILE] if 0 <= q < TILES else side[rows]

        for q in range(TILES):
            sides = jnp.where(lower, term(0, q), term(0, q - 1)) + jnp.where(lower, term(2, q + 1), term(2, q))
            at = slice(q * TILE, (q + 1) * TILE)
            out[0, b, :, at] = ((term(1, q) + swap_halves(sides)) * present[b : b + 1, at]).astype(jnp.bfloat16)


def forward_kernel(
    near, head, above, table, inner, tails, present, out, heads, ends, parts, middle, select_y, select_z
):
    set_selection(select_y, select_z)
    set_ends(near, 1, head, above, ends, parts)
    shift_all(parts, select_y, select_z, middle, heads, 1)
    lower = lane_of(heads.shape[1:]) < 64
    convolve(table, inner, lambda b: jnp.where(lower, heads[b], tails[b]), present, out, False)


def backward_kernel(table, inner, heads, tails, present, out):
    lower = lane_of(heads.shape[1:]) < 64
    convolve(table, inner, lambda b: jnp.where(lower, tails[b], heads[b]), present, out, True)


def unpack_kernel(groups, mine, theirs, out, whole):
    place = lax.axis_index("space") * lax.axis_size("scene") + lax.axis_index("scene")
    odd = place % 2
    where = place // 2 % groups
    size = mine.shape[0] // groups
    for k in range(groups):
        chunk = jnp.bitwise_xor(where, k)
        at = pl.multiple_of((odd * groups + chunk) * size, 8)
        whole[pl.ds(at, size), :] = mine[k * size : (k + 1) * size, :]
        at = pl.multiple_of(((1 - odd) * groups + chunk) * size, 8)
        whole[pl.ds(at, size), :] = theirs[k * size : (k + 1) * size, :]
    channels = out.shape[1]
    count, half = 9 * channels, 9 * channels // 2
    for yz in range(9):
        both = whole[yz * channels : (yz + 1) * channels, :]
        out[yz] = both[:, :channels]
        out[18 + yz] = both[:, channels:]
    for row in range(0, half, 32):
        both = whole[count + row : count + row + 32, :]
        for side in range(2):
            at = row + side * half
            out[9 + at // channels, at % channels : at % channels + 32, :] = both[
                :, side * channels : (side + 1) * channels
            ]


def exchange(x, bit):
    count = lax.axis_size("space") * lax.axis_size("scene")
    return lax.ppermute(x, AXES, [(i, i ^ bit) for i in range(count)])


def all_sum(part, groups):
    count = lax.axis_size("space") * lax.axis_size("scene")
    place = lax.axis_index("space") * lax.axis_size("scene") + lax.axis_index("scene")
    odd, where = place % 2, place // 2 % groups
    half = part.shape[0] // 2
    size = half // groups
    keep = lax.dynamic_slice_in_dim(part, odd * half, half, 0)
    send = lax.dynamic_slice_in_dim(part, (1 - odd) * half, half, 0)
    mine = keep + exchange(send, 1)
    own = lax.dynamic_slice_in_dim(mine, where * size, size, 0)
    got = []
    for k in range(1, groups):
        got.append(exchange(lax.dynamic_slice_in_dim(mine, (where ^ k) * size, size, 0), 2 * k))
    for one in got:
        own = own + one
    bit = 2 * groups
    while bit < count:
        wide = 4 if 4 * bit <= count else 2
        got = []
        for k in range(1, wide):
            got.append(exchange(own, bit * k))
        own = own + got[0]
        if wide == 4:
            own = own + (got[1] + got[2])
        bit *= wide
    chunks = [own]
    for k in range(1, groups):
        chunks.append(exchange(own, 2 * k))
    mine = jnp.concatenate(chunks)
    return mine, exchange(mine, 1)


def program(features, cotangent, weight, neighbours, occupancy):
    bricks, channels = features.shape[1], features.shape[2]
    spaces, scenes = lax.axis_size("space"), lax.axis_size("scene")
    scale = 1.0 / math.sqrt(scenes * bricks * spaces * 512)
    groups = 4
    unit = 16 * groups
    rows = -(-(27 * channels // 2) // unit) * unit

    def call(kernel, shapes, inputs, specs, scratch, limit=32 << 20):
        single = not isinstance(shapes, list)
        return pl.pallas_call(
            kernel,
            out_shape=shapes,
            in_specs=specs,
            out_specs=VMEM if single else [VMEM] * len(shapes),
            scratch_shapes=scratch,
            compiler_params=pltpu.CompilerParams(vmem_limit_bytes=limit),
            cost_estimate=pl.CostEstimate(flops=10**8, bytes_accessed=10**6, transcendentals=0),
        )(*inputs)

    def shape(*dims, dtype=jnp.bfloat16):
        return jax.ShapeDtypeStruct(dims, dtype)

    def scratch(*dims, dtype=jnp.bfloat16):
        return pltpu.VMEM(dims, dtype)

    many = bricks * TILES * channels
    parts = [scratch(2 * many, 2 * TILE), scratch(3 * many, 2 * TILE)]
    few = bricks * channels
    ends = [scratch(2 * bricks + 1, channels, TILE), scratch(2 * few, 2 * TILE), scratch(3 * few, 2 * TILE)]
    select = [scratch(2 * TILE, 3 * TILE)] * 2
    face, brick = shape(bricks, channels, TILE), shape(bricks + 1, channels, 512)
    head, tail, own_x, own_g, present, near = call(
        faces_kernel,
        [face, face, brick, brick, shape(bricks, 512, dtype=jnp.float32), shape(*neighbours.shape, dtype=jnp.int32)],
        tuple(
            pltpu.with_memory_space_constraint(a, pltpu.HBM) for a in (features, cotangent, occupancy, neighbours)
        ),
        [HBM] * 4,
        [
            scratch(*occupancy.shape, dtype=jnp.int32),
            scratch(*features.shape),
            scratch(*features.shape),
            pltpu.SemaphoreType.DMA((4,)),
        ],
        limit=16 << 20,
    )
    below = lax.ppermute(tail, "space", [(i, i + 1) for i in range(spaces - 1)])
    above = lax.ppermute(head, "space", [(i + 1, i) for i in range(spaces - 1)])
    volume, grads = shape(bricks, 9 * channels, 512), shape(rows, 2 * channels, dtype=jnp.float32)
    shifted = shape(bricks, 9 * channels, TILE)
    inner_x, grad = call(
        functools.partial(inner_kernel, scale),
        [volume, grads],
        (near, own_x, own_g),
        [SMEM, VMEM, VMEM],
        [*parts, *select, scratch(bricks, 3 * channels, 512)],
    )
    tails, grad = call(
        functools.partial(outer_kernel, scale),
        [shifted, grads],
        (near, head, tail, below, grad),
        [SMEM] + [VMEM] * 4,
        [*ends, *select],
    )
    table = shape(3 * channels, 9 * channels)
    table_y, table_g = call(tables_kernel, [table, table], (weight,), [VMEM], [])
    inner_g = call(shift_kernel, volume, (near, own_g), [SMEM, VMEM], [*parts, *select])
    out_y, heads = call(
        forward_kernel,
        [shape(*features.shape), shifted],
        (near, head, above, table_y, inner_x, tails, present),
        [SMEM] + [VMEM] * 6,
        [*ends, *select],
    )
    out_g = call(backward_kernel, shape(*cotangent.shape), (table_g, inner_g, heads, tails, present), [VMEM] * 5, [])
    mine, theirs = all_sum(grad, groups)
    out_w = call(
        functools.partial(unpack_kernel, groups),
        shape(27, channels, channels, dtype=jnp.float32),
        (mine, theirs),
        [VMEM] * 2,
        [pltpu.VMEM((rows, 2 * channels), jnp.float32)],
    )
    return out_y, out_g, out_w


def solution(mesh):
    in_specs = (
        P("scene", "space", None, None),
        P("scene", "space", None, None),
        P(),
        P("scene", "space", None),
        P("scene", "space", None),
    )
    out_specs = (P("scene", "space", None, None), P("scene", "space", None, None), P())
    return jax.shard_map(program, mesh=mesh, in_specs=in_specs, out_specs=out_specs, check_vma=False)
```

```python
import functools
import math

import jax
import jax.numpy as jnp
from jax import lax
from jax.experimental import pallas as pl
from jax.experimental.pallas import tpu as pltpu
from jax.sharding import PartitionSpec as P


TILE = 128
TILES = 4
AXES = ("space", "scene")
SMEM = pl.BlockSpec(memory_space=pltpu.SMEM)
VMEM = pl.BlockSpec(memory_space=pltpu.VMEM)
HBM = pl.BlockSpec(memory_space=pltpu.HBM)
SIDES = [(c, e) for c in (-1, 0, 1) for e in (-1, 0, 1)]


def set_selection(select_y, select_z):
    row = lax.broadcasted_iota(jnp.int32, (TILE, TILE), 0)
    lane = lax.broadcasted_iota(jnp.int32, (TILE, TILE), 1)
    for select, step in ((select_y, 8), (select_z, 1)):
        now = lane // step % 8
        for t in range(3):
            moved = now + t - 1
            wanted = lane + step * (jnp.bitwise_and(moved, 7) - now)
            beyond = jnp.where(moved == jnp.bitwise_and(moved, 7), 0, 1)
            for source in range(2):
                hit = jnp.where(beyond == source, wanted, -1) == row
                select[source * TILE : (source + 1) * TILE, t * TILE : (t + 1) * TILE] = jnp.where(
                    hit, 1.0, 0.0
                ).astype(jnp.bfloat16)


def lane_of(shape):
    return lax.broadcasted_iota(jnp.int32, shape, len(shape) - 1)


def swap_halves(x):
    return pltpu.roll(x, 64, x.ndim - 1)


def set_groups(parts, row, pick):
    channels, rows = pick(0, 0).shape[0], parts.shape[0] // 2
    lane = lane_of((channels, TILE))
    j_high, k_high = lane % 64 >= 32, lane % 8 >= 4
    parts[row : row + channels, :TILE] = pick(0, 0)
    parts[row : row + channels, TILE:] = jnp.where(j_high, pick(-1, 0), pick(1, 0))
    row = rows + row
    parts[row : row + channels, :TILE] = jnp.where(k_high, pick(0, -1), pick(0, 1))
    parts[row : row + channels, TILE:] = jnp.where(
        j_high,
        jnp.where(k_high, pick(-1, -1), pick(-1, 1)),
        jnp.where(k_high, pick(1, -1), pick(1, 1)),
    )


def index_of(near, b, a, c, e, start, none):
    number = near[0, b, 9 * (a + 1) + 3 * (c + 1) + e + 1]
    return jnp.where(number < 0, none, number - start)


def shift_all(parts, select_y, select_z, middle, shifted, tiles):
    bricks, channels, rows = shifted.shape[0], shifted.shape[1] // 9, parts.shape[0] // 2
    for side in range(2):
        moved = jnp.dot(
            parts[side * rows : (side + 1) * rows, :], select_y[...], preferred_element_type=jnp.float32
        ).astype(jnp.bfloat16)
        for t in range(3):
            middle[t * rows : (t + 1) * rows, side * TILE : (side + 1) * TILE] = moved[:, t * TILE : (t + 1) * TILE]
    for ty in range(3):
        moved = jnp.dot(
            middle[ty * rows : (ty + 1) * rows, :], select_z[...], preferred_element_type=jnp.float32
        ).astype(jnp.bfloat16)
        for b in range(bricks):
            for q in range(tiles):
                row = (b * tiles + q) * channels
                for tz in range(3):
                    tap = 3 * ty + tz
                    shifted[b, tap * channels : (tap + 1) * channels, q * TILE : (q + 1) * TILE] = moved[
                        row : row + channels, tz * TILE : (tz + 1) * TILE
                    ]


def inner_parts(near, own, parts):
    bricks, channels = own.shape[0] - 1, own.shape[1]
    base = lax.axis_index("space") * bricks
    for b in range(bricks):
        here = {s: index_of(near, b, 0, *s, base, bricks) for s in SIDES}
        for q in range(TILES):
            set_groups(
                parts, (b * TILES + q) * channels, lambda c, e: own[here[c, e], :, q * TILE : (q + 1) * TILE]
            )


def on_odd():
    return lax.axis_index("scene") % 2


def set_ends(near, up, mine, other, table, parts):
    bricks, channels = mine.shape[0], mine.shape[1]
    for b in range(bricks):
        table[b] = other[b]
        table[bricks + b] = mine[b]
    table[2 * bricks] = jnp.zeros((channels, TILE), jnp.bfloat16)
    start = (lax.axis_index("space") - 1 + up) * bricks

    def place(b, c, e):
        number = near[0, b, 18 * up + 3 * (c + 1) + e + 1]
        at = number - start
        turned = jnp.where(at < bricks, at + bricks, at - bricks)
        return jnp.where(number < 0, 2 * bricks, jnp.where(up == 1, turned, at))

    for b in range(bricks):
        at = {s: place(b, *s) for s in SIDES}
        set_groups(parts, b * channels, lambda c, e: table[at[c, e]])


def faces_kernel(features, cotangent, mask, near, one, two, own_x, own_g, present, near_out, *rest):
    buffers, sems = rest[:3], rest[3]
    copies = [pltpu.make_async_copy(a, b, sems.at[n]) for n, (a, b) in enumerate(zip((mask, features, cotangent), buffers))]
    copies.append(pltpu.make_async_copy(near, near_out, sems.at[3]))
    for copy in copies:
        copy.start()
    bricks, channels = own_x.shape[0] - 1, own_x.shape[1]
    lower = lane_of((channels, TILE)) < 64
    odd = on_odd() == 1
    copies[0].wait()
    present[...] = buffers[0][0].astype(jnp.float32)
    for side, own in enumerate((own_x, own_g)):
        copies[1 + side].wait()
        for b in range(bricks):
            own[b] = buffers[1 + side][0, b] * jnp.broadcast_to(present[b : b + 1, :], (channels, 512)).astype(
                jnp.bfloat16
            )
        own[bricks] = jnp.zeros((channels, 512), jnp.bfloat16)
    for b in range(bricks):
        x, g = own_x[b].astype(jnp.float32), own_g[b].astype(jnp.float32)
        head = jnp.where(lower, x[:, :TILE], swap_halves(g[:, :TILE])).astype(jnp.bfloat16)
        tail = jnp.where(lower, swap_halves(g[:, 3 * TILE :]), x[:, 3 * TILE :]).astype(jnp.bfloat16)
        one[b] = jnp.where(odd, head, tail)
        two[b] = jnp.where(odd, tail, head)
    copies[3].wait()


def inner_kernel(scale, near, own, gradient, shifted, grad, parts, middle, select_y, select_z, placed):
    rows, bricks, channels = grad.shape[0], own.shape[0] - 1, own.shape[1]
    set_selection(select_y, select_z)
    inner_parts(near, own, parts)
    lower = lane_of((channels, TILE)) < 64
    zero = jnp.zeros((channels, TILE), jnp.float32)
    for b in range(bricks):
        masked = gradient[b].astype(jnp.float32)
        tile = [zero] + [masked[:, q * TILE : (q + 1) * TILE] for q in range(TILES)] + [zero]
        for q in range(TILES):
            at = slice(q * TILE, (q + 1) * TILE)
            placed[b, :channels, at] = swap_halves(jnp.where(lower, tile[q + 2], tile[q + 1])).astype(jnp.bfloat16)
            placed[b, channels : 2 * channels, at] = swap_halves(jnp.where(lower, tile[q + 1], tile[q])).astype(
                jnp.bfloat16
            )
            placed[b, 2 * channels :, at] = tile[q + 1].astype(jnp.bfloat16)
    shift_all(parts, select_y, select_z, middle, shifted, TILES)
    total = None
    for b in range(bricks):
        term = lax.dot_general(
            shifted[b], placed[b], (((1,), (1,)), ((), ())), preferred_element_type=jnp.float32
        )
        total = term if total is None else total + term
    total = total * scale
    count, half = 9 * channels, 9 * channels // 2
    grad[:count, :] = total[:, : 2 * channels]
    grad[count : count + half, :channels] = total[:half, 2 * channels :]
    grad[count : count + half, channels:] = total[half:, 2 * channels :]
    if rows > count + half:
        grad[count + half :, :] = jnp.zeros((rows - count - half, 2 * channels), jnp.float32)


def outer_kernel(
    scale, near, mine, facing, other, inner, shifted, grad, table, parts, middle, select_y, select_z
):
    bricks, channels = mine.shape[0], mine.shape[1]
    odd = on_odd()
    set_selection(select_y, select_z)
    set_ends(near, odd, mine, other, table, parts)
    shift_all(parts, select_y, select_z, middle, shifted, 1)
    x_half = lane_of((channels, TILE)) // 64 == odd
    contract = (((1,), (1,)), ((), ()))
    first = last = None
    for b in range(bricks):
        g, x = jnp.where(x_half, 0, facing[b]), jnp.where(x_half, facing[b], 0)
        one = lax.dot_general(shifted[b], g, contract, preferred_element_type=jnp.float32)
        two = lax.dot_general(x, shifted[b], contract, preferred_element_type=jnp.float32)
        first, last = (one, two) if b == 0 else (first + one, last + two)
    for yz in range(9):
        at = slice(yz * channels, (yz + 1) * channels)
        one, two = first[at], last[:, (8 - yz) * channels : (9 - yz) * channels]
        term = jnp.concatenate([jnp.where(odd == 1, two, one), jnp.where(odd == 1, one, two)], axis=1)
        grad[at, :] = inner[at, :] + term * scale
    grad[9 * channels :, :] = inner[9 * channels :, :]


def shift_kernel(near, own, shifted, parts, middle, select_y, select_z):
    set_selection(select_y, select_z)
    inner_parts(near, own, parts)
    shift_all(parts, select_y, select_z, middle, shifted, TILES)


def tables_kernel(weight, table_y, table_g):
    channels = weight.shape[1]
    for tx in range(3):
        for yz in range(9):
            at = (slice(tx * channels, (tx + 1) * channels), slice(yz * channels, (yz + 1) * channels))
            table_y[at] = weight[9 * tx + yz].astype(jnp.float32).T.astype(jnp.bfloat16)
            table_g[at] = weight[26 - 9 * tx - yz]


def convolve(table, inner, ends, present, out, swapped):
    bricks, channels = out.shape[1], out.shape[2]
    lower = lane_of((channels, TILE)) < 64
    for b in range(bricks):
        main = jnp.dot(table[...], inner[b], preferred_element_type=jnp.float32)
        side = jnp.dot(table[...], ends(b), preferred_element_type=jnp.float32)
        if swapped:
            side = swap_halves(side)

        def term(t, q):
            rows = slice(t * channels, (t + 1) * channels)
            return main[rows, q * TILE : (q + 1) * TILE] if 0 <= q < TILES else side[rows]

        for q in range(TILES):
            sides = jnp.where(lower, term(0, q), term(0, q - 1)) + jnp.where(lower, term(2, q + 1), term(2, q))
            at = slice(q * TILE, (q + 1) * TILE)
            out[0, b, :, at] = ((term(1, q) + swap_halves(sides)) * present[b : b + 1, at]).astype(jnp.bfloat16)


def forward_kernel(
    near, mine, other, table, inner, ends, present, out, more_ends, tiles, parts, middle, select_y, select_z
):
    odd = on_odd()
    set_selection(select_y, select_z)
    set_ends(near, 1 - odd, mine, other, tiles, parts)
    shift_all(parts, select_y, select_z, middle, more_ends, 1)
    half = lane_of(ends.shape[1:]) // 64 == odd
    convolve(table, inner, lambda b: jnp.where(half, more_ends[b], ends[b]), present, out, False)


def backward_kernel(table, inner, ends, more_ends, present, out):
    half = lane_of(ends.shape[1:]) // 64 == on_odd()
    convolve(table, inner, lambda b: jnp.where(half, ends[b], more_ends[b]), present, out, True)


def unpack_kernel(groups, mine, theirs, out, whole):
    place = lax.axis_index("space") * lax.axis_size("scene") + lax.axis_index("scene")
    odd = place % 2
    where = place // 2 % groups
    size = mine.shape[0] // groups
    for k in range(groups):
        chunk = jnp.bitwise_xor(where, k)
        at = pl.multiple_of((odd * groups + chunk) * size, 8)
        whole[pl.ds(at, size), :] = mine[k * size : (k + 1) * size, :]
        at = pl.multiple_of(((1 - odd) * groups + chunk) * size, 8)
        whole[pl.ds(at, size), :] = theirs[k * size : (k + 1) * size, :]
    channels = out.shape[1]
    count, half = 9 * channels, 9 * channels // 2
    for yz in range(9):
        both = whole[yz * channels : (yz + 1) * channels, :]
        out[yz] = both[:, :channels]
        out[18 + yz] = both[:, channels:]
    for row in range(0, half, 32):
        both = whole[count + row : count + row + 32, :]
        for side in range(2):
            at = row + side * half
            out[9 + at // channels, at % channels : at % channels + 32, :] = both[
                :, side * channels : (side + 1) * channels
            ]


def halo_pairs(spaces, scenes):
    pairs = []
    for scene in range(scenes):
        line = [space * scenes + scene for space in range(spaces)]
        line = line[::-1] if scene % 2 else line
        pairs += list(zip(line, line[1:]))
        if scene ^ 1 < scenes:
            pairs.append((line[-1], line[-1] + (scene ^ 1) - scene))
    return pairs


def exchange(x, bit):
    count = lax.axis_size("space") * lax.axis_size("scene")
    return lax.ppermute(x, AXES, [(i, i ^ bit) for i in range(count)])


def all_sum(part, groups):
    count = lax.axis_size("space") * lax.axis_size("scene")
    place = lax.axis_index("space") * lax.axis_size("scene") + lax.axis_index("scene")
    odd, where = place % 2, place // 2 % groups
    half = part.shape[0] // 2
    size = half // groups
    keep = lax.dynamic_slice_in_dim(part, odd * half, half, 0)
    send = lax.dynamic_slice_in_dim(part, (1 - odd) * half, half, 0)
    mine = keep + exchange(send, 1)
    own = lax.dynamic_slice_in_dim(mine, where * size, size, 0)
    got = []
    for k in range(1, groups):
        got.append(exchange(lax.dynamic_slice_in_dim(mine, (where ^ k) * size, size, 0), 2 * k))
    for one in got:
        own = own + one
    bit = 2 * groups
    while bit < count:
        wide = 4 if 4 * bit <= count else 2
        got = []
        for k in range(1, wide):
            got.append(exchange(own, bit * k))
        own = own + got[0]
        if wide == 4:
            own = own + (got[1] + got[2])
        bit *= wide
    chunks = [own]
    for k in range(1, groups):
        chunks.append(exchange(own, 2 * k))
    mine = jnp.concatenate(chunks)
    return mine, exchange(mine, 1)


def program(features, cotangent, weight, neighbours, occupancy):
    bricks, channels = features.shape[1], features.shape[2]
    spaces, scenes = lax.axis_size("space"), lax.axis_size("scene")
    scale = 1.0 / math.sqrt(scenes * bricks * spaces * 512)
    groups = 4
    unit = 16 * groups
    rows = -(-(27 * channels // 2) // unit) * unit

    def call(kernel, shapes, inputs, specs, scratch, limit=32 << 20):
        single = not isinstance(shapes, list)
        return pl.pallas_call(
            kernel,
            out_shape=shapes,
            in_specs=specs,
            out_specs=VMEM if single else [VMEM] * len(shapes),
            scratch_shapes=scratch,
            compiler_params=pltpu.CompilerParams(vmem_limit_bytes=limit),
            cost_estimate=pl.CostEstimate(flops=10**8, bytes_accessed=10**6, transcendentals=0),
        )(*inputs)

    def shape(*dims, dtype=jnp.bfloat16):
        return jax.ShapeDtypeStruct(dims, dtype)

    def scratch(*dims, dtype=jnp.bfloat16):
        return pltpu.VMEM(dims, dtype)

    many = bricks * TILES * channels
    parts = [scratch(2 * many, 2 * TILE), scratch(3 * many, 2 * TILE)]
    few = bricks * channels
    ends = [scratch(2 * bricks + 1, channels, TILE), scratch(2 * few, 2 * TILE), scratch(3 * few, 2 * TILE)]
    select = [scratch(2 * TILE, 3 * TILE)] * 2
    face, brick = shape(bricks, channels, TILE), shape(bricks + 1, channels, 512)
    one, two, own_x, own_g, present, near = call(
        faces_kernel,
        [face, face, brick, brick, shape(bricks, 512, dtype=jnp.float32), shape(*neighbours.shape, dtype=jnp.int32)],
        tuple(
            pltpu.with_memory_space_constraint(a, pltpu.HBM) for a in (features, cotangent, occupancy, neighbours)
        ),
        [HBM] * 4,
        [
            scratch(*occupancy.shape, dtype=jnp.int32),
            scratch(*features.shape),
            scratch(*features.shape),
            pltpu.SemaphoreType.DMA((4,)),
        ],
        limit=16 << 20,
    )
    forth = halo_pairs(spaces, scenes)
    got_one = lax.ppermute(one, AXES, forth)
    got_two = lax.ppermute(two, AXES, [(b, a) for a, b in forth])
    volume, grads = shape(bricks, 9 * channels, 512), shape(rows, 2 * channels, dtype=jnp.float32)
    shifted = shape(bricks, 9 * channels, TILE)
    inner_x, grad = call(
        functools.partial(inner_kernel, scale),
        [volume, grads],
        (near, own_x, own_g),
        [SMEM, VMEM, VMEM],
        [*parts, *select, scratch(bricks, 3 * channels, 512)],
    )
    ends_one, grad = call(
        functools.partial(outer_kernel, scale),
        [shifted, grads],
        (near, one, two, got_one, grad),
        [SMEM] + [VMEM] * 4,
        [*ends, *select],
    )
    table = shape(3 * channels, 9 * channels)
    table_y, table_g = call(tables_kernel, [table, table], (weight,), [VMEM], [])
    inner_g = call(shift_kernel, volume, (near, own_g), [SMEM, VMEM], [*parts, *select])
    out_y, ends_two = call(
        forward_kernel,
        [shape(*features.shape), shifted],
        (near, two, got_two, table_y, inner_x, ends_one, present),
        [SMEM] + [VMEM] * 6,
        [*ends, *select],
    )
    out_g = call(
        backward_kernel, shape(*cotangent.shape), (table_g, inner_g, ends_one, ends_two, present), [VMEM] * 5, []
    )
    mine, theirs = all_sum(grad, groups)
    out_w = call(
        functools.partial(unpack_kernel, groups),
        shape(27, channels, channels, dtype=jnp.float32),
        (mine, theirs),
        [VMEM] * 2,
        [pltpu.VMEM((rows, 2 * channels), jnp.float32)],
    )
    return out_y, out_g, out_w


def solution(mesh):
    in_specs = (
        P("scene", "space", None, None),
        P("scene", "space", None, None),
        P(),
        P("scene", "space", None),
        P("scene", "space", None),
    )
    out_specs = (P("scene", "space", None, None), P("scene", "space", None, None), P())
    return jax.shard_map(program, mesh=mesh, in_specs=in_specs, out_specs=out_specs, check_vma=False)
```

```python
import functools
import math

import jax
import jax.numpy as jnp
from jax import lax
from jax.experimental import pallas as pl
from jax.experimental.pallas import tpu as pltpu
from jax.sharding import PartitionSpec as P


TILE = 128
TILES = 4
AXES = ("space", "scene")
SMEM = pl.BlockSpec(memory_space=pltpu.SMEM)
VMEM = pl.BlockSpec(memory_space=pltpu.VMEM)
HBM = pl.BlockSpec(memory_space=pltpu.HBM)
SIDES = [(c, e) for c in (-1, 0, 1) for e in (-1, 0, 1)]


def set_selection(select_y, select_z):
    row = lax.broadcasted_iota(jnp.int32, (TILE, TILE), 0)
    lane = lax.broadcasted_iota(jnp.int32, (TILE, TILE), 1)
    for select, step in ((select_y, 8), (select_z, 1)):
        now = lane // step % 8
        for t in range(3):
            moved = now + t - 1
            wanted = lane + step * (jnp.bitwise_and(moved, 7) - now)
            beyond = jnp.where(moved == jnp.bitwise_and(moved, 7), 0, 1)
            for source in range(2):
                hit = jnp.where(beyond == source, wanted, -1) == row
                select[source * TILE : (source + 1) * TILE, t * TILE : (t + 1) * TILE] = jnp.where(
                    hit, 1.0, 0.0
                ).astype(jnp.bfloat16)


def lane_of(shape):
    return lax.broadcasted_iota(jnp.int32, shape, len(shape) - 1)


def swap_halves(x):
    return pltpu.roll(x, 64, x.ndim - 1)


def set_groups(parts, row, pick):
    channels, rows = pick(0, 0).shape[0], parts.shape[0] // 2
    lane = lane_of((channels, TILE))
    j_high, k_high = lane % 64 >= 32, lane % 8 >= 4
    parts[row : row + channels, :TILE] = pick(0, 0)
    parts[row : row + channels, TILE:] = jnp.where(j_high, pick(-1, 0), pick(1, 0))
    row = rows + row
    parts[row : row + channels, :TILE] = jnp.where(k_high, pick(0, -1), pick(0, 1))
    parts[row : row + channels, TILE:] = jnp.where(
        j_high,
        jnp.where(k_high, pick(-1, -1), pick(-1, 1)),
        jnp.where(k_high, pick(1, -1), pick(1, 1)),
    )


def index_of(near, b, a, c, e, start, none):
    number = near[0, b, 9 * (a + 1) + 3 * (c + 1) + e + 1]
    return jnp.where(number < 0, none, number - start)


def shift_all(parts, select_y, select_z, middle, shifted, tiles):
    bricks, channels, rows = shifted.shape[0], shifted.shape[1] // 9, parts.shape[0] // 2
    for side in range(2):
        moved = jnp.dot(
            parts[side * rows : (side + 1) * rows, :], select_y[...], preferred_element_type=jnp.float32
        ).astype(jnp.bfloat16)
        for t in range(3):
            middle[t * rows : (t + 1) * rows, side * TILE : (side + 1) * TILE] = moved[:, t * TILE : (t + 1) * TILE]
    for ty in range(3):
        moved = jnp.dot(
            middle[ty * rows : (ty + 1) * rows, :], select_z[...], preferred_element_type=jnp.float32
        ).astype(jnp.bfloat16)
        for b in range(bricks):
            for q in range(tiles):
                row = (b * tiles + q) * channels
                for tz in range(3):
                    tap = 3 * ty + tz
                    shifted[b, tap * channels : (tap + 1) * channels, q * TILE : (q + 1) * TILE] = moved[
                        row : row + channels, tz * TILE : (tz + 1) * TILE
                    ]


def inner_parts(near, own, parts):
    bricks, channels = own.shape[0] - 1, own.shape[1]
    base = lax.axis_index("space") * bricks
    for b in range(bricks):
        here = {s: index_of(near, b, 0, *s, base, bricks) for s in SIDES}
        for q in range(TILES):
            set_groups(
                parts, (b * TILES + q) * channels, lambda c, e: own[here[c, e], :, q * TILE : (q + 1) * TILE]
            )


def on_odd():
    return lax.axis_index("scene") % 2


def set_ends(near, up, mine, other, table, parts):
    bricks, channels = mine.shape[0], mine.shape[1]
    for b in range(bricks):
        table[b] = other[b]
        table[bricks + b] = mine[b]
    table[2 * bricks] = jnp.zeros((channels, TILE), jnp.bfloat16)
    start = (lax.axis_index("space") - 1 + up) * bricks

    def place(b, c, e):
        number = near[0, b, 18 * up + 3 * (c + 1) + e + 1]
        at = number - start
        turned = jnp.where(at < bricks, at + bricks, at - bricks)
        return jnp.where(number < 0, 2 * bricks, jnp.where(up == 1, turned, at))

    for b in range(bricks):
        at = {s: place(b, *s) for s in SIDES}
        set_groups(parts, b * channels, lambda c, e: table[at[c, e]])


def faces_kernel(features, cotangent, mask, near, one, two, own_x, own_g, present, near_out, *rest):
    buffers, sems = rest[:3], rest[3]
    copies = [pltpu.make_async_copy(a, b, sems.at[n]) for n, (a, b) in enumerate(zip((mask, features, cotangent), buffers))]
    copies.append(pltpu.make_async_copy(near, near_out, sems.at[3]))
    for copy in copies:
        copy.start()
    bricks, channels = own_x.shape[0] - 1, own_x.shape[1]
    lower = lane_of((channels, TILE)) < 64
    odd = on_odd() == 1
    copies[0].wait()
    present[...] = buffers[0][0].astype(jnp.float32)
    for side, own in enumerate((own_x, own_g)):
        copies[1 + side].wait()
        for b in range(bricks):
            own[b] = buffers[1 + side][0, b] * jnp.broadcast_to(present[b : b + 1, :], (channels, 512)).astype(
                jnp.bfloat16
            )
        own[bricks] = jnp.zeros((channels, 512), jnp.bfloat16)
    for b in range(bricks):
        x, g = own_x[b].astype(jnp.float32), own_g[b].astype(jnp.float32)
        head = jnp.where(lower, x[:, :TILE], swap_halves(g[:, :TILE])).astype(jnp.bfloat16)
        tail = jnp.where(lower, swap_halves(g[:, 3 * TILE :]), x[:, 3 * TILE :]).astype(jnp.bfloat16)
        one[b] = jnp.where(odd, head, tail)
        two[b] = jnp.where(odd, tail, head)
    copies[3].wait()


def inner_kernel(scale, near, own, gradient, shifted, grad, select_y, select_z, parts, middle, placed):
    rows, bricks, channels = grad.shape[0], own.shape[0] - 1, own.shape[1]
    set_selection(select_y, select_z)
    inner_parts(near, own, parts)
    lower = lane_of((channels, TILE)) < 64
    zero = jnp.zeros((channels, TILE), jnp.float32)
    for b in range(bricks):
        masked = gradient[b].astype(jnp.float32)
        tile = [zero] + [masked[:, q * TILE : (q + 1) * TILE] for q in range(TILES)] + [zero]
        for q in range(TILES):
            at = slice(q * TILE, (q + 1) * TILE)
            placed[b, :channels, at] = swap_halves(jnp.where(lower, tile[q + 2], tile[q + 1])).astype(jnp.bfloat16)
            placed[b, channels : 2 * channels, at] = swap_halves(jnp.where(lower, tile[q + 1], tile[q])).astype(
                jnp.bfloat16
            )
            placed[b, 2 * channels :, at] = tile[q + 1].astype(jnp.bfloat16)
    shift_all(parts, select_y, select_z, middle, shifted, TILES)
    total = None
    for b in range(bricks):
        term = lax.dot_general(
            shifted[b], placed[b], (((1,), (1,)), ((), ())), preferred_element_type=jnp.float32
        )
        total = term if total is None else total + term
    total = total * scale
    count, half = 9 * channels, 9 * channels // 2
    grad[:count, :] = total[:, : 2 * channels]
    grad[count : count + half, :channels] = total[:half, 2 * channels :]
    grad[count : count + half, channels:] = total[half:, 2 * channels :]
    if rows > count + half:
        grad[count + half :, :] = jnp.zeros((rows - count - half, 2 * channels), jnp.float32)


def outer_kernel(
    scale, near, mine, facing, other, inner, select_y, select_z, shifted, grad, table, parts, middle
):
    bricks, channels = mine.shape[0], mine.shape[1]
    odd = on_odd()
    set_ends(near, odd, mine, other, table, parts)
    shift_all(parts, select_y, select_z, middle, shifted, 1)
    x_half = lane_of((channels, TILE)) // 64 == odd
    contract = (((1,), (1,)), ((), ()))
    first = last = None
    for b in range(bricks):
        g, x = jnp.where(x_half, 0, facing[b]), jnp.where(x_half, facing[b], 0)
        one = lax.dot_general(shifted[b], g, contract, preferred_element_type=jnp.float32)
        two = lax.dot_general(x, shifted[b], contract, preferred_element_type=jnp.float32)
        first, last = (one, two) if b == 0 else (first + one, last + two)
    for yz in range(9):
        at = slice(yz * channels, (yz + 1) * channels)
        one, two = first[at], last[:, (8 - yz) * channels : (9 - yz) * channels]
        term = jnp.concatenate([jnp.where(odd == 1, two, one), jnp.where(odd == 1, one, two)], axis=1)
        grad[at, :] = inner[at, :] + term * scale
    grad[9 * channels :, :] = inner[9 * channels :, :]


def shift_kernel(near, own, select_y, select_z, shifted, parts, middle):
    inner_parts(near, own, parts)
    shift_all(parts, select_y, select_z, middle, shifted, TILES)


def tables_kernel(weight, table_y, table_g):
    channels = weight.shape[1]
    for tx in range(3):
        for yz in range(9):
            at = (slice(tx * channels, (tx + 1) * channels), slice(yz * channels, (yz + 1) * channels))
            table_y[at] = weight[9 * tx + yz].astype(jnp.float32).T.astype(jnp.bfloat16)
            table_g[at] = weight[26 - 9 * tx - yz]


def convolve(table, inner, ends, present, out, swapped):
    bricks, channels = out.shape[1], out.shape[2]
    lower = lane_of((channels, TILE)) < 64
    for b in range(bricks):
        main = jnp.dot(table[...], inner[b], preferred_element_type=jnp.float32)
        side = jnp.dot(table[...], ends(b), preferred_element_type=jnp.float32)
        if swapped:
            side = swap_halves(side)

        def term(t, q):
            rows = slice(t * channels, (t + 1) * channels)
            return main[rows, q * TILE : (q + 1) * TILE] if 0 <= q < TILES else side[rows]

        for q in range(TILES):
            sides = jnp.where(lower, term(0, q), term(0, q - 1)) + jnp.where(lower, term(2, q + 1), term(2, q))
            at = slice(q * TILE, (q + 1) * TILE)
            out[0, b, :, at] = ((term(1, q) + swap_halves(sides)) * present[b : b + 1, at]).astype(jnp.bfloat16)


def forward_kernel(
    near, mine, other, table, inner, ends, present, select_y, select_z, out, more_ends, tiles, parts, middle
):
    odd = on_odd()
    set_ends(near, 1 - odd, mine, other, tiles, parts)
    shift_all(parts, select_y, select_z, middle, more_ends, 1)
    half = lane_of(ends.shape[1:]) // 64 == odd
    convolve(table, inner, lambda b: jnp.where(half, more_ends[b], ends[b]), present, out, False)


def backward_kernel(table, inner, ends, more_ends, present, out):
    half = lane_of(ends.shape[1:]) // 64 == on_odd()
    convolve(table, inner, lambda b: jnp.where(half, ends[b], more_ends[b]), present, out, True)


def unpack_kernel(groups, own, *refs):
    part, out, whole, blocks, sem = refs[0], *refs[-4:]
    place = lax.axis_index("space") * lax.axis_size("scene") + lax.axis_index("scene")
    where = place // 2 % groups
    size, channels = part.shape[0] // groups, blocks.shape[1]
    for k in range(groups):
        at = pl.multiple_of(jnp.bitwise_xor(where, k) * size, 8)
        whole[pl.ds(at, size), :] = part[k * size : (k + 1) * size, :]
    half, count = part.shape[0], 9 * channels

    def write(low, high):
        runs = []

        def put(tap, lane, row, rows, first):
            if not runs or runs[-1][0] + runs[-1][2] not in (tap, tap + 1) or (first == 0) != (
                runs[-1][0] + runs[-1][2] == tap
            ):
                runs.append([tap, sum(run[2] for run in runs), 0])
            if first == 0:
                runs[-1][2] += 1
            at = runs[-1][1] + runs[-1][2] - 1
            blocks[at, first : first + rows, :] = whole[row : row + rows, lane * channels : (lane + 1) * channels]

        taps = range(low // channels, min(high, count) // channels)
        for lane, base in ((0, 0), (1, 18)):
            for yz in taps:
                put(base + yz, lane, yz * channels - low, channels, 0)
        if high > count:
            for lane in range(2):
                done = 0
                while done < count // 2:
                    at = lane * (count // 2) + done
                    rows = min(channels - at % channels, count // 2 - done)
                    put(9 + at // channels, lane, count - low + done, rows, at % channels)
                    done += rows
        copies = [
            pltpu.make_async_copy(blocks.at[start : start + n], out.at[tap : tap + n], sem.at[i])
            for i, (tap, start, n) in enumerate(runs)
        ]
        for copy in copies:
            copy.start()
        for copy in copies:
            copy.wait()

    lower = (place % 2 == 0) == own
    pl.when(lower)(lambda: write(0, half))
    pl.when(jnp.logical_not(lower))(lambda: write(half, 2 * half))


def halo_pairs(spaces, scenes):
    pairs = []
    for scene in range(scenes):
        line = [space * scenes + scene for space in range(spaces)]
        line = line[::-1] if scene % 2 else line
        pairs += list(zip(line, line[1:]))
        if scene ^ 1 < scenes:
            pairs.append((line[-1], line[-1] + (scene ^ 1) - scene))
    return pairs


def exchange(x, bit):
    count = lax.axis_size("space") * lax.axis_size("scene")
    return lax.ppermute(x, AXES, [(i, i ^ bit) for i in range(count)])


def all_sum(part, groups):
    count = lax.axis_size("space") * lax.axis_size("scene")
    place = lax.axis_index("space") * lax.axis_size("scene") + lax.axis_index("scene")
    odd, where = place % 2, place // 2 % groups
    half = part.shape[0] // 2
    size = half // groups
    keep = lax.dynamic_slice_in_dim(part, odd * half, half, 0)
    send = lax.dynamic_slice_in_dim(part, (1 - odd) * half, half, 0)
    mine = keep + exchange(send, 1)
    own = lax.dynamic_slice_in_dim(mine, where * size, size, 0)
    got = []
    for k in range(1, groups):
        got.append(exchange(lax.dynamic_slice_in_dim(mine, (where ^ k) * size, size, 0), 2 * k))
    for one in got:
        own = own + one
    bit = 2 * groups
    while bit < count:
        wide = 4 if 4 * bit <= count else 2
        got = []
        for k in range(1, wide):
            got.append(exchange(own, bit * k))
        own = own + got[0]
        if wide == 4:
            own = own + (got[1] + got[2])
        bit *= wide
    chunks = [own]
    for k in range(1, groups):
        chunks.append(exchange(own, 2 * k))
    mine = jnp.concatenate(chunks)
    return mine, exchange(mine, 1)


def program(features, cotangent, weight, neighbours, occupancy):
    bricks, channels = features.shape[1], features.shape[2]
    spaces, scenes = lax.axis_size("space"), lax.axis_size("scene")
    scale = 1.0 / math.sqrt(scenes * bricks * spaces * 512)
    groups = 4
    unit = 16 * groups
    rows = -(-(27 * channels // 2) // unit) * unit

    def call(kernel, shapes, inputs, specs, scratch, limit=32 << 20):
        single = not isinstance(shapes, list)
        return pl.pallas_call(
            kernel,
            out_shape=shapes,
            in_specs=specs,
            out_specs=VMEM if single else [VMEM] * len(shapes),
            scratch_shapes=scratch,
            compiler_params=pltpu.CompilerParams(vmem_limit_bytes=limit),
            cost_estimate=pl.CostEstimate(flops=10**8, bytes_accessed=10**6, transcendentals=0),
        )(*inputs)

    def shape(*dims, dtype=jnp.bfloat16):
        return jax.ShapeDtypeStruct(dims, dtype)

    def scratch(*dims, dtype=jnp.bfloat16):
        return pltpu.VMEM(dims, dtype)

    many = bricks * TILES * channels
    parts = [scratch(2 * many, 2 * TILE), scratch(3 * many, 2 * TILE)]
    few = bricks * channels
    ends = [scratch(2 * bricks + 1, channels, TILE), scratch(2 * few, 2 * TILE), scratch(3 * few, 2 * TILE)]
    chosen = shape(2 * TILE, 3 * TILE)
    face, brick = shape(bricks, channels, TILE), shape(bricks + 1, channels, 512)
    one, two, own_x, own_g, present, near = call(
        faces_kernel,
        [face, face, brick, brick, shape(bricks, 512, dtype=jnp.float32), shape(*neighbours.shape, dtype=jnp.int32)],
        tuple(
            pltpu.with_memory_space_constraint(a, pltpu.HBM) for a in (features, cotangent, occupancy, neighbours)
        ),
        [HBM] * 4,
        [
            scratch(*occupancy.shape, dtype=jnp.int32),
            scratch(*features.shape),
            scratch(*features.shape),
            pltpu.SemaphoreType.DMA((4,)),
        ],
        limit=16 << 20,
    )
    forth = halo_pairs(spaces, scenes)
    got_one = lax.ppermute(one, AXES, forth)
    got_two = lax.ppermute(two, AXES, [(b, a) for a, b in forth])
    volume, grads = shape(bricks, 9 * channels, 512), shape(rows, 2 * channels, dtype=jnp.float32)
    shifted = shape(bricks, 9 * channels, TILE)
    inner_x, grad, *select = call(
        functools.partial(inner_kernel, scale),
        [volume, grads, chosen, chosen],
        (near, own_x, own_g),
        [SMEM, VMEM, VMEM],
        [*parts, scratch(bricks, 3 * channels, 512)],
    )
    ends_one, grad = call(
        functools.partial(outer_kernel, scale),
        [shifted, grads],
        (near, one, two, got_one, grad, *select),
        [SMEM] + [VMEM] * 6,
        ends,
    )
    table = shape(3 * channels, 9 * channels)
    table_y, table_g = call(tables_kernel, [table, table], (weight,), [VMEM], [])
    inner_g = call(shift_kernel, volume, (near, own_g, *select), [SMEM] + [VMEM] * 3, parts)
    out_y, ends_two = call(
        forward_kernel,
        [shape(*features.shape), shifted],
        (near, two, got_two, table_y, inner_x, ends_one, present, *select),
        [SMEM] + [VMEM] * 8,
        ends,
    )
    out_g = call(
        backward_kernel, shape(*cotangent.shape), (table_g, inner_g, ends_one, ends_two, present), [VMEM] * 5, []
    )
    mine, theirs = all_sum(grad, groups)
    taps = shape(27, channels, channels, dtype=jnp.float32)

    def unpack(own, part, *before):
        return pl.pallas_call(
            functools.partial(unpack_kernel, groups, own),
            out_shape=taps,
            in_specs=[VMEM] + [HBM] * len(before),
            out_specs=HBM,
            scratch_shapes=[
                scratch(rows // 2, 2 * channels, dtype=jnp.float32),
                scratch(14, channels, channels, dtype=jnp.float32),
                pltpu.SemaphoreType.DMA((3,)),
            ],
            input_output_aliases={1: 0} if before else {},
            compiler_params=pltpu.CompilerParams(vmem_limit_bytes=16 << 20),
            cost_estimate=pl.CostEstimate(flops=10**6, bytes_accessed=10**6, transcendentals=0),
            name="unpack",
        )(part, *before)

    out_w = unpack(True, mine)
    out_w = unpack(False, theirs, out_w)
    return out_y, out_g, out_w


def solution(mesh):
    in_specs = (
        P("scene", "space", None, None),
        P("scene", "space", None, None),
        P(),
        P("scene", "space", None),
        P("scene", "space", None),
    )
    out_specs = (P("scene", "space", None, None), P("scene", "space", None, None), P())
    return jax.shard_map(program, mesh=mesh, in_specs=in_specs, out_specs=out_specs, check_vma=False)
```

```python
import functools
import math

import jax
import jax.numpy as jnp
from jax import lax
from jax.experimental import pallas as pl
from jax.experimental.pallas import tpu as pltpu
from jax.sharding import PartitionSpec as P


TILE = 128
TILES = 4
AXES = ("space", "scene")
SMEM = pl.BlockSpec(memory_space=pltpu.SMEM)
VMEM = pl.BlockSpec(memory_space=pltpu.VMEM)
HBM = pl.BlockSpec(memory_space=pltpu.HBM)
SIDES = [(c, e) for c in (-1, 0, 1) for e in (-1, 0, 1)]


def set_selection(select_y, select_z):
    row = lax.broadcasted_iota(jnp.int32, (TILE, TILE), 0)
    lane = lax.broadcasted_iota(jnp.int32, (TILE, TILE), 1)
    for select, step in ((select_y, 8), (select_z, 1)):
        now = lane // step % 8
        for t in range(3):
            moved = now + t - 1
            wanted = lane + step * (jnp.bitwise_and(moved, 7) - now)
            beyond = jnp.where(moved == jnp.bitwise_and(moved, 7), 0, 1)
            for source in range(2):
                hit = jnp.where(beyond == source, wanted, -1) == row
                select[source * TILE : (source + 1) * TILE, t * TILE : (t + 1) * TILE] = jnp.where(
                    hit, 1.0, 0.0
                ).astype(jnp.bfloat16)


def lane_of(shape):
    return lax.broadcasted_iota(jnp.int32, shape, len(shape) - 1)


def swap_halves(x):
    return pltpu.roll(x, 64, x.ndim - 1)


def set_groups(parts, row, pick):
    channels, rows = pick(0, 0).shape[0], parts.shape[0] // 2
    lane = lane_of((channels, TILE))
    j_high, k_high = lane % 64 >= 32, lane % 8 >= 4
    parts[row : row + channels, :TILE] = pick(0, 0)
    parts[row : row + channels, TILE:] = jnp.where(j_high, pick(-1, 0), pick(1, 0))
    row = rows + row
    parts[row : row + channels, :TILE] = jnp.where(k_high, pick(0, -1), pick(0, 1))
    parts[row : row + channels, TILE:] = jnp.where(
        j_high,
        jnp.where(k_high, pick(-1, -1), pick(-1, 1)),
        jnp.where(k_high, pick(1, -1), pick(1, 1)),
    )


def index_of(near, b, a, c, e, start, none):
    number = near[0, b, 9 * (a + 1) + 3 * (c + 1) + e + 1]
    return jnp.where(number < 0, none, number - start)


def shift_all(parts, select_y, select_z, middle, shifted, tiles):
    bricks, channels, rows = shifted.shape[0], shifted.shape[1] // 9, parts.shape[0] // 2
    for side in range(2):
        moved = jnp.dot(
            parts[side * rows : (side + 1) * rows, :], select_y[...], preferred_element_type=jnp.float32
        ).astype(jnp.bfloat16)
        for t in range(3):
            middle[t * rows : (t + 1) * rows, side * TILE : (side + 1) * TILE] = moved[:, t * TILE : (t + 1) * TILE]
    for ty in range(3):
        moved = jnp.dot(
            middle[ty * rows : (ty + 1) * rows, :], select_z[...], preferred_element_type=jnp.float32
        ).astype(jnp.bfloat16)
        for b in range(bricks):
            for q in range(tiles):
                row = (b * tiles + q) * channels
                for tz in range(3):
                    tap = 3 * ty + tz
                    shifted[b, tap * channels : (tap + 1) * channels, q * TILE : (q + 1) * TILE] = moved[
                        row : row + channels, tz * TILE : (tz + 1) * TILE
                    ]


def inner_parts(near, own, parts):
    bricks, channels = own.shape[0] - 1, own.shape[1]
    base = lax.axis_index("space") * bricks
    for b in range(bricks):
        here = {s: index_of(near, b, 0, *s, base, bricks) for s in SIDES}
        for q in range(TILES):
            set_groups(
                parts, (b * TILES + q) * channels, lambda c, e: own[here[c, e], :, q * TILE : (q + 1) * TILE]
            )


def on_odd():
    return lax.axis_index("scene") % 2


def set_ends(near, up, mine, other, table, parts):
    bricks, channels = mine.shape[0], mine.shape[1]
    for b in range(bricks):
        table[b] = other[b]
        table[bricks + b] = mine[b]
    table[2 * bricks] = jnp.zeros((channels, TILE), jnp.bfloat16)
    start = (lax.axis_index("space") - 1 + up) * bricks

    def place(b, c, e):
        number = near[0, b, 18 * up + 3 * (c + 1) + e + 1]
        at = number - start
        turned = jnp.where(at < bricks, at + bricks, at - bricks)
        return jnp.where(number < 0, 2 * bricks, jnp.where(up == 1, turned, at))

    for b in range(bricks):
        at = {s: place(b, *s) for s in SIDES}
        set_groups(parts, b * channels, lambda c, e: table[at[c, e]])


def faces_kernel(features, cotangent, mask, near, one, two, own_x, own_g, present, near_out, *rest):
    buffers, sems = rest[:3], rest[3]
    copies = [pltpu.make_async_copy(a, b, sems.at[n]) for n, (a, b) in enumerate(zip((mask, features, cotangent), buffers))]
    copies.append(pltpu.make_async_copy(near, near_out, sems.at[3]))
    for copy in copies:
        copy.start()
    bricks, channels = own_x.shape[0] - 1, own_x.shape[1]
    lower = lane_of((channels, TILE)) < 64
    odd = on_odd() == 1
    copies[0].wait()
    present[...] = buffers[0][0].astype(jnp.float32)
    for side, own in enumerate((own_x, own_g)):
        copies[1 + side].wait()
        for b in range(bricks):
            own[b] = buffers[1 + side][0, b] * jnp.broadcast_to(present[b : b + 1, :], (channels, 512)).astype(
                jnp.bfloat16
            )
        own[bricks] = jnp.zeros((channels, 512), jnp.bfloat16)
    for b in range(bricks):
        x, g = own_x[b].astype(jnp.float32), own_g[b].astype(jnp.float32)
        head = jnp.where(lower, x[:, :TILE], swap_halves(g[:, :TILE])).astype(jnp.bfloat16)
        tail = jnp.where(lower, swap_halves(g[:, 3 * TILE :]), x[:, 3 * TILE :]).astype(jnp.bfloat16)
        one[b] = jnp.where(odd, head, tail)
        two[b] = jnp.where(odd, tail, head)
    copies[3].wait()


def inner_kernel(scale, near, own, gradient, shifted, grad, select_y, select_z, parts, middle, placed):
    rows, bricks, channels = grad.shape[0], own.shape[0] - 1, own.shape[1]
    set_selection(select_y, select_z)
    inner_parts(near, own, parts)
    lower = lane_of((channels, TILE)) < 64
    zero = jnp.zeros((channels, TILE), jnp.float32)
    for b in range(bricks):
        masked = gradient[b].astype(jnp.float32)
        tile = [zero] + [masked[:, q * TILE : (q + 1) * TILE] for q in range(TILES)] + [zero]
        for q in range(TILES):
            at = slice(q * TILE, (q + 1) * TILE)
            placed[b, :channels, at] = swap_halves(jnp.where(lower, tile[q + 2], tile[q + 1])).astype(jnp.bfloat16)
            placed[b, channels : 2 * channels, at] = swap_halves(jnp.where(lower, tile[q + 1], tile[q])).astype(
                jnp.bfloat16
            )
            placed[b, 2 * channels :, at] = tile[q + 1].astype(jnp.bfloat16)
    shift_all(parts, select_y, select_z, middle, shifted, TILES)
    total = None
    for b in range(bricks):
        term = lax.dot_general(
            shifted[b], placed[b], (((1,), (1,)), ((), ())), preferred_element_type=jnp.float32
        )
        total = term if total is None else total + term
    total = total * scale
    count, half = 9 * channels, 9 * channels // 2
    grad[:count, :] = total[:, : 2 * channels]
    grad[count : count + half, :channels] = total[:half, 2 * channels :]
    grad[count : count + half, channels:] = total[half:, 2 * channels :]
    if rows > count + half:
        grad[count + half :, :] = jnp.zeros((rows - count - half, 2 * channels), jnp.float32)


def outer_kernel(
    scale, near, mine, facing, other, inner, select_y, select_z, shifted, grad, table, parts, middle
):
    bricks, channels = mine.shape[0], mine.shape[1]
    odd = on_odd()
    set_ends(near, odd, mine, other, table, parts)
    shift_all(parts, select_y, select_z, middle, shifted, 1)
    x_half = lane_of((channels, TILE)) // 64 == odd
    contract = (((1,), (1,)), ((), ()))
    first = last = None
    for b in range(bricks):
        g, x = jnp.where(x_half, 0, facing[b]), jnp.where(x_half, facing[b], 0)
        one = lax.dot_general(shifted[b], g, contract, preferred_element_type=jnp.float32)
        two = lax.dot_general(x, shifted[b], contract, preferred_element_type=jnp.float32)
        first, last = (one, two) if b == 0 else (first + one, last + two)
    for yz in range(9):
        at = slice(yz * channels, (yz + 1) * channels)
        one, two = first[at], last[:, (8 - yz) * channels : (9 - yz) * channels]
        term = jnp.concatenate([jnp.where(odd == 1, two, one), jnp.where(odd == 1, one, two)], axis=1)
        grad[at, :] = inner[at, :] + term * scale
    grad[9 * channels :, :] = inner[9 * channels :, :]


def shift_kernel(near, own, select_y, select_z, shifted, parts, middle):
    inner_parts(near, own, parts)
    shift_all(parts, select_y, select_z, middle, shifted, TILES)


def tables_kernel(weight, table_y, table_g):
    channels = weight.shape[1]
    for tx in range(3):
        for yz in range(9):
            at = (slice(tx * channels, (tx + 1) * channels), slice(yz * channels, (yz + 1) * channels))
            table_y[at] = weight[9 * tx + yz].astype(jnp.float32).T.astype(jnp.bfloat16)
            table_g[at] = weight[26 - 9 * tx - yz]


def convolve(table, inner, ends, present, out, swapped):
    bricks, channels = out.shape[1], out.shape[2]
    lower = lane_of((channels, TILE)) < 64
    for b in range(bricks):
        main = jnp.dot(table[...], inner[b], preferred_element_type=jnp.float32)
        side = jnp.dot(table[...], ends(b), preferred_element_type=jnp.float32)
        if swapped:
            side = swap_halves(side)

        def term(t, q):
            rows = slice(t * channels, (t + 1) * channels)
            return main[rows, q * TILE : (q + 1) * TILE] if 0 <= q < TILES else side[rows]

        for q in range(TILES):
            sides = jnp.where(lower, term(0, q), term(0, q - 1)) + jnp.where(lower, term(2, q + 1), term(2, q))
            at = slice(q * TILE, (q + 1) * TILE)
            out[0, b, :, at] = ((term(1, q) + swap_halves(sides)) * present[b : b + 1, at]).astype(jnp.bfloat16)


def forward_kernel(
    near, mine, other, table, inner, ends, present, select_y, select_z, out, more_ends, tiles, parts, middle
):
    odd = on_odd()
    set_ends(near, 1 - odd, mine, other, tiles, parts)
    shift_all(parts, select_y, select_z, middle, more_ends, 1)
    half = lane_of(ends.shape[1:]) // 64 == odd
    convolve(table, inner, lambda b: jnp.where(half, more_ends[b], ends[b]), present, out, False)


def backward_kernel(table, inner, ends, more_ends, present, out):
    half = lane_of(ends.shape[1:]) // 64 == on_odd()
    convolve(table, inner, lambda b: jnp.where(half, ends[b], more_ends[b]), present, out, True)


def unpack_kernel(groups, own, *refs):
    parts, (out, whole, blocks, sem) = refs[:groups], refs[-4:]
    place = lax.axis_index("space") * lax.axis_size("scene") + lax.axis_index("scene")
    where = place // 2 % groups
    size, channels = parts[0].shape[0], blocks.shape[1]
    for k in range(groups):
        at = pl.multiple_of(jnp.bitwise_xor(where, k) * size, 8)
        whole[pl.ds(at, size), :] = parts[k][...]
    half, count = groups * size, 9 * channels

    def write(low, high):
        runs = []

        def put(tap, lane, row, rows, first):
            if not runs or runs[-1][0] + runs[-1][2] not in (tap, tap + 1) or (first == 0) != (
                runs[-1][0] + runs[-1][2] == tap
            ):
                runs.append([tap, sum(run[2] for run in runs), 0])
            if first == 0:
                runs[-1][2] += 1
            at = runs[-1][1] + runs[-1][2] - 1
            blocks[at, first : first + rows, :] = whole[row : row + rows, lane * channels : (lane + 1) * channels]

        taps = range(low // channels, min(high, count) // channels)
        for lane, base in ((0, 0), (1, 18)):
            for yz in taps:
                put(base + yz, lane, yz * channels - low, channels, 0)
        if high > count:
            for lane in range(2):
                done = 0
                while done < count // 2:
                    at = lane * (count // 2) + done
                    rows = min(channels - at % channels, count // 2 - done)
                    put(9 + at // channels, lane, count - low + done, rows, at % channels)
                    done += rows
        copies = [
            pltpu.make_async_copy(blocks.at[start : start + n], out.at[tap : tap + n], sem.at[i])
            for i, (tap, start, n) in enumerate(runs)
        ]
        for copy in copies:
            copy.start()
        for copy in copies:
            copy.wait()

    lower = (place % 2 == 0) == own
    pl.when(lower)(lambda: write(0, half))
    pl.when(jnp.logical_not(lower))(lambda: write(half, 2 * half))


def halo_pairs(spaces, scenes):
    pairs = []
    for scene in range(scenes):
        line = [space * scenes + scene for space in range(spaces)]
        line = line[::-1] if scene % 2 else line
        pairs += list(zip(line, line[1:]))
        if scene ^ 1 < scenes:
            pairs.append((line[-1], line[-1] + (scene ^ 1) - scene))
    return pairs


def exchange(x, bit):
    count = lax.axis_size("space") * lax.axis_size("scene")
    return lax.ppermute(x, AXES, [(i, i ^ bit) for i in range(count)])


def all_sum(part, groups):
    count = lax.axis_size("space") * lax.axis_size("scene")
    place = lax.axis_index("space") * lax.axis_size("scene") + lax.axis_index("scene")
    odd, where = place % 2, place // 2 % groups
    half = part.shape[0] // 2
    size = half // groups
    keep = lax.dynamic_slice_in_dim(part, odd * half, half, 0)
    send = lax.dynamic_slice_in_dim(part, (1 - odd) * half, half, 0)
    mine = keep + exchange(send, 1)
    own = lax.dynamic_slice_in_dim(mine, where * size, size, 0)
    got = []
    for k in range(1, groups):
        got.append(exchange(lax.dynamic_slice_in_dim(mine, (where ^ k) * size, size, 0), 2 * k))
    for one in got:
        own = own + one
    bit = 2 * groups
    while bit < count:
        wide = 4 if 4 * bit <= count else 2
        got = []
        for k in range(1, wide):
            got.append(exchange(own, bit * k))
        own = own + got[0]
        if wide == 4:
            own = own + (got[1] + got[2])
        bit *= wide
    chunks = [own]
    for k in range(1, groups):
        chunks.append(exchange(own, 2 * k))
    theirs = []
    for k in range(groups):
        theirs.append(exchange(chunks[k], 1))
    return chunks, theirs


def program(features, cotangent, weight, neighbours, occupancy):
    bricks, channels = features.shape[1], features.shape[2]
    spaces, scenes = lax.axis_size("space"), lax.axis_size("scene")
    scale = 1.0 / math.sqrt(scenes * bricks * spaces * 512)
    groups = 4
    unit = 16 * groups
    rows = -(-(27 * channels // 2) // unit) * unit

    def call(kernel, shapes, inputs, specs, scratch, limit=32 << 20):
        single = not isinstance(shapes, list)
        return pl.pallas_call(
            kernel,
            out_shape=shapes,
            in_specs=specs,
            out_specs=VMEM if single else [VMEM] * len(shapes),
            scratch_shapes=scratch,
            compiler_params=pltpu.CompilerParams(vmem_limit_bytes=limit),
            cost_estimate=pl.CostEstimate(flops=10**8, bytes_accessed=10**6, transcendentals=0),
        )(*inputs)

    def shape(*dims, dtype=jnp.bfloat16):
        return jax.ShapeDtypeStruct(dims, dtype)

    def scratch(*dims, dtype=jnp.bfloat16):
        return pltpu.VMEM(dims, dtype)

    many = bricks * TILES * channels
    parts = [scratch(2 * many, 2 * TILE), scratch(3 * many, 2 * TILE)]
    few = bricks * channels
    ends = [scratch(2 * bricks + 1, channels, TILE), scratch(2 * few, 2 * TILE), scratch(3 * few, 2 * TILE)]
    chosen = shape(2 * TILE, 3 * TILE)
    face, brick = shape(bricks, channels, TILE), shape(bricks + 1, channels, 512)
    one, two, own_x, own_g, present, near = call(
        faces_kernel,
        [face, face, brick, brick, shape(bricks, 512, dtype=jnp.float32), shape(*neighbours.shape, dtype=jnp.int32)],
        tuple(
            pltpu.with_memory_space_constraint(a, pltpu.HBM) for a in (features, cotangent, occupancy, neighbours)
        ),
        [HBM] * 4,
        [
            scratch(*occupancy.shape, dtype=jnp.int32),
            scratch(*features.shape),
            scratch(*features.shape),
            pltpu.SemaphoreType.DMA((4,)),
        ],
        limit=16 << 20,
    )
    forth = halo_pairs(spaces, scenes)
    got_one = lax.ppermute(one, AXES, forth)
    got_two = lax.ppermute(two, AXES, [(b, a) for a, b in forth])
    volume, grads = shape(bricks, 9 * channels, 512), shape(rows, 2 * channels, dtype=jnp.float32)
    shifted = shape(bricks, 9 * channels, TILE)
    inner_x, grad, *select = call(
        functools.partial(inner_kernel, scale),
        [volume, grads, chosen, chosen],
        (near, own_x, own_g),
        [SMEM, VMEM, VMEM],
        [*parts, scratch(bricks, 3 * channels, 512)],
    )
    ends_one, grad = call(
        functools.partial(outer_kernel, scale),
        [shifted, grads],
        (near, one, two, got_one, grad, *select),
        [SMEM] + [VMEM] * 6,
        ends,
    )
    table = shape(3 * channels, 9 * channels)
    table_y, table_g = call(tables_kernel, [table, table], (weight,), [VMEM], [])
    inner_g = call(shift_kernel, volume, (near, own_g, *select), [SMEM] + [VMEM] * 3, parts)
    out_y, ends_two = call(
        forward_kernel,
        [shape(*features.shape), shifted],
        (near, two, got_two, table_y, inner_x, ends_one, present, *select),
        [SMEM] + [VMEM] * 8,
        ends,
    )
    out_g = call(
        backward_kernel, shape(*cotangent.shape), (table_g, inner_g, ends_one, ends_two, present), [VMEM] * 5, []
    )
    mine, theirs = all_sum(grad, groups)
    taps = shape(27, channels, channels, dtype=jnp.float32)

    def unpack(own, parts, *before):
        return pl.pallas_call(
            functools.partial(unpack_kernel, groups, own),
            out_shape=taps,
            in_specs=[VMEM] * groups + [HBM] * len(before),
            out_specs=HBM,
            scratch_shapes=[
                scratch(rows // 2, 2 * channels, dtype=jnp.float32),
                scratch(14, channels, channels, dtype=jnp.float32),
                pltpu.SemaphoreType.DMA((3,)),
            ],
            input_output_aliases={groups: 0} if before else {},
            compiler_params=pltpu.CompilerParams(vmem_limit_bytes=16 << 20),
            cost_estimate=pl.CostEstimate(flops=10**6, bytes_accessed=10**6, transcendentals=0),
            name="unpack",
        )(*parts, *before)

    out_w = unpack(True, mine)
    out_w = unpack(False, theirs, out_w)
    return out_y, out_g, out_w


def solution(mesh):
    in_specs = (
        P("scene", "space", None, None),
        P("scene", "space", None, None),
        P(),
        P("scene", "space", None),
        P("scene", "space", None),
    )
    out_specs = (P("scene", "space", None, None), P("scene", "space", None, None), P())
    return jax.shard_map(program, mesh=mesh, in_specs=in_specs, out_specs=out_specs, check_vma=False)
```

```python
import functools
import math

import jax
import jax.numpy as jnp
from jax import lax
from jax.experimental import pallas as pl
from jax.experimental.pallas import tpu as pltpu
from jax.sharding import PartitionSpec as P


TILE = 128
TILES = 4
AXES = ("space", "scene")
SMEM = pl.BlockSpec(memory_space=pltpu.SMEM)
VMEM = pl.BlockSpec(memory_space=pltpu.VMEM)
HBM = pl.BlockSpec(memory_space=pltpu.HBM)
SIDES = [(c, e) for c in (-1, 0, 1) for e in (-1, 0, 1)]


def set_selection(select_y, select_z):
    row = lax.broadcasted_iota(jnp.int32, (TILE, TILE), 0)
    lane = lax.broadcasted_iota(jnp.int32, (TILE, TILE), 1)
    for select, step in ((select_y, 8), (select_z, 1)):
        now = lane // step % 8
        for t in range(3):
            moved = now + t - 1
            wanted = lane + step * (jnp.bitwise_and(moved, 7) - now)
            beyond = jnp.where(moved == jnp.bitwise_and(moved, 7), 0, 1)
            for source in range(2):
                hit = jnp.where(beyond == source, wanted, -1) == row
                select[source * TILE : (source + 1) * TILE, t * TILE : (t + 1) * TILE] = jnp.where(
                    hit, 1.0, 0.0
                ).astype(jnp.bfloat16)


def lane_of(shape):
    return lax.broadcasted_iota(jnp.int32, shape, len(shape) - 1)


def swap_halves(x):
    return pltpu.roll(x, 64, x.ndim - 1)


def grouped(pick, shape):
    lane = lane_of(shape)
    j_high, k_high = lane % 64 >= 32, lane % 8 >= 4
    return (
        pick(0, 0),
        jnp.where(j_high, pick(-1, 0), pick(1, 0)),
        jnp.where(k_high, pick(0, -1), pick(0, 1)),
        jnp.where(
            j_high,
            jnp.where(k_high, pick(-1, -1), pick(-1, 1)),
            jnp.where(k_high, pick(1, -1), pick(1, 1)),
        ),
    )


def group_at(parts, row, channels, g):
    row = parts.shape[0] // 2 * (g // 2) + row
    return slice(row, row + channels), slice(g % 2 * TILE, (g % 2 + 1) * TILE)


def set_groups(parts, row, channels, pick):
    for g, tile in enumerate(grouped(pick, (channels, TILE))):
        parts[group_at(parts, row, channels, g)] = tile


def index_of(near, b, a, c, e, start, none):
    number = near[0, b, 9 * (a + 1) + 3 * (c + 1) + e + 1]
    return jnp.where(number < 0, none, number - start)


def shift_all(parts, select_y, select_z, middle, shifted, tiles):
    bricks, channels, rows = shifted.shape[0], shifted.shape[1] // 9, parts.shape[0] // 2
    for side in range(2):
        moved = jnp.dot(
            parts[side * rows : (side + 1) * rows, :], select_y[...], preferred_element_type=jnp.float32
        ).astype(jnp.bfloat16)
        for t in range(3):
            middle[t * rows : (t + 1) * rows, side * TILE : (side + 1) * TILE] = moved[:, t * TILE : (t + 1) * TILE]
    for ty in range(3):
        moved = jnp.dot(
            middle[ty * rows : (ty + 1) * rows, :], select_z[...], preferred_element_type=jnp.float32
        ).astype(jnp.bfloat16)
        for b in range(bricks):
            for q in range(tiles):
                row = (b * tiles + q) * channels
                for tz in range(3):
                    tap = 3 * ty + tz
                    shifted[b, tap * channels : (tap + 1) * channels, q * TILE : (q + 1) * TILE] = moved[
                        row : row + channels, tz * TILE : (tz + 1) * TILE
                    ]


def inner_parts(near, own, parts):
    bricks, channels = own.shape[0] - 1, own.shape[1]
    base = lax.axis_index("space") * bricks
    for b in range(bricks):
        here = {s: index_of(near, b, 0, *s, base, bricks) for s in SIDES}
        for q in range(TILES):
            set_groups(
                parts, (b * TILES + q) * channels, channels, lambda c, e: own[here[c, e], :, q * TILE : (q + 1) * TILE]
            )


def on_odd():
    return lax.axis_index("scene") % 2


def set_ends(near, up, mine, other, table, parts):
    bricks, channels = mine.shape[0], mine.shape[1]
    for b in range(bricks):
        table[b] = other[b]
        table[bricks + b] = mine[b]
    table[2 * bricks] = jnp.zeros((channels, TILE), jnp.bfloat16)
    start = (lax.axis_index("space") - 1 + up) * bricks

    def place(b, c, e):
        number = near[0, b, 18 * up + 3 * (c + 1) + e + 1]
        at = number - start
        turned = jnp.where(at < bricks, at + bricks, at - bricks)
        return jnp.where(number < 0, 2 * bricks, jnp.where(up == 1, turned, at))

    for b in range(bricks):
        at = {s: place(b, *s) for s in SIDES}
        set_groups(parts, b * channels, channels, lambda c, e: table[at[c, e]])


def prepare_ends(near, up, mine, table, local, weights):
    bricks, channels = mine.shape[0], mine.shape[1]
    for b in range(bricks):
        table[b] = mine[b]
    table[bricks] = jnp.zeros((channels, TILE), jnp.bfloat16)
    start = (lax.axis_index("space") - 1 + up) * bricks
    for b in range(bricks):
        own, other = {}, {}
        for c, e in SIDES:
            number = near[0, b, 18 * up + 3 * (c + 1) + e + 1]
            at = number - start
            at_own, at_other = at - bricks * (1 - up), at - bricks * up
            inside = (number >= 0) & (at_own >= 0) & (at_own < bricks)
            own[c, e] = jnp.where(inside, at_own, bricks)
            other[c, e] = jnp.where(number >= 0, at_other, -1)
        set_groups(local, b * channels, channels, lambda c, e: table[own[c, e]])
        for n in range(bricks):
            flags = grouped(lambda c, e: jnp.where(other[c, e] == n, 1.0, 0.0), weights.shape[3:])
            for g in range(4):
                weights[b, g, n] = jnp.broadcast_to(flags[g], weights.shape[3:]).astype(jnp.bfloat16)


def faces_kernel(features, cotangent, mask, near, one, two, own_x, own_g, present, near_out, *rest):
    buffers, sems = rest[:3], rest[3]
    copies = [pltpu.make_async_copy(a, b, sems.at[n]) for n, (a, b) in enumerate(zip((mask, features, cotangent), buffers))]
    copies.append(pltpu.make_async_copy(near, near_out, sems.at[3]))
    for copy in copies:
        copy.start()
    bricks, channels = own_x.shape[0] - 1, own_x.shape[1]
    lower = lane_of((channels, TILE)) < 64
    odd = on_odd() == 1
    copies[0].wait()
    present[...] = buffers[0][0].astype(jnp.float32)
    for side, own in enumerate((own_x, own_g)):
        copies[1 + side].wait()
        for b in range(bricks):
            own[b] = buffers[1 + side][0, b] * jnp.broadcast_to(present[b : b + 1, :], (channels, 512)).astype(
                jnp.bfloat16
            )
        own[bricks] = jnp.zeros((channels, 512), jnp.bfloat16)
    for b in range(bricks):
        x, g = own_x[b].astype(jnp.float32), own_g[b].astype(jnp.float32)
        head = jnp.where(lower, x[:, :TILE], swap_halves(g[:, :TILE])).astype(jnp.bfloat16)
        tail = jnp.where(lower, swap_halves(g[:, 3 * TILE :]), x[:, 3 * TILE :]).astype(jnp.bfloat16)
        one[b] = jnp.where(odd, head, tail)
        two[b] = jnp.where(odd, tail, head)
    copies[3].wait()


def inner_kernel(
    scale, near, own, gradient, mine, shifted, grad, select_y, select_z, local, weights, parts, middle, placed, table
):
    rows, bricks, channels = grad.shape[0], own.shape[0] - 1, own.shape[1]
    set_selection(select_y, select_z)
    prepare_ends(near, on_odd(), mine, table, local, weights)
    inner_parts(near, own, parts)
    lower = lane_of((channels, TILE)) < 64
    zero = jnp.zeros((channels, TILE), jnp.float32)
    for b in range(bricks):
        masked = gradient[b].astype(jnp.float32)
        tile = [zero] + [masked[:, q * TILE : (q + 1) * TILE] for q in range(TILES)] + [zero]
        for q in range(TILES):
            at = slice(q * TILE, (q + 1) * TILE)
            placed[b, :channels, at] = swap_halves(jnp.where(lower, tile[q + 2], tile[q + 1])).astype(jnp.bfloat16)
            placed[b, channels : 2 * channels, at] = swap_halves(jnp.where(lower, tile[q + 1], tile[q])).astype(
                jnp.bfloat16
            )
            placed[b, 2 * channels :, at] = tile[q + 1].astype(jnp.bfloat16)
    shift_all(parts, select_y, select_z, middle, shifted, TILES)
    total = None
    for b in range(bricks):
        term = lax.dot_general(
            shifted[b], placed[b], (((1,), (1,)), ((), ())), preferred_element_type=jnp.float32
        )
        total = term if total is None else total + term
    total = total * scale
    count, half = 9 * channels, 9 * channels // 2
    grad[:count, :] = total[:, : 2 * channels]
    grad[count : count + half, :channels] = total[:half, 2 * channels :]
    grad[count : count + half, channels:] = total[half:, 2 * channels :]
    if rows > count + half:
        grad[count + half :, :] = jnp.zeros((rows - count - half, 2 * channels), jnp.float32)


def outer_kernel(
    scale, facing, other, local, weights, inner, select_y, select_z, shifted, grad, parts, middle
):
    bricks, channels = other.shape[0], other.shape[1]
    odd = on_odd()
    for b in range(bricks):
        for g in range(4):
            at = group_at(parts, b * channels, channels, g)
            tile = local[at]
            for n in range(bricks):
                tile = tile + jnp.concatenate([weights[b, g, n]] * (channels // 16), axis=0) * other[n]
            parts[at] = tile
    shift_all(parts, select_y, select_z, middle, shifted, 1)
    x_half = lane_of((channels, TILE)) // 64 == odd
    contract = (((1,), (1,)), ((), ()))
    first = last = None
    for b in range(bricks):
        g, x = jnp.where(x_half, 0, facing[b]), jnp.where(x_half, facing[b], 0)
        one = lax.dot_general(shifted[b], g, contract, preferred_element_type=jnp.float32)
        two = lax.dot_general(x, shifted[b], contract, preferred_element_type=jnp.float32)
        first, last = (one, two) if b == 0 else (first + one, last + two)
    for yz in range(9):
        at = slice(yz * channels, (yz + 1) * channels)
        one, two = first[at], last[:, (8 - yz) * channels : (9 - yz) * channels]
        term = jnp.concatenate([jnp.where(odd == 1, two, one), jnp.where(odd == 1, one, two)], axis=1)
        grad[at, :] = inner[at, :] + term * scale
    grad[9 * channels :, :] = inner[9 * channels :, :]


def shift_kernel(near, own, select_y, select_z, shifted, parts, middle):
    inner_parts(near, own, parts)
    shift_all(parts, select_y, select_z, middle, shifted, TILES)


def tables_kernel(weight, table_y, table_g):
    channels = weight.shape[1]
    for tx in range(3):
        for yz in range(9):
            at = (slice(tx * channels, (tx + 1) * channels), slice(yz * channels, (yz + 1) * channels))
            table_y[at] = weight[9 * tx + yz].astype(jnp.float32).T.astype(jnp.bfloat16)
            table_g[at] = weight[26 - 9 * tx - yz]


def convolve(table, inner, ends, present, out, swapped):
    bricks, channels = out.shape[1], out.shape[2]
    lower = lane_of((channels, TILE)) < 64
    for b in range(bricks):
        main = jnp.dot(table[...], inner[b], preferred_element_type=jnp.float32)
        side = jnp.dot(table[...], ends(b), preferred_element_type=jnp.float32)
        if swapped:
            side = swap_halves(side)

        def term(t, q):
            rows = slice(t * channels, (t + 1) * channels)
            return main[rows, q * TILE : (q + 1) * TILE] if 0 <= q < TILES else side[rows]

        for q in range(TILES):
            sides = jnp.where(lower, term(0, q), term(0, q - 1)) + jnp.where(lower, term(2, q + 1), term(2, q))
            at = slice(q * TILE, (q + 1) * TILE)
            out[0, b, :, at] = ((term(1, q) + swap_halves(sides)) * present[b : b + 1, at]).astype(jnp.bfloat16)


def forward_kernel(
    near, mine, other, table, inner, ends, present, select_y, select_z, out, more_ends, tiles, parts, middle
):
    odd = on_odd()
    set_ends(near, 1 - odd, mine, other, tiles, parts)
    shift_all(parts, select_y, select_z, middle, more_ends, 1)
    half = lane_of(ends.shape[1:]) // 64 == odd
    convolve(table, inner, lambda b: jnp.where(half, more_ends[b], ends[b]), present, out, False)


def backward_kernel(table, inner, ends, more_ends, present, out):
    half = lane_of(ends.shape[1:]) // 64 == on_odd()
    convolve(table, inner, lambda b: jnp.where(half, ends[b], more_ends[b]), present, out, True)


def unpack_kernel(groups, own, *refs):
    parts, (out, whole, blocks, sem) = refs[:groups], refs[-4:]
    place = lax.axis_index("space") * lax.axis_size("scene") + lax.axis_index("scene")
    where = place // 2 % groups
    size, channels = parts[0].shape[0], blocks.shape[1]
    for k in range(groups):
        at = pl.multiple_of(jnp.bitwise_xor(where, k) * size, 8)
        whole[pl.ds(at, size), :] = parts[k][...]
    half, count = groups * size, 9 * channels

    def write(low, high):
        runs = []

        def put(tap, lane, row, rows, first):
            if not runs or runs[-1][0] + runs[-1][2] not in (tap, tap + 1) or (first == 0) != (
                runs[-1][0] + runs[-1][2] == tap
            ):
                runs.append([tap, sum(run[2] for run in runs), 0])
            if first == 0:
                runs[-1][2] += 1
            at = runs[-1][1] + runs[-1][2] - 1
            blocks[at, first : first + rows, :] = whole[row : row + rows, lane * channels : (lane + 1) * channels]

        taps = range(low // channels, min(high, count) // channels)
        for lane, base in ((0, 0), (1, 18)):
            for yz in taps:
                put(base + yz, lane, yz * channels - low, channels, 0)
        if high > count:
            for lane in range(2):
                done = 0
                while done < count // 2:
                    at = lane * (count // 2) + done
                    rows = min(channels - at % channels, count // 2 - done)
                    put(9 + at // channels, lane, count - low + done, rows, at % channels)
                    done += rows
        copies = [
            pltpu.make_async_copy(blocks.at[start : start + n], out.at[tap : tap + n], sem.at[i])
            for i, (tap, start, n) in enumerate(runs)
        ]
        for copy in copies:
            copy.start()
        for copy in copies:
            copy.wait()

    lower = (place % 2 == 0) == own
    pl.when(lower)(lambda: write(0, half))
    pl.when(jnp.logical_not(lower))(lambda: write(half, 2 * half))


def halo_pairs(spaces, scenes):
    pairs = []
    for scene in range(scenes):
        line = [space * scenes + scene for space in range(spaces)]
        line = line[::-1] if scene % 2 else line
        pairs += list(zip(line, line[1:]))
        if scene ^ 1 < scenes:
            pairs.append((line[-1], line[-1] + (scene ^ 1) - scene))
    return pairs


def exchange(x, bit):
    count = lax.axis_size("space") * lax.axis_size("scene")
    return lax.ppermute(x, AXES, [(i, i ^ bit) for i in range(count)])


def all_sum(part, groups):
    count = lax.axis_size("space") * lax.axis_size("scene")
    place = lax.axis_index("space") * lax.axis_size("scene") + lax.axis_index("scene")
    odd, where = place % 2, place // 2 % groups
    half = part.shape[0] // 2
    size = half // groups
    keep = lax.dynamic_slice_in_dim(part, odd * half, half, 0)
    send = lax.dynamic_slice_in_dim(part, (1 - odd) * half, half, 0)
    mine = keep + exchange(send, 1)
    own = lax.dynamic_slice_in_dim(mine, where * size, size, 0)
    got = []
    for k in range(1, groups):
        got.append(exchange(lax.dynamic_slice_in_dim(mine, (where ^ k) * size, size, 0), 2 * k))
    for one in got:
        own = own + one
    bit = 2 * groups
    while bit < count:
        wide = 4 if 4 * bit <= count else 2
        got = []
        for k in range(1, wide):
            got.append(exchange(own, bit * k))
        own = own + got[0]
        if wide == 4:
            own = own + (got[1] + got[2])
        bit *= wide
    chunks = [own]
    for k in range(1, groups):
        chunks.append(exchange(own, 2 * k))
    theirs = []
    for k in range(groups):
        theirs.append(exchange(chunks[k], 1))
    return chunks, theirs


def program(features, cotangent, weight, neighbours, occupancy):
    bricks, channels = features.shape[1], features.shape[2]
    spaces, scenes = lax.axis_size("space"), lax.axis_size("scene")
    scale = 1.0 / math.sqrt(scenes * bricks * spaces * 512)
    groups = 4
    unit = 16 * groups
    rows = -(-(27 * channels // 2) // unit) * unit

    def call(kernel, shapes, inputs, specs, scratch, limit=32 << 20):
        single = not isinstance(shapes, list)
        return pl.pallas_call(
            kernel,
            out_shape=shapes,
            in_specs=specs,
            out_specs=VMEM if single else [VMEM] * len(shapes),
            scratch_shapes=scratch,
            compiler_params=pltpu.CompilerParams(vmem_limit_bytes=limit),
            cost_estimate=pl.CostEstimate(flops=10**8, bytes_accessed=10**6, transcendentals=0),
        )(*inputs)

    def shape(*dims, dtype=jnp.bfloat16):
        return jax.ShapeDtypeStruct(dims, dtype)

    def scratch(*dims, dtype=jnp.bfloat16):
        return pltpu.VMEM(dims, dtype)

    many = bricks * TILES * channels
    parts = [scratch(2 * many, 2 * TILE), scratch(3 * many, 2 * TILE)]
    few = bricks * channels
    ends = [scratch(2 * bricks + 1, channels, TILE), scratch(2 * few, 2 * TILE), scratch(3 * few, 2 * TILE)]
    chosen = shape(2 * TILE, 3 * TILE)
    face, brick = shape(bricks, channels, TILE), shape(bricks + 1, channels, 512)
    one, two, own_x, own_g, present, near = call(
        faces_kernel,
        [face, face, brick, brick, shape(bricks, 512, dtype=jnp.float32), shape(*neighbours.shape, dtype=jnp.int32)],
        tuple(
            pltpu.with_memory_space_constraint(a, pltpu.HBM) for a in (features, cotangent, occupancy, neighbours)
        ),
        [HBM] * 4,
        [
            scratch(*occupancy.shape, dtype=jnp.int32),
            scratch(*features.shape),
            scratch(*features.shape),
            pltpu.SemaphoreType.DMA((4,)),
        ],
        limit=16 << 20,
    )
    forth = halo_pairs(spaces, scenes)
    got_one = lax.ppermute(one, AXES, forth)
    got_two = lax.ppermute(two, AXES, [(b, a) for a, b in forth])
    volume, grads = shape(bricks, 9 * channels, 512), shape(rows, 2 * channels, dtype=jnp.float32)
    shifted = shape(bricks, 9 * channels, TILE)
    inner_x, grad, *select, near_ends, weights = call(
        functools.partial(inner_kernel, scale),
        [volume, grads, chosen, chosen, shape(2 * few, 2 * TILE), shape(bricks, 4, bricks, 16, TILE)],
        (near, own_x, own_g, one),
        [SMEM] + [VMEM] * 3,
        [*parts, scratch(bricks, 3 * channels, 512), scratch(bricks + 1, channels, TILE)],
    )
    ends_one, grad = call(
        functools.partial(outer_kernel, scale),
        [shifted, grads],
        (two, got_one, near_ends, weights, grad, *select),
        [VMEM] * 7,
        ends[1:],
    )
    table = shape(3 * channels, 9 * channels)
    table_y, table_g = call(tables_kernel, [table, table], (weight,), [VMEM], [])
    inner_g = call(shift_kernel, volume, (near, own_g, *select), [SMEM] + [VMEM] * 3, parts)
    out_y, ends_two = call(
        forward_kernel,
        [shape(*features.shape), shifted],
        (near, two, got_two, table_y, inner_x, ends_one, present, *select),
        [SMEM] + [VMEM] * 8,
        ends,
    )
    out_g = call(
        backward_kernel, shape(*cotangent.shape), (table_g, inner_g, ends_one, ends_two, present), [VMEM] * 5, []
    )
    mine, theirs = all_sum(grad, groups)
    taps = shape(27, channels, channels, dtype=jnp.float32)

    def unpack(own, parts, *before):
        return pl.pallas_call(
            functools.partial(unpack_kernel, groups, own),
            out_shape=taps,
            in_specs=[VMEM] * groups + [HBM] * len(before),
            out_specs=HBM,
            scratch_shapes=[
                scratch(rows // 2, 2 * channels, dtype=jnp.float32),
                scratch(14, channels, channels, dtype=jnp.float32),
                pltpu.SemaphoreType.DMA((3,)),
            ],
            input_output_aliases={groups: 0} if before else {},
            compiler_params=pltpu.CompilerParams(vmem_limit_bytes=16 << 20),
            cost_estimate=pl.CostEstimate(flops=10**6, bytes_accessed=10**6, transcendentals=0),
            name="unpack",
        )(*parts, *before)

    out_w = unpack(True, mine)
    out_w = unpack(False, theirs, out_w)
    return out_y, out_g, out_w


def solution(mesh):
    in_specs = (
        P("scene", "space", None, None),
        P("scene", "space", None, None),
        P(),
        P("scene", "space", None),
        P("scene", "space", None),
    )
    out_specs = (P("scene", "space", None, None), P("scene", "space", None, None), P())
    return jax.shard_map(program, mesh=mesh, in_specs=in_specs, out_specs=out_specs, check_vma=False)
```

```python
import functools
import math

import jax
import jax.numpy as jnp
from jax import lax
from jax.experimental import pallas as pl
from jax.experimental.pallas import tpu as pltpu
from jax.sharding import PartitionSpec as P


TILE = 128
TILES = 4
AXES = ("space", "scene")
SMEM = pl.BlockSpec(memory_space=pltpu.SMEM)
VMEM = pl.BlockSpec(memory_space=pltpu.VMEM)
HBM = pl.BlockSpec(memory_space=pltpu.HBM)
SIDES = [(c, e) for c in (-1, 0, 1) for e in (-1, 0, 1)]


def set_selection(select_y, select_z):
    row = lax.broadcasted_iota(jnp.int32, (TILE, TILE), 0)
    lane = lax.broadcasted_iota(jnp.int32, (TILE, TILE), 1)
    for select, step in ((select_y, 8), (select_z, 1)):
        now = lane // step % 8
        for t in range(3):
            moved = now + t - 1
            wanted = lane + step * (jnp.bitwise_and(moved, 7) - now)
            beyond = jnp.where(moved == jnp.bitwise_and(moved, 7), 0, 1)
            for source in range(2):
                hit = jnp.where(beyond == source, wanted, -1) == row
                select[source * TILE : (source + 1) * TILE, t * TILE : (t + 1) * TILE] = jnp.where(
                    hit, 1.0, 0.0
                ).astype(jnp.bfloat16)


def lane_of(shape):
    return lax.broadcasted_iota(jnp.int32, shape, len(shape) - 1)


def swap_halves(x):
    return pltpu.roll(x, 64, x.ndim - 1)


def grouped(pick, shape):
    lane = lane_of(shape)
    j_high, k_high = lane % 64 >= 32, lane % 8 >= 4
    return (
        pick(0, 0),
        jnp.where(j_high, pick(-1, 0), pick(1, 0)),
        jnp.where(k_high, pick(0, -1), pick(0, 1)),
        jnp.where(
            j_high,
            jnp.where(k_high, pick(-1, -1), pick(-1, 1)),
            jnp.where(k_high, pick(1, -1), pick(1, 1)),
        ),
    )


def group_at(parts, row, channels, g):
    row = parts.shape[0] // 2 * (g // 2) + row
    return slice(row, row + channels), slice(g % 2 * TILE, (g % 2 + 1) * TILE)


def set_groups(parts, row, channels, pick):
    for g, tile in enumerate(grouped(pick, (channels, TILE))):
        parts[group_at(parts, row, channels, g)] = tile


def index_of(near, b, a, c, e, start, none):
    number = near[0, b, 9 * (a + 1) + 3 * (c + 1) + e + 1]
    return jnp.where(number < 0, none, number - start)


def shift_all(parts, select_y, select_z, middle, shifted, tiles):
    bricks, channels, rows = shifted.shape[0], shifted.shape[1] // 9, parts.shape[0] // 2
    for side in range(2):
        moved = jnp.dot(
            parts[side * rows : (side + 1) * rows, :], select_y[...], preferred_element_type=jnp.float32
        ).astype(jnp.bfloat16)
        for t in range(3):
            middle[t * rows : (t + 1) * rows, side * TILE : (side + 1) * TILE] = moved[:, t * TILE : (t + 1) * TILE]
    for ty in range(3):
        moved = jnp.dot(
            middle[ty * rows : (ty + 1) * rows, :], select_z[...], preferred_element_type=jnp.float32
        ).astype(jnp.bfloat16)
        for b in range(bricks):
            for q in range(tiles):
                row = (b * tiles + q) * channels
                for tz in range(3):
                    tap = 3 * ty + tz
                    shifted[b, tap * channels : (tap + 1) * channels, q * TILE : (q + 1) * TILE] = moved[
                        row : row + channels, tz * TILE : (tz + 1) * TILE
                    ]


def inner_parts(near, own, parts):
    bricks, channels = own.shape[0] - 1, own.shape[1]
    base = lax.axis_index("space") * bricks
    for b in range(bricks):
        here = {s: index_of(near, b, 0, *s, base, bricks) for s in SIDES}
        for q in range(TILES):
            set_groups(
                parts, (b * TILES + q) * channels, channels, lambda c, e: own[here[c, e], :, q * TILE : (q + 1) * TILE]
            )


def on_odd():
    return lax.axis_index("scene") % 2


def set_ends(near, up, mine, other, table, parts):
    bricks, channels = mine.shape[0], mine.shape[1]
    for b in range(bricks):
        table[b] = other[b]
        table[bricks + b] = mine[b]
    table[2 * bricks] = jnp.zeros((channels, TILE), jnp.bfloat16)
    start = (lax.axis_index("space") - 1 + up) * bricks

    def place(b, c, e):
        number = near[0, b, 18 * up + 3 * (c + 1) + e + 1]
        at = number - start
        turned = jnp.where(at < bricks, at + bricks, at - bricks)
        return jnp.where(number < 0, 2 * bricks, jnp.where(up == 1, turned, at))

    for b in range(bricks):
        at = {s: place(b, *s) for s in SIDES}
        set_groups(parts, b * channels, channels, lambda c, e: table[at[c, e]])


def prepare_ends(near, up, mine, table, local, weights):
    bricks, channels = mine.shape[0], mine.shape[1]
    for b in range(bricks):
        table[b] = mine[b]
    table[bricks] = jnp.zeros((channels, TILE), jnp.bfloat16)
    start = (lax.axis_index("space") - 1 + up) * bricks
    for b in range(bricks):
        own, other = {}, {}
        for c, e in SIDES:
            number = near[0, b, 18 * up + 3 * (c + 1) + e + 1]
            at = number - start
            at_own, at_other = at - bricks * (1 - up), at - bricks * up
            inside = (number >= 0) & (at_own >= 0) & (at_own < bricks)
            own[c, e] = jnp.where(inside, at_own, bricks)
            other[c, e] = jnp.where(number >= 0, at_other, -1)
        set_groups(local, b * channels, channels, lambda c, e: table[own[c, e]])
        for n in range(bricks):
            flags = grouped(lambda c, e: jnp.where(other[c, e] == n, 1.0, 0.0), weights.shape[3:])
            for g in range(4):
                weights[b, g, n] = jnp.broadcast_to(flags[g], weights.shape[3:]).astype(jnp.bfloat16)


def faces_kernel(features, cotangent, mask, near, one, two, own_x, own_g, present, near_out, *rest):
    buffers, sems = rest[:3], rest[3]
    copies = [pltpu.make_async_copy(a, b, sems.at[n]) for n, (a, b) in enumerate(zip((mask, features, cotangent), buffers))]
    copies.append(pltpu.make_async_copy(near, near_out, sems.at[3]))
    for copy in copies:
        copy.start()
    bricks, channels = own_x.shape[0] - 1, own_x.shape[1]
    lower = lane_of((channels, TILE)) < 64
    odd = on_odd() == 1
    copies[0].wait()
    present[...] = buffers[0][0].astype(jnp.float32)
    for side, own in enumerate((own_x, own_g)):
        copies[1 + side].wait()
        for b in range(bricks):
            own[b] = buffers[1 + side][0, b] * jnp.broadcast_to(present[b : b + 1, :], (channels, 512)).astype(
                jnp.bfloat16
            )
        own[bricks] = jnp.zeros((channels, 512), jnp.bfloat16)
    for b in range(bricks):
        x, g = own_x[b].astype(jnp.float32), own_g[b].astype(jnp.float32)
        head = jnp.where(lower, x[:, :TILE], swap_halves(g[:, :TILE])).astype(jnp.bfloat16)
        tail = jnp.where(lower, swap_halves(g[:, 3 * TILE :]), x[:, 3 * TILE :]).astype(jnp.bfloat16)
        one[b] = jnp.where(odd, head, tail)
        two[b] = jnp.where(odd, tail, head)
    copies[3].wait()


def inner_kernel(
    scale, near, own, gradient, mine, shifted, grad, select_y, select_z, local, weights, parts, middle, placed, table
):
    rows, bricks, channels = grad.shape[0], own.shape[0] - 1, own.shape[1]
    set_selection(select_y, select_z)
    prepare_ends(near, on_odd(), mine, table, local, weights)
    inner_parts(near, own, parts)
    lower = lane_of((channels, TILE)) < 64
    zero = jnp.zeros((channels, TILE), jnp.float32)
    for b in range(bricks):
        masked = gradient[b].astype(jnp.float32)
        tile = [zero] + [masked[:, q * TILE : (q + 1) * TILE] for q in range(TILES)] + [zero]
        for q in range(TILES):
            at = slice(q * TILE, (q + 1) * TILE)
            placed[b, :channels, at] = swap_halves(jnp.where(lower, tile[q + 2], tile[q + 1])).astype(jnp.bfloat16)
            placed[b, channels : 2 * channels, at] = swap_halves(jnp.where(lower, tile[q + 1], tile[q])).astype(
                jnp.bfloat16
            )
            placed[b, 2 * channels :, at] = tile[q + 1].astype(jnp.bfloat16)
    shift_all(parts, select_y, select_z, middle, shifted, TILES)
    total = None
    for b in range(bricks):
        term = lax.dot_general(
            shifted[b], placed[b], (((1,), (1,)), ((), ())), preferred_element_type=jnp.float32
        )
        total = term if total is None else total + term
    total = total * scale
    count, half = 9 * channels, 9 * channels // 2
    grad[:count, :] = total[:, : 2 * channels]
    grad[count : count + half, :channels] = total[:half, 2 * channels :]
    grad[count : count + half, channels:] = total[half:, 2 * channels :]
    if rows > count + half:
        grad[count + half :, :] = jnp.zeros((rows - count - half, 2 * channels), jnp.float32)


def device_place():
    return lax.axis_index("space") * lax.axis_size("scene") + lax.axis_index("scene")


def outer_kernel(
    scale, groups, facing, other, local, weights, inner, select_y, select_z,
    shifted, send_far, send_rest, keep_far, keep_rest, parts, middle, grad
):
    bricks, channels = other.shape[0], other.shape[1]
    odd = on_odd()
    for b in range(bricks):
        for g in range(4):
            at = group_at(parts, b * channels, channels, g)
            tile = local[at]
            for n in range(bricks):
                tile = tile + jnp.concatenate([weights[b, g, n]] * (channels // 16), axis=0) * other[n]
            parts[at] = tile
    shift_all(parts, select_y, select_z, middle, shifted, 1)
    x_half = lane_of((channels, TILE)) // 64 == odd
    contract = (((1,), (1,)), ((), ()))
    first = last = None
    for b in range(bricks):
        g, x = jnp.where(x_half, 0, facing[b]), jnp.where(x_half, facing[b], 0)
        one = lax.dot_general(shifted[b], g, contract, preferred_element_type=jnp.float32)
        two = lax.dot_general(x, shifted[b], contract, preferred_element_type=jnp.float32)
        first, last = (one, two) if b == 0 else (first + one, last + two)
    for yz in range(9):
        at = slice(yz * channels, (yz + 1) * channels)
        one, two = first[at], last[:, (8 - yz) * channels : (9 - yz) * channels]
        term = jnp.concatenate([jnp.where(odd == 1, two, one), jnp.where(odd == 1, one, two)], axis=1)
        grad[at, :] = inner[at, :] + term * scale
    grad[9 * channels :, :] = inner[9 * channels :, :]
    place = device_place()
    size = send_far.shape[0]
    for side, far, rest in ((1 - place % 2, send_far, send_rest), (place % 2, keep_far, keep_rest)):
        for k in range(groups):
            at = pl.multiple_of((side * groups + jnp.bitwise_xor(place // 2 % groups, k)) * size, 8)
            if k == groups - 1:
                far[...] = grad[pl.ds(at, size), :]
            else:
                rest[k * size : (k + 1) * size, :] = grad[pl.ds(at, size), :]


def shift_kernel(near, own, select_y, select_z, shifted, parts, middle):
    inner_parts(near, own, parts)
    shift_all(parts, select_y, select_z, middle, shifted, TILES)


def tables_kernel(weight, table_y, table_g):
    channels = weight.shape[1]
    for tx in range(3):
        for yz in range(9):
            at = (slice(tx * channels, (tx + 1) * channels), slice(yz * channels, (yz + 1) * channels))
            table_y[at] = weight[9 * tx + yz].astype(jnp.float32).T.astype(jnp.bfloat16)
            table_g[at] = weight[26 - 9 * tx - yz]


def convolve(table, inner, ends, present, out, swapped):
    bricks, channels = out.shape[1], out.shape[2]
    lower = lane_of((channels, TILE)) < 64
    for b in range(bricks):
        main = jnp.dot(table[...], inner[b], preferred_element_type=jnp.float32)
        side = jnp.dot(table[...], ends(b), preferred_element_type=jnp.float32)
        if swapped:
            side = swap_halves(side)

        def term(t, q):
            rows = slice(t * channels, (t + 1) * channels)
            return main[rows, q * TILE : (q + 1) * TILE] if 0 <= q < TILES else side[rows]

        for q in range(TILES):
            sides = jnp.where(lower, term(0, q), term(0, q - 1)) + jnp.where(lower, term(2, q + 1), term(2, q))
            at = slice(q * TILE, (q + 1) * TILE)
            out[0, b, :, at] = ((term(1, q) + swap_halves(sides)) * present[b : b + 1, at]).astype(jnp.bfloat16)


def forward_kernel(
    near, mine, other, table, inner, ends, present, select_y, select_z, out, more_ends, tiles, parts, middle
):
    odd = on_odd()
    set_ends(near, 1 - odd, mine, other, tiles, parts)
    shift_all(parts, select_y, select_z, middle, more_ends, 1)
    half = lane_of(ends.shape[1:]) // 64 == odd
    convolve(table, inner, lambda b: jnp.where(half, more_ends[b], ends[b]), present, out, False)


def backward_kernel(table, inner, ends, more_ends, present, out):
    half = lane_of(ends.shape[1:]) // 64 == on_odd()
    convolve(table, inner, lambda b: jnp.where(half, ends[b], more_ends[b]), present, out, True)


def unpack_kernel(groups, own, *refs):
    parts, (out, whole, blocks, sem) = refs[:groups], refs[-4:]
    place = device_place()
    where = place // 2 % groups
    size, channels = parts[0].shape[0], blocks.shape[1]
    for k in range(groups):
        at = pl.multiple_of(jnp.bitwise_xor(where, k) * size, 8)
        whole[pl.ds(at, size), :] = parts[k][...]
    half, count = groups * size, 9 * channels

    def write(low, high):
        copies = []

        def send(tap):
            n = len(copies)
            copies.append(pltpu.make_async_copy(blocks.at[n], out.at[tap], sem.at[n]))
            copies[-1].start()

        for lane, base in ((0, 0), (1, 18)):
            for yz in range(low // channels, min(high, count) // channels):
                row = yz * channels - low
                blocks[len(copies)] = whole[row : row + channels, lane * channels : (lane + 1) * channels]
                send(base + yz)
        if high > count:
            for lane in range(2):
                done = 0
                while done < count // 2:
                    at = lane * (count // 2) + done
                    first = at % channels
                    size = min(channels - first, count // 2 - done)
                    row = count - low + done
                    blocks[len(copies), first : first + size, :] = whole[
                        row : row + size, lane * channels : (lane + 1) * channels
                    ]
                    if first + size == channels:
                        send(9 + at // channels)
                    done += size
        for copy in copies:
            copy.wait()

    lower = (place % 2 == 0) == own
    pl.when(lower)(lambda: write(0, half))
    pl.when(jnp.logical_not(lower))(lambda: write(half, 2 * half))


def halo_pairs(spaces, scenes):
    pairs = []
    for scene in range(scenes):
        line = [space * scenes + scene for space in range(spaces)]
        line = line[::-1] if scene % 2 else line
        pairs += list(zip(line, line[1:]))
        if scene ^ 1 < scenes:
            pairs.append((line[-1], line[-1] + (scene ^ 1) - scene))
    return pairs


def exchange(x, bit):
    count = lax.axis_size("space") * lax.axis_size("scene")
    return lax.ppermute(x, AXES, [(i, i ^ bit) for i in range(count)])


def all_sum(send_far, send_rest, keep_far, keep_rest, groups):
    count = lax.axis_size("space") * lax.axis_size("scene")
    size = send_far.shape[0]
    far = keep_far + exchange(send_far, 1)
    rest = keep_rest + exchange(send_rest, 1)
    mine = [rest[k * size : (k + 1) * size] for k in range(groups - 1)] + [far]
    own, got = mine[0], []
    for k in range(1, groups):
        got.append(exchange(mine[k], 2 * k))
    for one in got:
        own = own + one
    bit = 2 * groups
    while bit < count:
        wide = 4 if 4 * bit <= count else 2
        got = []
        for k in range(1, wide):
            got.append(exchange(own, bit * k))
        own = own + got[0]
        if wide == 4:
            own = own + (got[1] + got[2])
        bit *= wide
    chunks = [own]
    for k in range(1, groups):
        chunks.append(exchange(own, 2 * k))
    theirs = []
    for k in range(groups):
        theirs.append(exchange(chunks[k], 1))
    return chunks, theirs


def program(features, cotangent, weight, neighbours, occupancy):
    bricks, channels = features.shape[1], features.shape[2]
    spaces, scenes = lax.axis_size("space"), lax.axis_size("scene")
    scale = 1.0 / math.sqrt(scenes * bricks * spaces * 512)
    groups = 4
    unit = 16 * groups
    rows = -(-(27 * channels // 2) // unit) * unit

    def call(kernel, shapes, inputs, specs, scratch, limit=32 << 20):
        single = not isinstance(shapes, list)
        return pl.pallas_call(
            kernel,
            out_shape=shapes,
            in_specs=specs,
            out_specs=VMEM if single else [VMEM] * len(shapes),
            scratch_shapes=scratch,
            compiler_params=pltpu.CompilerParams(vmem_limit_bytes=limit),
            cost_estimate=pl.CostEstimate(flops=10**8, bytes_accessed=10**6, transcendentals=0),
        )(*inputs)

    def shape(*dims, dtype=jnp.bfloat16):
        return jax.ShapeDtypeStruct(dims, dtype)

    def scratch(*dims, dtype=jnp.bfloat16):
        return pltpu.VMEM(dims, dtype)

    many = bricks * TILES * channels
    parts = [scratch(2 * many, 2 * TILE), scratch(3 * many, 2 * TILE)]
    few = bricks * channels
    ends = [scratch(2 * bricks + 1, channels, TILE), scratch(2 * few, 2 * TILE), scratch(3 * few, 2 * TILE)]
    chosen = shape(2 * TILE, 3 * TILE)
    face, brick = shape(bricks, channels, TILE), shape(bricks + 1, channels, 512)
    one, two, own_x, own_g, present, near = call(
        faces_kernel,
        [face, face, brick, brick, shape(bricks, 512, dtype=jnp.float32), shape(*neighbours.shape, dtype=jnp.int32)],
        tuple(
            pltpu.with_memory_space_constraint(a, pltpu.HBM) for a in (features, cotangent, occupancy, neighbours)
        ),
        [HBM] * 4,
        [
            scratch(*occupancy.shape, dtype=jnp.int32),
            scratch(*features.shape),
            scratch(*features.shape),
            pltpu.SemaphoreType.DMA((4,)),
        ],
        limit=16 << 20,
    )
    forth = halo_pairs(spaces, scenes)
    got_one = lax.ppermute(one, AXES, forth)
    got_two = lax.ppermute(two, AXES, [(b, a) for a, b in forth])
    volume, grads = shape(bricks, 9 * channels, 512), shape(rows, 2 * channels, dtype=jnp.float32)
    shifted = shape(bricks, 9 * channels, TILE)
    inner_x, grad, *select, near_ends, weights = call(
        functools.partial(inner_kernel, scale),
        [volume, grads, chosen, chosen, shape(2 * few, 2 * TILE), shape(bricks, 4, bricks, 16, TILE)],
        (near, own_x, own_g, one),
        [SMEM] + [VMEM] * 3,
        [*parts, scratch(bricks, 3 * channels, 512), scratch(bricks + 1, channels, TILE)],
    )
    far = shape(rows // 2 // groups, 2 * channels, dtype=jnp.float32)
    rest = shape(rows // 2 // groups * (groups - 1), 2 * channels, dtype=jnp.float32)
    ends_one, *halves = call(
        functools.partial(outer_kernel, scale, groups),
        [shifted, far, rest, far, rest],
        (two, got_one, near_ends, weights, grad, *select),
        [VMEM] * 7,
        [*ends[1:], scratch(rows, 2 * channels, dtype=jnp.float32)],
    )
    table = shape(3 * channels, 9 * channels)
    table_y, table_g = call(tables_kernel, [table, table], (weight,), [VMEM], [])
    inner_g = call(shift_kernel, volume, (near, own_g, *select), [SMEM] + [VMEM] * 3, parts)
    out_y, ends_two = call(
        forward_kernel,
        [shape(*features.shape), shifted],
        (near, two, got_two, table_y, inner_x, ends_one, present, *select),
        [SMEM] + [VMEM] * 8,
        ends,
    )
    out_g = call(
        backward_kernel, shape(*cotangent.shape), (table_g, inner_g, ends_one, ends_two, present), [VMEM] * 5, []
    )
    mine, theirs = all_sum(*halves, groups)
    taps = shape(27, channels, channels, dtype=jnp.float32)

    def unpack(own, parts, *before):
        return pl.pallas_call(
            functools.partial(unpack_kernel, groups, own),
            out_shape=taps,
            in_specs=[VMEM] * groups + [HBM] * len(before),
            out_specs=HBM,
            scratch_shapes=[
                scratch(rows // 2, 2 * channels, dtype=jnp.float32),
                scratch(14, channels, channels, dtype=jnp.float32),
                pltpu.SemaphoreType.DMA((14,)),
            ],
            input_output_aliases={groups: 0} if before else {},
            compiler_params=pltpu.CompilerParams(vmem_limit_bytes=16 << 20),
            cost_estimate=pl.CostEstimate(flops=10**6, bytes_accessed=10**6, transcendentals=0),
            name="unpack",
        )(*parts, *before)

    out_w = unpack(True, mine)
    out_w = unpack(False, theirs, out_w)
    return out_y, out_g, out_w


def solution(mesh):
    in_specs = (
        P("scene", "space", None, None),
        P("scene", "space", None, None),
        P(),
        P("scene", "space", None),
        P("scene", "space", None),
    )
    out_specs = (P("scene", "space", None, None), P("scene", "space", None, None), P())
    return jax.shard_map(program, mesh=mesh, in_specs=in_specs, out_specs=out_specs, check_vma=False)
```

```python
import functools
import math

import jax
import jax.numpy as jnp
from jax import lax
from jax.experimental import pallas as pl
from jax.experimental.pallas import tpu as pltpu
from jax.sharding import PartitionSpec as P


TILE = 128
TILES = 4
AXES = ("space", "scene")
SMEM = pl.BlockSpec(memory_space=pltpu.SMEM)
VMEM = pl.BlockSpec(memory_space=pltpu.VMEM)
HBM = pl.BlockSpec(memory_space=pltpu.HBM)
SIDES = [(c, e) for c in (-1, 0, 1) for e in (-1, 0, 1)]


def set_selection(select_y, select_z):
    row = lax.broadcasted_iota(jnp.int32, (TILE, TILE), 0)
    lane = lax.broadcasted_iota(jnp.int32, (TILE, TILE), 1)
    for select, step in ((select_y, 8), (select_z, 1)):
        now = lane // step % 8
        for t in range(3):
            moved = now + t - 1
            wanted = lane + step * (jnp.bitwise_and(moved, 7) - now)
            beyond = jnp.where(moved == jnp.bitwise_and(moved, 7), 0, 1)
            for source in range(2):
                hit = jnp.where(beyond == source, wanted, -1) == row
                select[source * TILE : (source + 1) * TILE, t * TILE : (t + 1) * TILE] = jnp.where(
                    hit, 1.0, 0.0
                ).astype(jnp.bfloat16)


def lane_of(shape):
    return lax.broadcasted_iota(jnp.int32, shape, len(shape) - 1)


def swap_halves(x):
    return pltpu.roll(x, 64, x.ndim - 1)


def grouped(pick, shape):
    lane = lane_of(shape)
    j_high, k_high = lane % 64 >= 32, lane % 8 >= 4
    return (
        pick(0, 0),
        jnp.where(j_high, pick(-1, 0), pick(1, 0)),
        jnp.where(k_high, pick(0, -1), pick(0, 1)),
        jnp.where(
            j_high,
            jnp.where(k_high, pick(-1, -1), pick(-1, 1)),
            jnp.where(k_high, pick(1, -1), pick(1, 1)),
        ),
    )


def group_at(parts, row, channels, g):
    row = parts.shape[0] // 2 * (g // 2) + row
    return slice(row, row + channels), slice(g % 2 * TILE, (g % 2 + 1) * TILE)


def set_groups(parts, row, channels, pick):
    for g, tile in enumerate(grouped(pick, (channels, TILE))):
        parts[group_at(parts, row, channels, g)] = tile


def index_of(near, b, a, c, e, start, none):
    number = near[0, b, 9 * (a + 1) + 3 * (c + 1) + e + 1]
    return jnp.where(number < 0, none, number - start)


def shift_all(parts, select_y, select_z, middle, shifted, tiles):
    bricks, channels, rows = shifted.shape[0], shifted.shape[1] // 9, parts.shape[0] // 2
    for side in range(2):
        moved = jnp.dot(
            parts[side * rows : (side + 1) * rows, :], select_y[...], preferred_element_type=jnp.float32
        ).astype(jnp.bfloat16)
        for t in range(3):
            middle[t * rows : (t + 1) * rows, side * TILE : (side + 1) * TILE] = moved[:, t * TILE : (t + 1) * TILE]
    for ty in range(3):
        moved = jnp.dot(
            middle[ty * rows : (ty + 1) * rows, :], select_z[...], preferred_element_type=jnp.float32
        ).astype(jnp.bfloat16)
        for b in range(bricks):
            for q in range(tiles):
                row = (b * tiles + q) * channels
                for tz in range(3):
                    tap = 3 * ty + tz
                    shifted[b, tap * channels : (tap + 1) * channels, q * TILE : (q + 1) * TILE] = moved[
                        row : row + channels, tz * TILE : (tz + 1) * TILE
                    ]


def inner_parts(near, own, parts):
    bricks, channels = own.shape[0] - 1, own.shape[1]
    base = lax.axis_index("space") * bricks
    for b in range(bricks):
        here = {s: index_of(near, b, 0, *s, base, bricks) for s in SIDES}
        for q in range(TILES):
            set_groups(
                parts, (b * TILES + q) * channels, channels, lambda c, e: own[here[c, e], :, q * TILE : (q + 1) * TILE]
            )


def on_odd():
    return lax.axis_index("scene") % 2


def set_ends(near, up, mine, other, table, parts):
    bricks, channels = mine.shape[0], mine.shape[1]
    for b in range(bricks):
        table[b] = other[b]
        table[bricks + b] = mine[b]
    table[2 * bricks] = jnp.zeros((channels, TILE), jnp.bfloat16)
    start = (lax.axis_index("space") - 1 + up) * bricks

    def place(b, c, e):
        number = near[0, b, 18 * up + 3 * (c + 1) + e + 1]
        at = number - start
        turned = jnp.where(at < bricks, at + bricks, at - bricks)
        return jnp.where(number < 0, 2 * bricks, jnp.where(up == 1, turned, at))

    for b in range(bricks):
        at = {s: place(b, *s) for s in SIDES}
        set_groups(parts, b * channels, channels, lambda c, e: table[at[c, e]])


def prepare_ends(near, up, mine, table, local, weights):
    bricks, channels = mine.shape[0], mine.shape[1]
    for b in range(bricks):
        table[b] = mine[b]
    table[bricks] = jnp.zeros((channels, TILE), jnp.bfloat16)
    start = (lax.axis_index("space") - 1 + up) * bricks
    for b in range(bricks):
        own, other = {}, {}
        for c, e in SIDES:
            number = near[0, b, 18 * up + 3 * (c + 1) + e + 1]
            at = number - start
            at_own, at_other = at - bricks * (1 - up), at - bricks * up
            inside = (number >= 0) & (at_own >= 0) & (at_own < bricks)
            own[c, e] = jnp.where(inside, at_own, bricks)
            other[c, e] = jnp.where(number >= 0, at_other, -1)
        set_groups(local, b * channels, channels, lambda c, e: table[own[c, e]])
        for n in range(bricks):
            flags = grouped(lambda c, e: jnp.where(other[c, e] == n, 1.0, 0.0), weights.shape[3:])
            for g in range(4):
                weights[b, g, n] = jnp.broadcast_to(flags[g], weights.shape[3:]).astype(jnp.bfloat16)


def faces_kernel(features, cotangent, mask, near, one, two, own_x, own_g, present, near_out, *rest):
    (mask_here, *arrays), sems = rest[:3], rest[3]
    bricks, channels = own_x.shape[0] - 1, own_x.shape[1]
    copies = [pltpu.make_async_copy(mask, mask_here, sems.at[0])]
    for b in range(bricks):
        for side, array in enumerate((features, cotangent)):
            copies.append(pltpu.make_async_copy(array.at[0, b], arrays[side].at[0, b], sems.at[len(copies)]))
    copies.append(pltpu.make_async_copy(near, near_out, sems.at[len(copies)]))
    for copy in copies:
        copy.start()
    lower = lane_of((channels, TILE)) < 64
    odd = on_odd() == 1
    for own in (own_x, own_g):
        own[bricks] = jnp.zeros((channels, 512), jnp.bfloat16)
    copies[0].wait()
    present[...] = mask_here[0].astype(jnp.float32)
    for b in range(bricks):
        there = jnp.broadcast_to(present[b : b + 1, :], (channels, 512)).astype(jnp.bfloat16)
        for side, own in enumerate((own_x, own_g)):
            copies[1 + 2 * b + side].wait()
            own[b] = arrays[side][0, b] * there
        x, g = own_x[b].astype(jnp.float32), own_g[b].astype(jnp.float32)
        head = jnp.where(lower, x[:, :TILE], swap_halves(g[:, :TILE])).astype(jnp.bfloat16)
        tail = jnp.where(lower, swap_halves(g[:, 3 * TILE :]), x[:, 3 * TILE :]).astype(jnp.bfloat16)
        one[b] = jnp.where(odd, head, tail)
        two[b] = jnp.where(odd, tail, head)
    copies[-1].wait()


def prepare_ends(near, up, mine, table, local, weights):
    bricks, channels = mine.shape[0], mine.shape[1]
    for b in range(bricks):
        table[b] = mine[b]
    table[bricks] = jnp.zeros((channels, TILE), jnp.bfloat16)
    start = (lax.axis_index("space") - 1 + up) * bricks
    for b in range(bricks):
        own, other = {}, {}
        for c, e in SIDES:
            number = near[0, b, 18 * up + 3 * (c + 1) + e + 1]
            at = number - start
            at_own, at_other = at - bricks * (1 - up), at - bricks * up
            inside = (number >= 0) & (at_own >= 0) & (at_own < bricks)
            own[c, e] = jnp.where(inside, at_own, bricks)
            other[c, e] = jnp.where(number >= 0, at_other, -1)
        set_groups(local, b * channels, channels, lambda c, e: table[own[c, e]])
        for n in range(bricks):
            flags = grouped(lambda c, e: jnp.where(other[c, e] == n, 1.0, 0.0), weights.shape[3:])
            for g in range(4):
                weights[b, g, n] = jnp.broadcast_to(flags[g], weights.shape[3:]).astype(jnp.bfloat16)


def faces_kernel(features, cotangent, mask, near, one, two, own_x, own_g, present, near_out, *rest):
    buffers, sems = rest[:3], rest[3]
    copies = [pltpu.make_async_copy(a, b, sems.at[n]) for n, (a, b) in enumerate(zip((mask, features, cotangent), buffers))]
    copies.append(pltpu.make_async_copy(near, near_out, sems.at[3]))
    for copy in copies:
        copy.start()
    bricks, channels = own_x.shape[0] - 1, own_x.shape[1]
    lower = lane_of((channels, TILE)) < 64
    odd = on_odd() == 1
    copies[0].wait()
    present[...] = buffers[0][0].astype(jnp.float32)
    for side, own in enumerate((own_x, own_g)):
        copies[1 + side].wait()
        for b in range(bricks):
            own[b] = buffers[1 + side][0, b] * jnp.broadcast_to(present[b : b + 1, :], (channels, 512)).astype(
                jnp.bfloat16
            )
        own[bricks] = jnp.zeros((channels, 512), jnp.bfloat16)
    for b in range(bricks):
        x, g = own_x[b].astype(jnp.float32), own_g[b].astype(jnp.float32)
        head = jnp.where(lower, x[:, :TILE], swap_halves(g[:, :TILE])).astype(jnp.bfloat16)
        tail = jnp.where(lower, swap_halves(g[:, 3 * TILE :]), x[:, 3 * TILE :]).astype(jnp.bfloat16)
        one[b] = jnp.where(odd, head, tail)
        two[b] = jnp.where(odd, tail, head)
    copies[3].wait()


def inner_kernel(
    scale, near, own, gradient, mine, shifted, grad, select_y, select_z, local, weights, parts, middle, placed, table
):
    rows, bricks, channels = grad.shape[0], own.shape[0] - 1, own.shape[1]
    set_selection(select_y, select_z)
    prepare_ends(near, on_odd(), mine, table, local, weights)
    inner_parts(near, own, parts)
    lower = lane_of((channels, TILE)) < 64
    zero = jnp.zeros((channels, TILE), jnp.float32)
    for b in range(bricks):
        masked = gradient[b].astype(jnp.float32)
        tile = [zero] + [masked[:, q * TILE : (q + 1) * TILE] for q in range(TILES)] + [zero]
        for q in range(TILES):
            at = slice(q * TILE, (q + 1) * TILE)
            placed[b, :channels, at] = swap_halves(jnp.where(lower, tile[q + 2], tile[q + 1])).astype(jnp.bfloat16)
            placed[b, channels : 2 * channels, at] = swap_halves(jnp.where(lower, tile[q + 1], tile[q])).astype(
                jnp.bfloat16
            )
            placed[b, 2 * channels :, at] = tile[q + 1].astype(jnp.bfloat16)
    shift_all(parts, select_y, select_z, middle, shifted, TILES)
    total = None
    for b in range(bricks):
        term = lax.dot_general(
            shifted[b], placed[b], (((1,), (1,)), ((), ())), preferred_element_type=jnp.float32
        )
        total = term if total is None else total + term
    total = total * scale
    count, half = 9 * channels, 9 * channels // 2
    grad[:count, :] = total[:, : 2 * channels]
    grad[count : count + half, :channels] = total[:half, 2 * channels :]
    grad[count : count + half, channels:] = total[half:, 2 * channels :]
    if rows > count + half:
        grad[count + half :, :] = jnp.zeros((rows - count - half, 2 * channels), jnp.float32)


def device_place():
    return lax.axis_index("space") * lax.axis_size("scene") + lax.axis_index("scene")


def outer_kernel(
    scale, groups, facing, other, local, weights, inner, select_y, select_z,
    shifted, send_far, send_rest, keep_far, keep_rest, parts, middle, grad
):
    bricks, channels = other.shape[0], other.shape[1]
    odd = on_odd()
    for b in range(bricks):
        for g in range(4):
            at = group_at(parts, b * channels, channels, g)
            tile = local[at]
            for n in range(bricks):
                tile = tile + jnp.concatenate([weights[b, g, n]] * (channels // 16), axis=0) * other[n]
            parts[at] = tile
    shift_all(parts, select_y, select_z, middle, shifted, 1)
    x_half = lane_of((channels, TILE)) // 64 == odd
    contract = (((1,), (1,)), ((), ()))
    first = last = None
    for b in range(bricks):
        g, x = jnp.where(x_half, 0, facing[b]), jnp.where(x_half, facing[b], 0)
        one = lax.dot_general(shifted[b], g, contract, preferred_element_type=jnp.float32)
        two = lax.dot_general(x, shifted[b], contract, preferred_element_type=jnp.float32)
        first, last = (one, two) if b == 0 else (first + one, last + two)
    for yz in range(9):
        at = slice(yz * channels, (yz + 1) * channels)
        one, two = first[at], last[:, (8 - yz) * channels : (9 - yz) * channels]
        term = jnp.concatenate([jnp.where(odd == 1, two, one), jnp.where(odd == 1, one, two)], axis=1)
        grad[at, :] = inner[at, :] + term * scale
    grad[9 * channels :, :] = inner[9 * channels :, :]
    place = device_place()
    size = send_far.shape[0]
    for side, far, rest in ((1 - place % 2, send_far, send_rest), (place % 2, keep_far, keep_rest)):
        for k in range(groups):
            at = pl.multiple_of((side * groups + jnp.bitwise_xor(place // 2 % groups, k)) * size, 8)
            if k == groups - 1:
                far[...] = grad[pl.ds(at, size), :]
            else:
                rest[k * size : (k + 1) * size, :] = grad[pl.ds(at, size), :]


def shift_kernel(near, own, select_y, select_z, shifted, parts, middle):
    inner_parts(near, own, parts)
    shift_all(parts, select_y, select_z, middle, shifted, TILES)


def tables_kernel(weight, table_y, table_g):
    channels = weight.shape[1]
    for tx in range(3):
        for yz in range(9):
            at = (slice(tx * channels, (tx + 1) * channels), slice(yz * channels, (yz + 1) * channels))
            table_y[at] = weight[9 * tx + yz].astype(jnp.float32).T.astype(jnp.bfloat16)
            table_g[at] = weight[26 - 9 * tx - yz]


def convolve(table, inner, ends, present, out, swapped):
    bricks, channels = out.shape[1], out.shape[2]
    lower = lane_of((channels, TILE)) < 64
    for b in range(bricks):
        main = jnp.dot(table[...], inner[b], preferred_element_type=jnp.float32)
        side = jnp.dot(table[...], ends(b), preferred_element_type=jnp.float32)
        if swapped:
            side = swap_halves(side)

        def term(t, q):
            rows = slice(t * channels, (t + 1) * channels)
            return main[rows, q * TILE : (q + 1) * TILE] if 0 <= q < TILES else side[rows]

        for q in range(TILES):
            sides = jnp.where(lower, term(0, q), term(0, q - 1)) + jnp.where(lower, term(2, q + 1), term(2, q))
            at = slice(q * TILE, (q + 1) * TILE)
            out[0, b, :, at] = ((term(1, q) + swap_halves(sides)) * present[b : b + 1, at]).astype(jnp.bfloat16)


def forward_kernel(
    near, mine, other, table, inner, ends, present, select_y, select_z, out, more_ends, tiles, parts, middle
):
    odd = on_odd()
    set_ends(near, 1 - odd, mine, other, tiles, parts)
    shift_all(parts, select_y, select_z, middle, more_ends, 1)
    half = lane_of(ends.shape[1:]) // 64 == odd
    convolve(table, inner, lambda b: jnp.where(half, more_ends[b], ends[b]), present, out, False)


def backward_kernel(table, inner, ends, more_ends, present, out):
    half = lane_of(ends.shape[1:]) // 64 == on_odd()
    convolve(table, inner, lambda b: jnp.where(half, ends[b], more_ends[b]), present, out, True)


def unpack_kernel(groups, own, *refs):
    parts, (out, whole, blocks, sem) = refs[:groups], refs[-4:]
    place = device_place()
    where = place // 2 % groups
    size, channels = parts[0].shape[0], blocks.shape[1]
    for k in range(groups):
        at = pl.multiple_of(jnp.bitwise_xor(where, k) * size, 8)
        whole[pl.ds(at, size), :] = parts[k][...]
    half, count = groups * size, 9 * channels

    def write(low, high):
        copies = []

        def send(tap):
            n = len(copies)
            copies.append(pltpu.make_async_copy(blocks.at[n], out.at[tap], sem.at[n]))
            copies[-1].start()

        for lane, base in ((0, 0), (1, 18)):
            for yz in range(low // channels, min(high, count) // channels):
                row = yz * channels - low
                blocks[len(copies)] = whole[row : row + channels, lane * channels : (lane + 1) * channels]
                send(base + yz)
        if high > count:
            for lane in range(2):
                done = 0
                while done < count // 2:
                    at = lane * (count // 2) + done
                    first = at % channels
                    size = min(channels - first, count // 2 - done)
                    row = count - low + done
                    blocks[len(copies), first : first + size, :] = whole[
                        row : row + size, lane * channels : (lane + 1) * channels
                    ]
                    if first + size == channels:
                        send(9 + at // channels)
                    done += size
        for copy in copies:
            copy.wait()

    lower = (place % 2 == 0) == own
    pl.when(lower)(lambda: write(0, half))
    pl.when(jnp.logical_not(lower))(lambda: write(half, 2 * half))


def halo_pairs(spaces, scenes):
    pairs = []
    for scene in range(scenes):
        line = [space * scenes + scene for space in range(spaces)]
        line = line[::-1] if scene % 2 else line
        pairs += list(zip(line, line[1:]))
        if scene ^ 1 < scenes:
            pairs.append((line[-1], line[-1] + (scene ^ 1) - scene))
    return pairs


def exchange(x, bit):
    count = lax.axis_size("space") * lax.axis_size("scene")
    return lax.ppermute(x, AXES, [(i, i ^ bit) for i in range(count)])


def all_sum(send_far, send_rest, keep_far, keep_rest, groups):
    count = lax.axis_size("space") * lax.axis_size("scene")
    size = send_far.shape[0]
    far = keep_far + exchange(send_far, 1)
    rest = keep_rest + exchange(send_rest, 1)
    mine = [rest[k * size : (k + 1) * size] for k in range(groups - 1)] + [far]
    own, got = mine[0], []
    for k in range(1, groups):
        got.append(exchange(mine[k], 2 * k))
    for one in got:
        own = own + one
    bit = 2 * groups
    while bit < count:
        wide = 4 if 4 * bit <= count else 2
        got = []
        for k in range(1, wide):
            got.append(exchange(own, bit * k))
        own = own + got[0]
        if wide == 4:
            own = own + (got[1] + got[2])
        bit *= wide
    chunks = [own]
    for k in range(1, groups):
        chunks.append(exchange(own, 2 * k))
    theirs = []
    for k in range(groups):
        theirs.append(exchange(chunks[k], 1))
    return chunks, theirs


def program(features, cotangent, weight, neighbours, occupancy):
    bricks, channels = features.shape[1], features.shape[2]
    spaces, scenes = lax.axis_size("space"), lax.axis_size("scene")
    scale = 1.0 / math.sqrt(scenes * bricks * spaces * 512)
    groups = 4
    unit = 16 * groups
    rows = -(-(27 * channels // 2) // unit) * unit

    def call(kernel, shapes, inputs, specs, scratch, limit=32 << 20):
        single = not isinstance(shapes, list)
        return pl.pallas_call(
            kernel,
            out_shape=shapes,
            in_specs=specs,
            out_specs=VMEM if single else [VMEM] * len(shapes),
            scratch_shapes=scratch,
            compiler_params=pltpu.CompilerParams(vmem_limit_bytes=limit),
            cost_estimate=pl.CostEstimate(flops=10**8, bytes_accessed=10**6, transcendentals=0),
        )(*inputs)

    def shape(*dims, dtype=jnp.bfloat16):
        return jax.ShapeDtypeStruct(dims, dtype)

    def scratch(*dims, dtype=jnp.bfloat16):
        return pltpu.VMEM(dims, dtype)

    many = bricks * TILES * channels
    parts = [scratch(2 * many, 2 * TILE), scratch(3 * many, 2 * TILE)]
    few = bricks * channels
    ends = [scratch(2 * bricks + 1, channels, TILE), scratch(2 * few, 2 * TILE), scratch(3 * few, 2 * TILE)]
    chosen = shape(2 * TILE, 3 * TILE)
    face, brick = shape(bricks, channels, TILE), shape(bricks + 1, channels, 512)
    one, two, own_x, own_g, present, near = call(
        faces_kernel,
        [face, face, brick, brick, shape(bricks, 512, dtype=jnp.float32), shape(*neighbours.shape, dtype=jnp.int32)],
        tuple(
            pltpu.with_memory_space_constraint(a, pltpu.HBM) for a in (features, cotangent, occupancy, neighbours)
        ),
        [HBM] * 4,
        [
            scratch(*occupancy.shape, dtype=jnp.int32),
            scratch(*features.shape),
            scratch(*features.shape),
            pltpu.SemaphoreType.DMA((2 * bricks + 2,)),
        ],
        limit=16 << 20,
    )
    forth = halo_pairs(spaces, scenes)
    got_one = lax.ppermute(one, AXES, forth)
    got_two = lax.ppermute(two, AXES, [(b, a) for a, b in forth])
    volume, grads = shape(bricks, 9 * channels, 512), shape(rows, 2 * channels, dtype=jnp.float32)
    shifted = shape(bricks, 9 * channels, TILE)
    inner_x, grad, *select, near_ends, weights = call(
        functools.partial(inner_kernel, scale),
        [volume, grads, chosen, chosen, shape(2 * few, 2 * TILE), shape(bricks, 4, bricks, 16, TILE)],
        (near, own_x, own_g, one),
        [SMEM] + [VMEM] * 3,
        [*parts, scratch(bricks, 3 * channels, 512), scratch(bricks + 1, channels, TILE)],
    )
    far = shape(rows // 2 // groups, 2 * channels, dtype=jnp.float32)
    rest = shape(rows // 2 // groups * (groups - 1), 2 * channels, dtype=jnp.float32)
    ends_one, *halves = call(
        functools.partial(outer_kernel, scale, groups),
        [shifted, far, rest, far, rest],
        (two, got_one, near_ends, weights, grad, *select),
        [VMEM] * 7,
        [*ends[1:], scratch(rows, 2 * channels, dtype=jnp.float32)],
    )
    table = shape(3 * channels, 9 * channels)
    table_y, table_g = call(tables_kernel, [table, table], (weight,), [VMEM], [])
    inner_g = call(shift_kernel, volume, (near, own_g, *select), [SMEM] + [VMEM] * 3, parts)
    out_y, ends_two = call(
        forward_kernel,
        [shape(*features.shape), shifted],
        (near, two, got_two, table_y, inner_x, ends_one, present, *select),
        [SMEM] + [VMEM] * 8,
        ends,
    )
    out_g = call(
        backward_kernel, shape(*cotangent.shape), (table_g, inner_g, ends_one, ends_two, present), [VMEM] * 5, []
    )
    mine, theirs = all_sum(*halves, groups)
    taps = shape(27, channels, channels, dtype=jnp.float32)

    def unpack(own, parts, *before):
        return pl.pallas_call(
            functools.partial(unpack_kernel, groups, own),
            out_shape=taps,
            in_specs=[VMEM] * groups + [HBM] * len(before),
            out_specs=HBM,
            scratch_shapes=[
                scratch(rows // 2, 2 * channels, dtype=jnp.float32),
                scratch(14, channels, channels, dtype=jnp.float32),
                pltpu.SemaphoreType.DMA((14,)),
            ],
            input_output_aliases={groups: 0} if before else {},
            compiler_params=pltpu.CompilerParams(vmem_limit_bytes=16 << 20),
            cost_estimate=pl.CostEstimate(flops=10**6, bytes_accessed=10**6, transcendentals=0),
            name="unpack",
        )(*parts, *before)

    out_w = unpack(True, mine)
    out_w = unpack(False, theirs, out_w)
    return out_y, out_g, out_w


def solution(mesh):
    in_specs = (
        P("scene", "space", None, None),
        P("scene", "space", None, None),
        P(),
        P("scene", "space", None),
        P("scene", "space", None),
    )
    out_specs = (P("scene", "space", None, None), P("scene", "space", None, None), P())
    return jax.shard_map(program, mesh=mesh, in_specs=in_specs, out_specs=out_specs, check_vma=False)
```

```python
import functools
import math

import jax
import jax.numpy as jnp
from jax import lax
from jax.experimental import pallas as pl
from jax.experimental.pallas import tpu as pltpu
from jax.sharding import PartitionSpec as P


TILE = 128
TILES = 4
AXES = ("space", "scene")
SMEM = pl.BlockSpec(memory_space=pltpu.SMEM)
VMEM = pl.BlockSpec(memory_space=pltpu.VMEM)
HBM = pl.BlockSpec(memory_space=pltpu.HBM)
SIDES = [(c, e) for c in (-1, 0, 1) for e in (-1, 0, 1)]


def set_selection(select_y, select_z):
    row = lax.broadcasted_iota(jnp.int32, (TILE, TILE), 0)
    lane = lax.broadcasted_iota(jnp.int32, (TILE, TILE), 1)
    for select, step in ((select_y, 8), (select_z, 1)):
        now = lane // step % 8
        for t in range(3):
            moved = now + t - 1
            wanted = lane + step * (jnp.bitwise_and(moved, 7) - now)
            beyond = jnp.where(moved == jnp.bitwise_and(moved, 7), 0, 1)
            for source in range(2):
                hit = jnp.where(beyond == source, wanted, -1) == row
                select[source * TILE : (source + 1) * TILE, t * TILE : (t + 1) * TILE] = jnp.where(
                    hit, 1.0, 0.0
                ).astype(jnp.bfloat16)


def lane_of(shape):
    return lax.broadcasted_iota(jnp.int32, shape, len(shape) - 1)


def swap_halves(x):
    return pltpu.roll(x, 64, x.ndim - 1)


def grouped(pick, shape):
    lane = lane_of(shape)
    j_high, k_high = lane % 64 >= 32, lane % 8 >= 4
    return (
        pick(0, 0),
        jnp.where(j_high, pick(-1, 0), pick(1, 0)),
        jnp.where(k_high, pick(0, -1), pick(0, 1)),
        jnp.where(
            j_high,
            jnp.where(k_high, pick(-1, -1), pick(-1, 1)),
            jnp.where(k_high, pick(1, -1), pick(1, 1)),
        ),
    )


def group_at(parts, row, channels, g):
    row = parts.shape[0] // 2 * (g // 2) + row
    return slice(row, row + channels), slice(g % 2 * TILE, (g % 2 + 1) * TILE)


def set_groups(parts, row, channels, pick):
    for g, tile in enumerate(grouped(pick, (channels, TILE))):
        parts[group_at(parts, row, channels, g)] = tile


def index_of(near, b, a, c, e, start, none):
    number = near[0, b, 9 * (a + 1) + 3 * (c + 1) + e + 1]
    return jnp.where(number < 0, none, number - start)


def shift_all(parts, select_y, select_z, middle, shifted, tiles):
    bricks, channels, rows = shifted.shape[0], shifted.shape[1] // 9, parts.shape[0] // 2
    for side in range(2):
        moved = jnp.dot(
            parts[side * rows : (side + 1) * rows, :], select_y[...], preferred_element_type=jnp.float32
        ).astype(jnp.bfloat16)
        for t in range(3):
            middle[t * rows : (t + 1) * rows, side * TILE : (side + 1) * TILE] = moved[:, t * TILE : (t + 1) * TILE]
    for ty in range(3):
        moved = jnp.dot(
            middle[ty * rows : (ty + 1) * rows, :], select_z[...], preferred_element_type=jnp.float32
        ).astype(jnp.bfloat16)
        for b in range(bricks):
            for q in range(tiles):
                row = (b * tiles + q) * channels
                for tz in range(3):
                    tap = 3 * ty + tz
                    shifted[b, tap * channels : (tap + 1) * channels, q * TILE : (q + 1) * TILE] = moved[
                        row : row + channels, tz * TILE : (tz + 1) * TILE
                    ]


def inner_parts(near, own, parts):
    bricks, channels = own.shape[0] - 1, own.shape[1]
    base = lax.axis_index("space") * bricks
    for b in range(bricks):
        here = {s: index_of(near, b, 0, *s, base, bricks) for s in SIDES}
        for q in range(TILES):
            set_groups(
                parts, (b * TILES + q) * channels, channels, lambda c, e: own[here[c, e], :, q * TILE : (q + 1) * TILE]
            )


def on_odd():
    return lax.axis_index("scene") % 2


def set_ends(near, up, mine, other, table, parts):
    bricks, channels = mine.shape[0], mine.shape[1]
    for b in range(bricks):
        table[b] = other[b]
        table[bricks + b] = mine[b]
    table[2 * bricks] = jnp.zeros((channels, TILE), jnp.bfloat16)
    start = (lax.axis_index("space") - 1 + up) * bricks

    def place(b, c, e):
        number = near[0, b, 18 * up + 3 * (c + 1) + e + 1]
        at = number - start
        turned = jnp.where(at < bricks, at + bricks, at - bricks)
        return jnp.where(number < 0, 2 * bricks, jnp.where(up == 1, turned, at))

    for b in range(bricks):
        at = {s: place(b, *s) for s in SIDES}
        set_groups(parts, b * channels, channels, lambda c, e: table[at[c, e]])


def prepare_ends(near, up, mine, table, local, weights):
    bricks, channels = mine.shape[0], mine.shape[1]
    for b in range(bricks):
        table[b] = mine[b]
    table[bricks] = jnp.zeros((channels, TILE), jnp.bfloat16)
    start = (lax.axis_index("space") - 1 + up) * bricks
    for b in range(bricks):
        own, other = {}, {}
        for c, e in SIDES:
            number = near[0, b, 18 * up + 3 * (c + 1) + e + 1]
            at = number - start
            at_own, at_other = at - bricks * (1 - up), at - bricks * up
            inside = (number >= 0) & (at_own >= 0) & (at_own < bricks)
            own[c, e] = jnp.where(inside, at_own, bricks)
            other[c, e] = jnp.where(number >= 0, at_other, -1)
        set_groups(local, b * channels, channels, lambda c, e: table[own[c, e]])
        for n in range(bricks):
            flags = grouped(lambda c, e: jnp.where(other[c, e] == n, 1.0, 0.0), weights.shape[3:])
            for g in range(4):
                weights[b, g, n] = jnp.broadcast_to(flags[g], weights.shape[3:]).astype(jnp.bfloat16)


def faces_kernel(features, cotangent, mask, near, one, two, own_x, own_g, present, near_out, *rest):
    (mask_here, *arrays), sems = rest[:3], rest[3]
    bricks, channels = own_x.shape[0] - 1, own_x.shape[1]
    copies = [pltpu.make_async_copy(mask, mask_here, sems.at[0])]
    for b in range(bricks):
        for side, array in enumerate((features, cotangent)):
            copies.append(pltpu.make_async_copy(array.at[0, b], arrays[side].at[0, b], sems.at[len(copies)]))
    copies.append(pltpu.make_async_copy(near, near_out, sems.at[len(copies)]))
    for copy in copies:
        copy.start()
    lower = lane_of((channels, TILE)) < 64
    odd = on_odd() == 1
    for own in (own_x, own_g):
        own[bricks] = jnp.zeros((channels, 512), jnp.bfloat16)
    copies[0].wait()
    present[...] = mask_here[0].astype(jnp.float32)
    for b in range(bricks):
        there = jnp.broadcast_to(present[b : b + 1, :], (channels, 512)).astype(jnp.bfloat16)
        for side, own in enumerate((own_x, own_g)):
            copies[1 + 2 * b + side].wait()
            own[b] = arrays[side][0, b] * there
        x, g = own_x[b].astype(jnp.float32), own_g[b].astype(jnp.float32)
        head = jnp.where(lower, x[:, :TILE], swap_halves(g[:, :TILE])).astype(jnp.bfloat16)
        tail = jnp.where(lower, swap_halves(g[:, 3 * TILE :]), x[:, 3 * TILE :]).astype(jnp.bfloat16)
        one[b] = jnp.where(odd, head, tail)
        two[b] = jnp.where(odd, tail, head)
    copies[-1].wait()


def prepare_ends(near, up, mine, table, local, weights):
    bricks, channels = mine.shape[0], mine.shape[1]
    for b in range(bricks):
        table[b] = mine[b]
    table[bricks] = jnp.zeros((channels, TILE), jnp.bfloat16)
    start = (lax.axis_index("space") - 1 + up) * bricks
    for b in range(bricks):
        own, other = {}, {}
        for c, e in SIDES:
            number = near[0, b, 18 * up + 3 * (c + 1) + e + 1]
            at = number - start
            at_own, at_other = at - bricks * (1 - up), at - bricks * up
            inside = (number >= 0) & (at_own >= 0) & (at_own < bricks)
            own[c, e] = jnp.where(inside, at_own, bricks)
            other[c, e] = jnp.where(number >= 0, at_other, -1)
        set_groups(local, b * channels, channels, lambda c, e: table[own[c, e]])
        for n in range(bricks):
            flags = grouped(lambda c, e: jnp.where(other[c, e] == n, 1.0, 0.0), weights.shape[3:])
            for g in range(4):
                weights[b, g, n] = jnp.broadcast_to(flags[g], weights.shape[3:]).astype(jnp.bfloat16)


def faces_kernel(features, cotangent, mask, near, one, two, own_x, own_g, present, near_out, *rest):
    buffers, sems = rest[:3], rest[3]
    copies = [pltpu.make_async_copy(a, b, sems.at[n]) for n, (a, b) in enumerate(zip((mask, features, cotangent), buffers))]
    copies.append(pltpu.make_async_copy(near, near_out, sems.at[3]))
    for copy in copies:
        copy.start()
    bricks, channels = own_x.shape[0] - 1, own_x.shape[1]
    lower = lane_of((channels, TILE)) < 64
    odd = on_odd() == 1
    copies[0].wait()
    present[...] = buffers[0][0].astype(jnp.float32)
    for side, own in enumerate((own_x, own_g)):
        copies[1 + side].wait()
        for b in range(bricks):
            own[b] = buffers[1 + side][0, b] * jnp.broadcast_to(present[b : b + 1, :], (channels, 512)).astype(
                jnp.bfloat16
            )
        own[bricks] = jnp.zeros((channels, 512), jnp.bfloat16)
    for b in range(bricks):
        x, g = own_x[b].astype(jnp.float32), own_g[b].astype(jnp.float32)
        head = jnp.where(lower, x[:, :TILE], swap_halves(g[:, :TILE])).astype(jnp.bfloat16)
        tail = jnp.where(lower, swap_halves(g[:, 3 * TILE :]), x[:, 3 * TILE :]).astype(jnp.bfloat16)
        one[b] = jnp.where(odd, head, tail)
        two[b] = jnp.where(odd, tail, head)
    copies[3].wait()


def inner_kernel(
    scale, near, own, gradient, mine, shifted, grad, select_y, select_z, local, weights, parts, middle, placed, table
):
    rows, bricks, channels = grad.shape[0], own.shape[0] - 1, own.shape[1]
    set_selection(select_y, select_z)
    prepare_ends(near, on_odd(), mine, table, local, weights)
    inner_parts(near, own, parts)
    lower = lane_of((channels, TILE)) < 64
    zero = jnp.zeros((channels, TILE), jnp.float32)
    for b in range(bricks):
        masked = gradient[b].astype(jnp.float32)
        tile = [zero] + [masked[:, q * TILE : (q + 1) * TILE] for q in range(TILES)] + [zero]
        for q in range(TILES):
            at = slice(q * TILE, (q + 1) * TILE)
            placed[b, :channels, at] = swap_halves(jnp.where(lower, tile[q + 2], tile[q + 1])).astype(jnp.bfloat16)
            placed[b, channels : 2 * channels, at] = swap_halves(jnp.where(lower, tile[q + 1], tile[q])).astype(
                jnp.bfloat16
            )
            placed[b, 2 * channels :, at] = tile[q + 1].astype(jnp.bfloat16)
    shift_all(parts, select_y, select_z, middle, shifted, TILES)
    total = None
    for b in range(bricks):
        term = lax.dot_general(
            shifted[b], placed[b], (((1,), (1,)), ((), ())), preferred_element_type=jnp.float32
        )
        total = term if total is None else total + term
    total = total * scale
    count, half = 9 * channels, 9 * channels // 2
    grad[:count, :] = total[:, : 2 * channels]
    grad[count : count + half, :channels] = total[:half, 2 * channels :]
    grad[count : count + half, channels:] = total[half:, 2 * channels :]
    if rows > count + half:
        grad[count + half :, :] = jnp.zeros((rows - count - half, 2 * channels), jnp.float32)


def device_place():
    return lax.axis_index("space") * lax.axis_size("scene") + lax.axis_index("scene")


def device_half():
    place = device_place()
    return jnp.bitwise_xor(place, place // 2) % 2


def outer_kernel(
    scale, groups, facing, other, local, weights, inner, select_y, select_z,
    shifted, send_far, send_rest, keep_far, keep_rest, parts, middle, grad
):
    bricks, channels = other.shape[0], other.shape[1]
    odd = on_odd()
    for b in range(bricks):
        for g in range(4):
            at = group_at(parts, b * channels, channels, g)
            tile = local[at]
            for n in range(bricks):
                tile = tile + jnp.concatenate([weights[b, g, n]] * (channels // 16), axis=0) * other[n]
            parts[at] = tile
    shift_all(parts, select_y, select_z, middle, shifted, 1)
    x_half = lane_of((channels, TILE)) // 64 == odd
    contract = (((1,), (1,)), ((), ()))
    first = last = None
    for b in range(bricks):
        g, x = jnp.where(x_half, 0, facing[b]), jnp.where(x_half, facing[b], 0)
        one = lax.dot_general(shifted[b], g, contract, preferred_element_type=jnp.float32)
        two = lax.dot_general(x, shifted[b], contract, preferred_element_type=jnp.float32)
        first, last = (one, two) if b == 0 else (first + one, last + two)
    for yz in range(9):
        at = slice(yz * channels, (yz + 1) * channels)
        one, two = first[at], last[:, (8 - yz) * channels : (9 - yz) * channels]
        term = jnp.concatenate([jnp.where(odd == 1, two, one), jnp.where(odd == 1, one, two)], axis=1)
        grad[at, :] = inner[at, :] + term * scale
    grad[9 * channels :, :] = inner[9 * channels :, :]
    place = device_place()
    size = send_far.shape[0]
    for side, far, rest in ((1 - device_half(), send_far, send_rest), (device_half(), keep_far, keep_rest)):
        for k in range(groups):
            at = pl.multiple_of((side * groups + jnp.bitwise_xor(place // 2 % groups, k)) * size, 8)
            if k == groups - 1:
                far[...] = grad[pl.ds(at, size), :]
            else:
                rest[k * size : (k + 1) * size, :] = grad[pl.ds(at, size), :]


def shift_kernel(near, own, select_y, select_z, shifted, parts, middle):
    inner_parts(near, own, parts)
    shift_all(parts, select_y, select_z, middle, shifted, TILES)


def tables_kernel(weight, table_y, table_g):
    channels = weight.shape[1]
    for tx in range(3):
        for yz in range(9):
            at = (slice(tx * channels, (tx + 1) * channels), slice(yz * channels, (yz + 1) * channels))
            table_y[at] = weight[9 * tx + yz].astype(jnp.float32).T.astype(jnp.bfloat16)
            table_g[at] = weight[26 - 9 * tx - yz]


def convolve(table, inner, ends, present, out, swapped):
    bricks, channels = out.shape[1], out.shape[2]
    lower = lane_of((channels, TILE)) < 64
    for b in range(bricks):
        main = jnp.dot(table[...], inner[b], preferred_element_type=jnp.float32)
        side = jnp.dot(table[...], ends(b), preferred_element_type=jnp.float32)
        if swapped:
            side = swap_halves(side)

        def term(t, q):
            rows = slice(t * channels, (t + 1) * channels)
            return main[rows, q * TILE : (q + 1) * TILE] if 0 <= q < TILES else side[rows]

        for q in range(TILES):
            sides = jnp.where(lower, term(0, q), term(0, q - 1)) + jnp.where(lower, term(2, q + 1), term(2, q))
            at = slice(q * TILE, (q + 1) * TILE)
            out[0, b, :, at] = ((term(1, q) + swap_halves(sides)) * present[b : b + 1, at]).astype(jnp.bfloat16)


def forward_kernel(
    near, mine, other, table, inner, ends, present, select_y, select_z, out, more_ends, tiles, parts, middle
):
    odd = on_odd()
    set_ends(near, 1 - odd, mine, other, tiles, parts)
    shift_all(parts, select_y, select_z, middle, more_ends, 1)
    half = lane_of(ends.shape[1:]) // 64 == odd
    convolve(table, inner, lambda b: jnp.where(half, more_ends[b], ends[b]), present, out, False)


def backward_kernel(table, inner, ends, more_ends, present, out):
    half = lane_of(ends.shape[1:]) // 64 == on_odd()
    convolve(table, inner, lambda b: jnp.where(half, ends[b], more_ends[b]), present, out, True)


def unpack_kernel(groups, own, *refs):
    parts, (out, whole, blocks, sem) = refs[:groups], refs[-4:]
    place = device_place()
    where = place // 2 % groups
    size, channels = parts[0].shape[0], blocks.shape[1]
    for k in range(groups):
        at = pl.multiple_of(jnp.bitwise_xor(where, k) * size, 8)
        whole[pl.ds(at, size), :] = parts[k][...]
    half, count = groups * size, 9 * channels

    def write(low, high):
        copies = []

        def send(tap):
            n = len(copies)
            copies.append(pltpu.make_async_copy(blocks.at[n], out.at[tap], sem.at[n]))
            copies[-1].start()

        for lane, base in ((0, 0), (1, 18)):
            for yz in range(low // channels, min(high, count) // channels):
                row = yz * channels - low
                blocks[len(copies)] = whole[row : row + channels, lane * channels : (lane + 1) * channels]
                send(base + yz)
        if high > count:
            for lane in range(2):
                done = 0
                while done < count // 2:
                    at = lane * (count // 2) + done
                    first = at % channels
                    size = min(channels - first, count // 2 - done)
                    row = count - low + done
                    blocks[len(copies), first : first + size, :] = whole[
                        row : row + size, lane * channels : (lane + 1) * channels
                    ]
                    if first + size == channels:
                        send(9 + at // channels)
                    done += size
        for copy in copies:
            copy.wait()

    lower = (device_half() == 0) == own
    pl.when(lower)(lambda: write(0, half))
    pl.when(jnp.logical_not(lower))(lambda: write(half, 2 * half))


def halo_pairs(spaces, scenes):
    pairs = []
    for scene in range(scenes):
        line = [space * scenes + scene for space in range(spaces)]
        line = line[::-1] if scene % 2 else line
        pairs += list(zip(line, line[1:]))
        if scene ^ 1 < scenes:
            pairs.append((line[-1], line[-1] + (scene ^ 1) - scene))
    return pairs


def exchange(x, bit):
    count = lax.axis_size("space") * lax.axis_size("scene")
    return lax.ppermute(x, AXES, [(i, i ^ bit) for i in range(count)])


def all_sum(send_far, send_rest, keep_far, keep_rest, groups):
    count = lax.axis_size("space") * lax.axis_size("scene")
    size = send_far.shape[0]
    far = keep_far + exchange(send_far, 1)
    rest = keep_rest + exchange(send_rest, 1)
    mine = [rest[k * size : (k + 1) * size] for k in range(groups - 1)] + [far]
    own, got = mine[0], []
    for k in range(1, groups):
        got.append(exchange(mine[k], 2 * k + k % 2))
    for one in got:
        own = own + one
    bit = 2 * groups
    while bit < count:
        wide = 4 if 4 * bit <= count else 2
        got = []
        for k in range(1, wide):
            got.append(exchange(own, bit * k))
        own = own + got[0]
        if wide == 4:
            own = own + (got[1] + got[2])
        bit *= wide
    chunks = [own]
    for k in range(1, groups):
        chunks.append(exchange(own, 2 * k + k % 2))
    theirs = []
    for k in range(groups):
        theirs.append(exchange(chunks[k], 1))
    return chunks, theirs


def program(features, cotangent, weight, neighbours, occupancy):
    bricks, channels = features.shape[1], features.shape[2]
    spaces, scenes = lax.axis_size("space"), lax.axis_size("scene")
    scale = 1.0 / math.sqrt(scenes * bricks * spaces * 512)
    groups = 4
    unit = 16 * groups
    rows = -(-(27 * channels // 2) // unit) * unit

    def call(kernel, shapes, inputs, specs, scratch, limit=32 << 20):
        single = not isinstance(shapes, list)
        return pl.pallas_call(
            kernel,
            out_shape=shapes,
            in_specs=specs,
            out_specs=VMEM if single else [VMEM] * len(shapes),
            scratch_shapes=scratch,
            compiler_params=pltpu.CompilerParams(vmem_limit_bytes=limit),
            cost_estimate=pl.CostEstimate(flops=10**8, bytes_accessed=10**6, transcendentals=0),
        )(*inputs)

    def shape(*dims, dtype=jnp.bfloat16):
        return jax.ShapeDtypeStruct(dims, dtype)

    def scratch(*dims, dtype=jnp.bfloat16):
        return pltpu.VMEM(dims, dtype)

    many = bricks * TILES * channels
    parts = [scratch(2 * many, 2 * TILE), scratch(3 * many, 2 * TILE)]
    few = bricks * channels
    ends = [scratch(2 * bricks + 1, channels, TILE), scratch(2 * few, 2 * TILE), scratch(3 * few, 2 * TILE)]
    chosen = shape(2 * TILE, 3 * TILE)
    face, brick = shape(bricks, channels, TILE), shape(bricks + 1, channels, 512)
    one, two, own_x, own_g, present, near = call(
        faces_kernel,
        [face, face, brick, brick, shape(bricks, 512, dtype=jnp.float32), shape(*neighbours.shape, dtype=jnp.int32)],
        tuple(
            pltpu.with_memory_space_constraint(a, pltpu.HBM) for a in (features, cotangent, occupancy, neighbours)
        ),
        [HBM] * 4,
        [
            scratch(*occupancy.shape, dtype=jnp.int32),
            scratch(*features.shape),
            scratch(*features.shape),
            pltpu.SemaphoreType.DMA((2 * bricks + 2,)),
        ],
        limit=16 << 20,
    )
    forth = halo_pairs(spaces, scenes)
    got_one = lax.ppermute(one, AXES, forth)
    got_two = lax.ppermute(two, AXES, [(b, a) for a, b in forth])
    volume, grads = shape(bricks, 9 * channels, 512), shape(rows, 2 * channels, dtype=jnp.float32)
    shifted = shape(bricks, 9 * channels, TILE)
    inner_x, grad, *select, near_ends, weights = call(
        functools.partial(inner_kernel, scale),
        [volume, grads, chosen, chosen, shape(2 * few, 2 * TILE), shape(bricks, 4, bricks, 16, TILE)],
        (near, own_x, own_g, one),
        [SMEM] + [VMEM] * 3,
        [*parts, scratch(bricks, 3 * channels, 512), scratch(bricks + 1, channels, TILE)],
    )
    far = shape(rows // 2 // groups, 2 * channels, dtype=jnp.float32)
    rest = shape(rows // 2 // groups * (groups - 1), 2 * channels, dtype=jnp.float32)
    ends_one, *halves = call(
        functools.partial(outer_kernel, scale, groups),
        [shifted, far, rest, far, rest],
        (two, got_one, near_ends, weights, grad, *select),
        [VMEM] * 7,
        [*ends[1:], scratch(rows, 2 * channels, dtype=jnp.float32)],
    )
    table = shape(3 * channels, 9 * channels)
    table_y, table_g = call(tables_kernel, [table, table], (weight,), [VMEM], [])
    inner_g = call(shift_kernel, volume, (near, own_g, *select), [SMEM] + [VMEM] * 3, parts)
    out_y, ends_two = call(
        forward_kernel,
        [shape(*features.shape), shifted],
        (near, two, got_two, table_y, inner_x, ends_one, present, *select),
        [SMEM] + [VMEM] * 8,
        ends,
    )
    out_g = call(
        backward_kernel, shape(*cotangent.shape), (table_g, inner_g, ends_one, ends_two, present), [VMEM] * 5, []
    )
    mine, theirs = all_sum(*halves, groups)
    taps = shape(27, channels, channels, dtype=jnp.float32)

    def unpack(own, parts, *before):
        return pl.pallas_call(
            functools.partial(unpack_kernel, groups, own),
            out_shape=taps,
            in_specs=[VMEM] * groups + [HBM] * len(before),
            out_specs=HBM,
            scratch_shapes=[
                scratch(rows // 2, 2 * channels, dtype=jnp.float32),
                scratch(14, channels, channels, dtype=jnp.float32),
                pltpu.SemaphoreType.DMA((14,)),
            ],
            input_output_aliases={groups: 0} if before else {},
            compiler_params=pltpu.CompilerParams(vmem_limit_bytes=16 << 20),
            cost_estimate=pl.CostEstimate(flops=10**6, bytes_accessed=10**6, transcendentals=0),
            name="unpack",
        )(*parts, *before)

    out_w = unpack(True, mine)
    out_w = unpack(False, theirs, out_w)
    return out_y, out_g, out_w


def solution(mesh):
    in_specs = (
        P("scene", "space", None, None),
        P("scene", "space", None, None),
        P(),
        P("scene", "space", None),
        P("scene", "space", None),
    )
    out_specs = (P("scene", "space", None, None), P("scene", "space", None, None), P())
    return jax.shard_map(program, mesh=mesh, in_specs=in_specs, out_specs=out_specs, check_vma=False)
```
